256 devices in a mesh: row: 8 (over y_lo, x), col: 32 (over z, y_hi, core).
Axes of the slice: x: 4, y: 4 (y_hi: 2, y_lo: 2; y = y_hi * 2 + y_lo), z: 8, core: 2. Of those that a mesh axis runs over, the one named last changes fastest.
Arguments:
- tile_counts: int32 [8, 32, 160, 128, 128], P('row', 'col'), may hold values from 0 to 1536, as said below
- tile_rows: int32 [8, 32, 160], P('row', 'col'), may hold values from 0 to 127, as said below
- tile_cols: int32 [8, 32, 160], P('row', 'col'), may hold values from 0 to 31
- panel: bfloat16 [131072, 128], P(('col', 'row')), may hold values from -0.059814453 to 0.059814453
Outputs:
- word_panel: float32 [131072, 128], P(('row', 'col'))
- context_panel: float32 [131072, 128], P(('col', 'row'))
The draws below stay inside these ranges and needn't reach their ends.
Inputs may be any that keep to these rules, and one draw needn't show every extreme that they name: `tile_counts`: on each device the occupied tiles come first: every slot at or after that device's number of occupied tiles holds only zeros, and some device has all 160 slots occupied. On each device the pairs (tile_rows, tile_cols) of the slots are distinct.
All inputs are finite; a program needn't handle non-finite values.
Results may differ from the reference program's by a relative error of at most 0.0029.
Values may be sent and summed in bfloat16 or wider, within the bound.
A program may use at most 128 MiB of HBM per device.

```python
import math
import jax
import jax.numpy as jnp
from jax import lax

VOCAB = 131072
TILE = 128
PANEL = 128
NEG_SAMPLES = 15
TILES_DEV = 160
N_ROW = 8
N_COL = 32


def tile_layout(key):
    layout_key = jax.random.fold_in(key, 11)
    slot_total = VOCAB // (TILE * N_ROW) * (VOCAB // (TILE * N_COL))
    device_keys = jax.random.split(layout_key, N_ROW * N_COL)
    chosen = jax.vmap(lambda one_key: jax.random.permutation(one_key, slot_total)[:TILES_DEV])(device_keys)
    chosen = chosen.reshape(N_ROW, N_COL, TILES_DEV).astype(jnp.int32)
    band_cols = VOCAB // (TILE * N_COL)
    return (chosen // band_cols, chosen % band_cols)


def live_slots(key):
    live_key = jax.random.fold_in(key, 23)
    drawn = jax.random.randint(jax.random.fold_in(live_key, 1), (N_ROW * N_COL,), TILES_DEV // 8, TILES_DEV + 1)
    fullest = jax.random.randint(jax.random.fold_in(live_key, 2), (), 0, N_ROW * N_COL)
    drawn = jnp.where(jnp.arange(N_ROW * N_COL, dtype=jnp.int32) == fullest, TILES_DEV, drawn)
    return drawn.reshape(N_ROW, N_COL).astype(jnp.int32)


def draw_tile_rows(key, part):
    return tile_layout(key)[0]


def draw_tile_cols(key, part):
    return tile_layout(key)[1]


def draw_tile_counts(key, part):
    word_tiles, context_tiles = tile_layout(key)
    live = live_slots(key)
    band_rows = VOCAB // (TILE * N_ROW)
    band_cols = VOCAB // (TILE * N_COL)
    word_scale = jnp.left_shift(jnp.int32(1), jax.random.randint(jax.random.fold_in(key, 31), (VOCAB,), 0, 4))
    context_band = jnp.arange(VOCAB, dtype=jnp.int32) // (VOCAB // N_COL)
    context_scale = jnp.left_shift(jnp.int32(1), jax.random.randint(jax.random.fold_in(key, 37), (VOCAB,), 0, 3))
    context_scale = context_scale * (1 + 2 * context_band // (N_COL - 1))
    within = jnp.arange(TILE, dtype=jnp.int32)
    row_ids = jnp.arange(N_ROW, dtype=jnp.int32)[:, None, None, None]
    col_ids = jnp.arange(N_COL, dtype=jnp.int32)[None, :, None, None]
    word_ids = row_ids * band_rows * TILE + word_tiles[..., None] * TILE + within
    context_ids = col_ids * band_cols * TILE + context_tiles[..., None] * TILE + within
    spread = 3 * (N_ROW - 1)
    raw = jax.random.randint(jax.random.fold_in(key, 41), (N_ROW, N_COL, TILES_DEV, TILE, TILE), 0, 5 * spread)
    keep = raw // 5 < N_ROW - 1 + 2 * row_ids[..., None]
    alive = jnp.arange(TILES_DEV, dtype=jnp.int32)[None, None, :] < live[:, :, None]
    values = jnp.left_shift(jnp.int32(1), raw % 5) * word_scale[word_ids][..., :, None] * context_scale[context_ids][..., None, :]
    return jnp.where(keep & alive[..., None, None], values, 0).astype(jnp.int32)


def steps_of(rng, dims, shards, low, top_value):
    gain = 1.0
    for axis_at, parts in shards:
        draws = jax.random.uniform(jax.random.fold_in(jax.random.fold_in(rng, 6), axis_at), (parts,), jnp.float32, low / len(shards), top_value / len(shards))
        gain = gain * jnp.repeat(jnp.exp(draws), dims[axis_at] // parts).reshape((-1,) + (1,) * (len(dims) - 1 - axis_at))
    return gain


def bell_draw(rng, dims, scale, most, cuts=(), held_as=jnp.bfloat16):
    loudness = steps_of(rng, dims, cuts, -0.22, 0.18) if cuts else 1.0
    array = jax.random.normal(rng, dims, jnp.float32) * scale * loudness
    return jnp.minimum(jnp.maximum(array, -most), most).astype(held_as)


def setup_inputs(seed: int = 0) -> dict:
    keys = jax.random.split(jax.random.key(seed), 5)
    return {
        "tile_counts": draw_tile_counts(jax.random.fold_in(keys[4], 71), 0),
        "tile_rows": draw_tile_rows(jax.random.fold_in(keys[4], 71), 0),
        "tile_cols": draw_tile_cols(jax.random.fold_in(keys[4], 71), 0),
        "panel": bell_draw(keys[3], (VOCAB, PANEL), 0.01, 0.059814453, ((0, 256),)),
    }


def ppmi_tiles(counts, word_rows, context_cols, row_totals, context_powers, log_scale):
    counts_float = counts.astype(jnp.float32)
    word_log = jnp.log(jnp.maximum(row_totals[word_rows], 1.0))
    context_log = jnp.log(jnp.maximum(context_powers[context_cols], 1.0))
    pointwise = jnp.log(jnp.maximum(counts_float, 1.0)) + log_scale - word_log[:, :, None] - context_log[:, None, :]
    return jnp.where(counts > 0, jnp.maximum(pointwise, 0.0), 0.0).astype(jnp.bfloat16)


def reference(tile_counts, tile_rows, tile_cols, panel):
    band_rows = VOCAB // (TILE * N_ROW)
    band_cols = VOCAB // (TILE * N_COL)
    word_part = jnp.sum(tile_counts, axis=4).astype(jnp.float32)
    context_part = jnp.sum(tile_counts, axis=3).astype(jnp.float32)
    row_index = jnp.broadcast_to(jnp.arange(N_ROW, dtype=jnp.int32)[:, None, None], tile_rows.shape)
    col_index = jnp.broadcast_to(jnp.arange(N_COL, dtype=jnp.int32)[None, :, None], tile_cols.shape)
    row_totals = jnp.zeros((N_ROW, band_rows, TILE), jnp.float32).at[row_index, tile_rows].add(word_part)
    context_totals = jnp.zeros((N_COL, band_cols, TILE), jnp.float32).at[col_index, tile_cols].add(context_part)
    context_powers = context_totals ** 0.75
    log_scale = jnp.log(jnp.sum(context_powers)) - math.log(NEG_SAMPLES)
    panel_bands = panel.reshape(N_COL, band_cols, TILE, PANEL)

    def device_tiles(row_id, col_id):
        return ppmi_tiles(tile_counts[row_id, col_id], tile_rows[row_id, col_id], tile_cols[row_id, col_id],
                          row_totals[row_id], context_powers[col_id], log_scale)

    def word_band(row_id):
        def add_device(total, col_id):
            tiles = device_tiles(row_id, col_id)
            picked = panel_bands[col_id][tile_cols[row_id, col_id]]
            product = jnp.einsum("nij,njk->nik", tiles.astype(jnp.float32), picked.astype(jnp.float32))
            partial_sum = jax.ops.segment_sum(product, tile_rows[row_id, col_id], num_segments=band_rows)
            return total + partial_sum, None
        start = jnp.zeros((band_rows, TILE, PANEL), jnp.float32)
        return lax.scan(add_device, start, jnp.arange(N_COL, dtype=jnp.int32))[0]

    word_panel = lax.map(word_band, jnp.arange(N_ROW, dtype=jnp.int32))
    word_rounded = word_panel.astype(jnp.bfloat16)

    def context_band(col_id):
        def add_device(total, row_id):
            tiles = device_tiles(row_id, col_id)
            picked = word_rounded[row_id][tile_rows[row_id, col_id]]
            product = jnp.einsum("nji,njk->nik", tiles.astype(jnp.float32), picked.astype(jnp.float32))
            partial_sum = jax.ops.segment_sum(product, tile_cols[row_id, col_id], num_segments=band_cols)
            return total + partial_sum, None
        start = jnp.zeros((band_cols, TILE, PANEL), jnp.float32)
        return lax.scan(add_device, start, jnp.arange(N_ROW, dtype=jnp.int32))[0]

    context_panel = lax.map(context_band, jnp.arange(N_COL, dtype=jnp.int32))
    return word_panel.reshape(VOCAB, PANEL), (context_panel / TILE).reshape(VOCAB, PANEL)
```

```python
import functools
import math

import jax
import jax.numpy as jnp
from jax import lax
from jax.experimental import pallas as pl
from jax.experimental.pallas import tpu as pltpu
from jax.sharding import Mesh
from jax.sharding import PartitionSpec as P

NEG_SAMPLES = 15
T = 128
NX, NYL, NYH, NZ, NC = 4, 2, 2, 8, 2
N_ROW, N_COL = NX * NYL, NZ * NYH * NC
ROW_TILES, COL_TILES = 128, 32
SHARE = 512
CODE = SHARE + 16
MESH = pl.DeviceIdType.MESH
F32, BF16, I32, I16 = jnp.float32, jnp.bfloat16, jnp.int32, jnp.int16
ANY = pl.BlockSpec(memory_space=pl.ANY)
VMEM = pl.BlockSpec(memory_space=pltpu.VMEM)
DMA = pltpu.SemaphoreType.DMA
LN2 = math.log(2.0)


def remote(src, dst, ssem, rsem, device):
    return pltpu.make_async_remote_copy(
        src_ref=src, dst_ref=dst, send_sem=ssem, recv_sem=rsem,
        device_id=device, device_id_type=MESH,
    )


def greet(devices):
    barrier = pltpu.get_barrier_semaphore()
    for device in devices:
        pl.semaphore_signal(barrier, inc=1, device_id=device, device_id_type=MESH)
    pl.semaphore_wait(barrier, len(devices))


def encode(value, ref):
    top = jnp.max(jnp.abs(value), axis=0, keepdims=True)
    expo = jnp.ceil(jnp.log(jnp.maximum(top, 1e-30)) * (1.0 / LN2) + 0.001) - 14.0
    scaled = jnp.round(value * jnp.exp(expo * -LN2))
    ref[pl.ds(0, SHARE), :] = scaled.astype(I32).astype(I16)
    ref[pl.ds(SHARE, 16), :] = jnp.broadcast_to(expo, (16, T)).astype(I32).astype(I16)


def decode(ref):
    expo = ref[pl.ds(SHARE, 16), :].astype(I32).astype(F32)[0:1]
    return ref[pl.ds(0, SHARE), :].astype(I32).astype(F32) * jnp.exp(expo * LN2)


def count_kernel(group, rows, cols, counts, words, contexts, wacc, cacc):
    step = pl.program_id(0)

    @pl.when(step == 0)
    def _():
        wacc[...] = jnp.zeros_like(wacc)
        cacc[...] = jnp.zeros_like(cacc)

    lanes = lax.broadcasted_iota(I32, (T, T), 1)
    total = wacc[...]
    for g in range(group):
        slot = step * group + g
        value = counts[g]
        cacc[pl.ds(cols[slot], 1), :] += jnp.sum(value, axis=0, keepdims=True)
        per_word = jnp.sum(value.astype(F32), axis=1, keepdims=True)
        total = total + jnp.where(lanes == rows[slot], per_word, 0.0)
    wacc[...] = total

    @pl.when(step == pl.num_programs(0) - 1)
    def _():
        contexts[...] = cacc[...].astype(F32)
        words[...] = jnp.zeros_like(words)
        for d in range(N_COL):
            words[d, 0:4, :] = wacc[pl.ds(4 * d, 4), :]


def count_sums(rows, cols, counts, group=16):
    slots = counts.shape[0]
    return pl.pallas_call(
        functools.partial(count_kernel, group),
        grid_spec=pltpu.PrefetchScalarGridSpec(
            num_scalar_prefetch=2,
            grid=(slots // group,),
            in_specs=[pl.BlockSpec((group, T, T), lambda i, r, c: (i, 0, 0))],
            out_specs=[
                pl.BlockSpec((N_COL, 8, T), lambda i, r, c: (0, 0, 0)),
                pl.BlockSpec((COL_TILES, T), lambda i, r, c: (0, 0)),
            ],
            scratch_shapes=[pltpu.VMEM((T, ROW_TILES), F32), pltpu.VMEM((COL_TILES, T), I32)],
        ),
        out_shape=[
            jax.ShapeDtypeStruct((N_COL, 8, T), F32),
            jax.ShapeDtypeStruct((COL_TILES, T), F32),
        ],
        name="count_sums",
    )(rows, cols, counts)


def powers_of(totals):
    root = jnp.sqrt(totals)
    return root * jnp.sqrt(root)


def totals_kernel(words, contexts, panel, words_all, contexts_all, band,
                  wrecv, crecv, mine, wss, wrs, css, crs, ass, ars, pss, prs, lsem):
    x, yl = lax.axis_index("x"), lax.axis_index("yl")
    z, yh, c = lax.axis_index("z"), lax.axis_index("yh"), lax.axis_index("core")
    row = yl * NX + x
    col = (z * NYH + yh) * NC + c
    row_peers = [
        (dx * NYL + dy, {"x": lax.rem(x + dx, NX), "yl": lax.rem(yl + dy, NYL)})
        for dx in range(NX) for dy in range(NYL) if dx or dy
    ]
    col_peers = []
    for dz in (4, 3, 5, 2, 6, 1, 7, 0):
        for dy in (1, 0):
            for dc in range(NC):
                if dz or dy or dc:
                    pz, py, pc = lax.rem(z + dz, NZ), lax.rem(yh + dy, NYH), lax.rem(c + dc, NC)
                    col_peers.append(
                        ((dz * NYH + dy) * NC + dc, (pz * NYH + py) * NC + pc,
                         {"z": pz, "yh": py, "core": pc})
                    )
    greet([d for _, d in row_peers] + [d for _, _, d in col_peers])

    waits = []
    csends = [remote(contexts, crecv.at[k], css.at[k], crs.at[k], d) for k, d in row_peers]
    wsends = [remote(words.at[p], wrecv.at[k], wss.at[k], wrs.at[k], d) for k, p, d in col_peers]
    psends = [remote(panel, band.at[row], pss.at[k], prs.at[k], d) for k, d in row_peers]
    own = pltpu.make_async_copy(panel, band.at[row], lsem.at[0])
    for copy in csends + wsends + psends:
        copy.start()
    own.start()

    for copy in csends:
        copy.wait_recv()
    contexts_sum = contexts[...]
    for k, _ in row_peers:
        contexts_sum = contexts_sum + crecv[k]
    contexts_all[...] = contexts_sum
    band_power = jnp.sum(powers_of(contexts_sum), keepdims=True)

    for copy in wsends:
        copy.wait_recv()
    words_sum = words[col]
    for k, _, _ in col_peers:
        words_sum = words_sum + wrecv[k]
    at = lax.broadcasted_iota(I32, (8, T), 0)
    mine[...] = jnp.where(at == 4, jnp.broadcast_to(band_power, (8, T)), words_sum)
    asends = [remote(mine, words_all.at[col], ass.at[k], ars.at[k], d) for k, _, d in col_peers]
    for copy in asends:
        copy.start()
    words_all[col] = mine[...]
    for copy in asends:
        copy.wait()
    for copy in csends + wsends:
        copy.wait_send()
    for copy in psends:
        copy.wait()
    own.wait()


def totals(words, contexts, panel):
    return pl.pallas_call(
        totals_kernel,
        in_specs=[VMEM, VMEM, ANY],
        out_specs=[VMEM, VMEM, ANY],
        out_shape=[
            jax.ShapeDtypeStruct((N_COL, 8, T), F32),
            jax.ShapeDtypeStruct((COL_TILES, T), F32),
            jax.ShapeDtypeStruct((N_ROW, SHARE, T), BF16),
        ],
        scratch_shapes=[
            pltpu.VMEM((N_COL, 8, T), F32),
            pltpu.VMEM((N_ROW, COL_TILES, T), F32),
            pltpu.VMEM((8, T), F32),
            DMA((N_COL,)), DMA((N_COL,)), DMA((N_ROW,)), DMA((N_ROW,)),
            DMA((N_COL,)), DMA((N_COL,)), DMA((N_ROW,)), DMA((N_ROW,)), DMA((1,)),
        ],
        compiler_params=pltpu.CompilerParams(collective_id=0, has_side_effects=True),
        name="totals",
    )(words, contexts, panel)


def word_kernel(group, rows, cols, counts, words_all, contexts_all, band, tiles, partial,
                word_term, context_log):
    step = pl.program_id(0)

    @pl.when(step == 0)
    def _():
        power = jnp.zeros((1, T), F32)
        for d in range(N_COL):
            word_term[pl.ds(4 * d, 4), :] = words_all[d, 0:4, :]
            power = power + words_all[d, 4:5, :]
        log_scale = jnp.log(power) - math.log(NEG_SAMPLES)
        word_term[...] = log_scale - jnp.log(jnp.maximum(word_term[...], 1.0))
        context_log[...] = jnp.log(jnp.maximum(powers_of(contexts_all[...]), 1.0))
        partial[...] = jnp.zeros_like(partial)

    lanes = lax.broadcasted_iota(I32, (T, T), 1)
    for g in range(group):
        slot = step * group + g
        row, col = rows[slot], cols[slot]
        value = counts[g]
        per_word = jnp.sum(jnp.where(lanes == row, word_term[...], 0.0), axis=1, keepdims=True)
        pointwise = jnp.log(value.astype(F32)) + per_word - context_log[pl.ds(col, 1), :]
        tile = jnp.where(value > 0, jnp.maximum(pointwise, 0.0), 0.0).astype(BF16)
        tiles[g] = tile
        partial[row] += jnp.dot(tile, band[col], preferred_element_type=F32)


def word_products(rows, cols, counts, words_all, contexts_all, band, group=16):
    slots = counts.shape[0]
    whole3 = lambda i, r, c: (0, 0, 0)
    return pl.pallas_call(
        functools.partial(word_kernel, group),
        grid_spec=pltpu.PrefetchScalarGridSpec(
            num_scalar_prefetch=2,
            grid=(slots // group,),
            in_specs=[
                pl.BlockSpec((group, T, T), lambda i, r, c: (i, 0, 0)),
                pl.BlockSpec((N_COL, 8, T), whole3),
                pl.BlockSpec((COL_TILES, T), lambda i, r, c: (0, 0)),
                pl.BlockSpec((COL_TILES, T, T), whole3),
            ],
            out_specs=[
                pl.BlockSpec((group, T, T), lambda i, r, c: (i, 0, 0)),
                pl.BlockSpec((ROW_TILES, T, T), whole3),
            ],
            scratch_shapes=[pltpu.VMEM((T, ROW_TILES), F32), pltpu.VMEM((COL_TILES, T), F32)],
        ),
        out_shape=[
            jax.ShapeDtypeStruct((slots, T, T), BF16),
            jax.ShapeDtypeStruct((ROW_TILES, T, T), F32),
        ],
        name="word_products",
    )(rows, cols, counts, words_all, contexts_all, band)


def chain_steps(length):
    steps = []
    for s in range(length):
        for way, half in ((0, 1), (1, 0), (0, 0), (1, 1)):
            if s > 0 or way == half:
                steps.append((s, way, half))
    return steps


Z_STEPS = chain_steps(NZ // 2)
X_STEPS = chain_steps(NX // 2)


def word_panel_kernel(partial, share, everyone, own, sib, sendb, recvb, ysend, yrecv, mine,
                      lsem, xss, xrs, zss, zrs, yss, yrs, gss, grs, hss, hrs, ms):
    z, yh, c = lax.axis_index("z"), lax.axis_index("yh"), lax.axis_index("core")
    ways = ({"z": lax.rem(z + 1, NZ)}, {"z": lax.rem(z + NZ - 1, NZ)})
    other_y, other_core = {"yh": 1 - yh}, {"core": 1 - c}

    loads, swaps = {}, {}
    order = [(dz, h) for dz in (4, 3, 5, 2, 6, 1, 7, 0) for h in range(2)]
    for dz, h in order:
        slot, zz = dz * 2 + h, lax.rem(z + dz, NZ)
        loads[dz, h] = pltpu.make_async_copy(partial.at[zz, h, c], own.at[slot], lsem.at[slot])
        loads[dz, h].start()
    greet([*ways, other_y, other_core])
    for dz, h in order:
        slot, zz = dz * 2 + h, lax.rem(z + dz, NZ)
        swaps[dz, h] = remote(partial.at[zz, h, 1 - c], sib.at[slot], xss.at[slot], xrs.at[slot], other_core)
        swaps[dz, h].start()

    def block(dz, h):
        loads[dz, h].wait()
        swaps[dz, h].wait_recv()
        return own[dz * 2 + h] + sib[dz * 2 + h]

    sends = {}
    for n, (s, way, half) in enumerate(Z_STEPS):
        value = block((NZ // 2 - s) if way == 0 else (NZ // 2 + s), half)
        if (s - 1, way, half) in sends:
            before = sends[s - 1, way, half]
            before[1].wait_recv()
            value = value + decode(recvb.at[before[0]])
        encode(value, sendb.at[n])
        copy = remote(sendb.at[n], recvb.at[n], zss.at[n], zrs.at[n], ways[way])
        copy.start()
        sends[s, way, half] = (n, copy)

    last = NZ // 2 - 1
    for h in range(2):
        loads[0, h].wait()
        swaps[0, h].wait_recv()
        for way in range(2):
            sends[last, way, h][1].wait_recv()

    def arrived(h):
        value = own[h] + sib[h]
        for way in range(2):
            first, second = sends[last, way, 0][0], sends[last, way, 1][0]
            value = value + decode(recvb.at[first + h * (second - first)])
        return value

    encode(arrived(1 - yh), ysend)
    ycopy = remote(ysend, yrecv, yss.at[0], yrs.at[0], other_y)
    ycopy.start()
    kept = arrived(yh)
    ycopy.wait_recv()
    total = kept + decode(yrecv)
    share[...] = total
    for t in range(4):
        mine[t] = total[t * T : (t + 1) * T].T.astype(BF16)

    halves = (yh, 1 - yh)
    home = everyone.at[z, yh, c]
    keep = pltpu.make_async_copy(mine, home, ms.at[0])
    keep.start()
    ygive = remote(mine, home, yss.at[1], yrs.at[1], other_y)
    ygive.start()
    gives, hands = {}, []

    def hand(src, place, k):
        copy = remote(src, place, hss.at[k], hrs.at[k], other_core)
        copy.start()
        hands.append(copy)

    def give(s, way, r, src):
        zz = lax.rem(z + (NZ - s if way == 0 else s), NZ)
        place = everyone.at[zz, halves[r], c]
        k = (s * 2 + way) * 2 + r
        copy = remote(place if src is None else src, place, gss.at[k], grs.at[k], ways[way])
        copy.start()
        gives[s, way, r] = copy

    give(0, 0, 0, mine)
    give(0, 1, 0, mine)
    hand(mine, home, 0)
    ygive.wait_recv()
    give(0, 0, 1, None)
    give(0, 1, 1, None)
    hand(everyone.at[z, 1 - yh, c], everyone.at[z, 1 - yh, c], 1)
    k = 2
    for s in range(1, NZ // 2 + 1):
        for r in range(2):
            for way in range(2):
                if (s - 1, way, r) not in gives:
                    continue
                gives[s - 1, way, r].wait_recv()
                if s < last or (s == last and way == r):
                    give(s, way, r, None)
                zz = lax.rem(z + (NZ - s if way == 0 else s), NZ)
                place = everyone.at[zz, halves[r], c]
                hand(place, place, k)
                k += 1

    for copy in hands:
        copy.wait()
    for copy in gives.values():
        copy.wait_send()
    for _, copy in sends.values():
        copy.wait_send()
    for copy in swaps.values():
        copy.wait_send()
    ycopy.wait_send()
    ygive.wait_send()
    keep.wait()


def word_panel_sum(partial):
    n = len(Z_STEPS)
    return pl.pallas_call(
        word_panel_kernel,
        in_specs=[ANY],
        out_specs=[VMEM, ANY],
        out_shape=[
            jax.ShapeDtypeStruct((SHARE, T), F32),
            jax.ShapeDtypeStruct((NZ, NYH, NC, 4, T, T), BF16),
        ],
        scratch_shapes=[
            pltpu.VMEM((2 * NZ, SHARE, T), F32),
            pltpu.VMEM((2 * NZ, SHARE, T), F32),
            pltpu.VMEM((n, CODE, T), I16),
            pltpu.VMEM((n, CODE, T), I16),
            pltpu.VMEM((CODE, T), I16),
            pltpu.VMEM((CODE, T), I16),
            pltpu.VMEM((4, T, T), BF16),
            DMA((2 * NZ,)), DMA((2 * NZ,)), DMA((2 * NZ,)), DMA((n,)), DMA((n,)),
            DMA((2,)), DMA((2,)), DMA((2 * NZ,)), DMA((2 * NZ,)),
            DMA((2 * NZ,)), DMA((2 * NZ,)), DMA((1,)),
        ],
        compiler_params=pltpu.CompilerParams(collective_id=1, has_side_effects=True),
        name="word_panel_sum",
    )(partial)


def context_kernel(group, rows, cols, tiles, rounded, partial):
    step = pl.program_id(0)

    @pl.when(step == 0)
    def _():
        partial[...] = jnp.zeros_like(partial)

    for g in range(group):
        slot = step * group + g
        partial[cols[slot]] += jnp.dot(rounded[rows[slot]], tiles[g], preferred_element_type=F32)


def context_products(rows, cols, tiles, rounded, group=16):
    slots = tiles.shape[0]
    whole3 = lambda i, r, c: (0, 0, 0)
    return pl.pallas_call(
        functools.partial(context_kernel, group),
        grid_spec=pltpu.PrefetchScalarGridSpec(
            num_scalar_prefetch=2,
            grid=(slots // group,),
            in_specs=[
                pl.BlockSpec((group, T, T), lambda i, r, c: (i, 0, 0)),
                pl.BlockSpec((ROW_TILES, T, T), whole3),
            ],
            out_specs=pl.BlockSpec((COL_TILES, T, T), whole3),
        ),
        out_shape=jax.ShapeDtypeStruct((COL_TILES, T, T), F32),
        name="context_products",
    )(rows, cols, tiles, rounded)


def context_panel_kernel(partial, share, sendb, recvb, ysend, yrecv, xss, xrs, yss, yrs):
    x, yl = lax.axis_index("x"), lax.axis_index("yl")
    ways = ({"x": lax.rem(x + 1, NX)}, {"x": lax.rem(x + NX - 1, NX)})
    other_y = {"yl": 1 - yl}
    greet([*ways, other_y])
    sends = {}
    for n, (s, way, half) in enumerate(X_STEPS):
        value = partial[half, lax.rem(x + (NX // 2 - s if way == 0 else NX // 2 + s), NX)]
        if (s - 1, way, half) in sends:
            before = sends[s - 1, way, half]
            before[1].wait_recv()
            value = value + decode(recvb.at[before[0]])
        encode(value, sendb.at[n])
        copy = remote(sendb.at[n], recvb.at[n], xss.at[n], xrs.at[n], ways[way])
        copy.start()
        sends[s, way, half] = (n, copy)
    last = NX // 2 - 1
    for h in range(2):
        for way in range(2):
            sends[last, way, h][1].wait_recv()

    def arrived(h):
        value = partial[h, x]
        for way in range(2):
            first, second = sends[last, way, 0][0], sends[last, way, 1][0]
            value = value + decode(recvb.at[first + h * (second - first)])
        return value

    encode(arrived(1 - yl), ysend)
    ycopy = remote(ysend, yrecv, yss.at[0], yrs.at[0], other_y)
    ycopy.start()
    kept = arrived(yl)
    ycopy.wait_recv()
    total = (kept + decode(yrecv)) * (1.0 / T)
    for t in range(4):
        share[pl.ds(t * T, T), :] = total[t * T : (t + 1) * T].T
    for _, copy in sends.values():
        copy.wait_send()
    ycopy.wait_send()


def context_panel_sum(partial):
    n = len(X_STEPS)
    return pl.pallas_call(
        context_panel_kernel,
        in_specs=[VMEM],
        out_specs=VMEM,
        out_shape=jax.ShapeDtypeStruct((SHARE, T), F32),
        scratch_shapes=[
            pltpu.VMEM((n, CODE, T), I16),
            pltpu.VMEM((n, CODE, T), I16),
            pltpu.VMEM((CODE, T), I16),
            pltpu.VMEM((CODE, T), I16),
            DMA((n,)), DMA((n,)), DMA((1,)), DMA((1,)),
        ],
        compiler_params=pltpu.CompilerParams(collective_id=2, has_side_effects=True),
        name="context_panel_sum",
    )(partial)


def shards(tile_counts, tile_rows, tile_cols, panel):
    counts, rows, cols = tile_counts[0, 0], tile_rows[0, 0], tile_cols[0, 0]
    words, contexts = count_sums(rows, cols, counts)
    words_all, contexts_all, band = totals(words, contexts, panel)
    band = band.reshape(COL_TILES, T, T)
    tiles, partial = word_products(rows, cols, counts, words_all, contexts_all, band)
    share, everyone = word_panel_sum(partial.reshape(NZ, NYH, NC, SHARE, T))
    rounded = everyone.reshape(ROW_TILES, T, T)
    context_partial = context_products(rows, cols, tiles, rounded)
    context_share = context_panel_sum(context_partial.reshape(NYL, NX, SHARE, T))
    return share, context_share


def solution(mesh):
    split = Mesh(
        mesh.devices.reshape(NYL, NX, NZ, NYH, NC), ("yl", "x", "z", "yh", "core")
    )
    row, col = ("yl", "x"), ("z", "yh", "core")
    in_specs = (
        P(row, col, None, None, None),
        P(row, col, None),
        P(row, col, None),
        P(col + row, None),
    )
    out_specs = (P(row + col, None), P(col + row, None))
    return jax.shard_map(shards, mesh=split, in_specs=in_specs, out_specs=out_specs, check_vma=False)
```

```python
import functools
import math

import jax
import jax.numpy as jnp
from jax import lax
from jax.experimental import pallas as pl
from jax.experimental.pallas import tpu as pltpu
from jax.sharding import Mesh
from jax.sharding import PartitionSpec as P

NEG_SAMPLES = 15
T = 128
NX, NYL, NYH, NZ, NC = 4, 2, 2, 8, 2
N_ROW, N_COL = NX * NYL, NZ * NYH * NC
ROW_TILES, COL_TILES = 128, 32
SHARE = 512
CODE = SHARE + 16
MESH = pl.DeviceIdType.MESH
F32, BF16, I32, I16 = jnp.float32, jnp.bfloat16, jnp.int32, jnp.int16
ANY = pl.BlockSpec(memory_space=pl.ANY)
VMEM = pl.BlockSpec(memory_space=pltpu.VMEM)
SMEM = pl.BlockSpec(memory_space=pltpu.SMEM)
DMA = pltpu.SemaphoreType.DMA
LN2 = math.log(2.0)


def remote(src, dst, ssem, rsem, device):
    return pltpu.make_async_remote_copy(
        src_ref=src, dst_ref=dst, send_sem=ssem, recv_sem=rsem,
        device_id=device, device_id_type=MESH,
    )


def greet(devices):
    barrier = pltpu.get_barrier_semaphore()
    for device in devices:
        pl.semaphore_signal(barrier, inc=1, device_id=device, device_id_type=MESH)
    pl.semaphore_wait(barrier, len(devices))


def encode(value, ref):
    top = jnp.max(jnp.abs(value), axis=0, keepdims=True)
    expo = jnp.ceil(jnp.log(jnp.maximum(top, 1e-30)) * (1.0 / LN2) + 0.001) - 14.0
    scaled = jnp.round(value * jnp.exp(expo * -LN2))
    ref[pl.ds(0, SHARE), :] = scaled.astype(I32).astype(I16)
    ref[pl.ds(SHARE, 16), :] = jnp.broadcast_to(expo, (16, T)).astype(I32).astype(I16)


def decode(ref):
    expo = ref[pl.ds(SHARE, 16), :].astype(I32).astype(F32)[0:1]
    return ref[pl.ds(0, SHARE), :].astype(I32).astype(F32) * jnp.exp(expo * LN2)


GROUP = 16


def powers_of(totals):
    root = jnp.sqrt(totals)
    return root * jnp.sqrt(root)


def load_counts(counts, held, sem):
    copies = []
    for b in range(counts.shape[0] // GROUP):
        part = pl.ds(b * GROUP, GROUP)
        copies.append(pltpu.make_async_copy(counts.at[part], held.at[part], sem.at[b]))
        copies[-1].start()
    return copies


def await_counts(counts, held, sem, b):
    part = pl.ds(b * GROUP, GROUP)
    pltpu.make_async_copy(counts.at[part], held.at[part], sem.at[b]).wait()


def totals_kernel(rows, cols, counts, panel, words_all, contexts_all, band, held,
                  wacc, words, contexts, wrecv, crecv, mine,
                  cs, wss, wrs, css, crs, ass, ars, pss, prs, lsem):
    x, yl = lax.axis_index("x"), lax.axis_index("yl")
    z, yh, c = lax.axis_index("z"), lax.axis_index("yh"), lax.axis_index("core")
    row = yl * NX + x
    col = (z * NYH + yh) * NC + c
    row_peers = [
        (dx * NYL + dy, {"x": lax.rem(x + dx, NX), "yl": lax.rem(yl + dy, NYL)})
        for dx in range(NX) for dy in range(NYL) if dx or dy
    ]
    col_peers = []
    for dz in (4, 3, 5, 2, 6, 1, 7, 0):
        for dy in (1, 0):
            for dc in range(NC):
                if dz or dy or dc:
                    pz, py, pc = lax.rem(z + dz, NZ), lax.rem(yh + dy, NYH), lax.rem(c + dc, NC)
                    col_peers.append(
                        ((dz * NYH + dy) * NC + dc, (pz * NYH + py) * NC + pc,
                         {"z": pz, "yh": py, "core": pc})
                    )
    load_counts(counts, held, cs)
    greet([d for _, d in row_peers] + [d for _, _, d in col_peers])
    psends = [remote(panel, band.at[row], pss.at[k], prs.at[k], d) for k, d in row_peers]
    own = pltpu.make_async_copy(panel, band.at[row], lsem.at[0])
    for copy in psends:
        copy.start()
    own.start()

    wacc[...] = jnp.zeros_like(wacc)
    lanes = lax.broadcasted_iota(I32, (T, T), 1)
    bands = lax.broadcasted_iota(I32, (COL_TILES, T), 0)

    def some(b, per_context):
        await_counts(counts, held, cs, b)
        per_word = wacc[...]
        for g in range(GROUP):
            slot = b * GROUP + g
            value = held[slot]
            per_context = per_context + jnp.where(
                bands == cols[slot], jnp.sum(value, axis=0, keepdims=True), 0
            )
            sums = jnp.sum(value.astype(F32), axis=1, keepdims=True)
            per_word = per_word + jnp.where(lanes == rows[slot], sums, 0.0)
        wacc[...] = per_word
        return per_context

    per_context = lax.fori_loop(0, counts.shape[0] // GROUP, some, jnp.zeros((COL_TILES, T), I32))
    contexts[...] = per_context.astype(F32)
    csends = [remote(contexts, crecv.at[k], css.at[k], crs.at[k], d) for k, d in row_peers]
    for copy in csends:
        copy.start()
    for d in range(N_COL):
        words[d, 0:4, :] = wacc[pl.ds(4 * d, 4), :]
        words[d, 4:8, :] = jnp.zeros((4, T), F32)
    wsends = [remote(words.at[p], wrecv.at[k], wss.at[k], wrs.at[k], d) for k, p, d in col_peers]
    for copy in wsends:
        copy.start()

    for copy in csends:
        copy.wait_recv()
    contexts_sum = contexts[...]
    for k, _ in row_peers:
        contexts_sum = contexts_sum + crecv[k]
    contexts_all[...] = contexts_sum
    band_power = jnp.sum(powers_of(contexts_sum), keepdims=True)

    for copy in wsends:
        copy.wait_recv()
    words_sum = words[col]
    for k, _, _ in col_peers:
        words_sum = words_sum + wrecv[k]
    at = lax.broadcasted_iota(I32, (8, T), 0)
    mine[...] = jnp.where(at == 4, jnp.broadcast_to(band_power, (8, T)), words_sum)
    asends = [remote(mine, words_all.at[col], ass.at[k], ars.at[k], d) for k, _, d in col_peers]
    for copy in asends:
        copy.start()
    words_all[col] = mine[...]
    for copy in asends:
        copy.wait()
    for copy in csends + wsends:
        copy.wait_send()
    for copy in psends:
        copy.wait()
    own.wait()


def totals(rows, cols, counts, panel):
    slots = counts.shape[0]
    return pl.pallas_call(
        totals_kernel,
        in_specs=[SMEM, SMEM, ANY, ANY],
        out_specs=[VMEM, VMEM, ANY, VMEM],
        out_shape=[
            jax.ShapeDtypeStruct((N_COL, 8, T), F32),
            jax.ShapeDtypeStruct((COL_TILES, T), F32),
            jax.ShapeDtypeStruct((N_ROW, SHARE, T), BF16),
            jax.ShapeDtypeStruct((slots, T, T), I32),
        ],
        scratch_shapes=[
            pltpu.VMEM((T, ROW_TILES), F32),
            pltpu.VMEM((N_COL, 8, T), F32),
            pltpu.VMEM((COL_TILES, T), F32),
            pltpu.VMEM((N_COL, 8, T), F32),
            pltpu.VMEM((N_ROW, COL_TILES, T), F32),
            pltpu.VMEM((8, T), F32),
            DMA((slots // GROUP,)),
            DMA((N_COL,)), DMA((N_COL,)), DMA((N_ROW,)), DMA((N_ROW,)),
            DMA((N_COL,)), DMA((N_COL,)), DMA((N_ROW,)), DMA((N_ROW,)), DMA((1,)),
        ],
        compiler_params=pltpu.CompilerParams(collective_id=0, has_side_effects=True, vmem_limit_bytes=16 << 20),
        name="totals",
    )(rows, cols, counts, panel)


def word_kernel(rows, cols, counts, words_all, contexts_all, band, tiles, partial,
                word_term, context_log):
    power = jnp.zeros((1, T), F32)
    for d in range(N_COL):
        word_term[pl.ds(4 * d, 4), :] = words_all[d, 0:4, :]
        power = power + words_all[d, 4:5, :]
    log_scale = jnp.log(power) - math.log(NEG_SAMPLES)
    word_term[...] = log_scale - jnp.log(jnp.maximum(word_term[...], 1.0))
    context_log[...] = jnp.log(jnp.maximum(powers_of(contexts_all[...]), 1.0))

    def clear(t, carry):
        partial[t] = jnp.zeros((T, T), F32)
        return carry

    lax.fori_loop(0, ROW_TILES, clear, 0, unroll=4)

    def some(b, carry):
        for g in range(GROUP):
            slot = b * GROUP + g
            row, col = rows[slot], cols[slot]
            value = counts[slot]
            per_word = jnp.take_along_axis(word_term[...], jnp.full((T, T), row, I32), axis=1)
            pointwise = jnp.log(value.astype(F32)) + per_word - context_log[pl.ds(col, 1), :]
            tile = jnp.where(value > 0, jnp.maximum(pointwise, 0.0), 0.0).astype(BF16)
            tiles[slot] = tile
            partial[row] += jnp.dot(tile, band[col], preferred_element_type=F32)
        return carry

    lax.fori_loop(0, counts.shape[0] // GROUP, some, 0)


def word_products(rows, cols, counts, words_all, contexts_all, band):
    slots = counts.shape[0]
    return pl.pallas_call(
        word_kernel,
        in_specs=[SMEM, SMEM, VMEM, VMEM, VMEM, VMEM],
        out_specs=[VMEM, VMEM],
        scratch_shapes=[pltpu.VMEM((T, ROW_TILES), F32), pltpu.VMEM((COL_TILES, T), F32)],
        out_shape=[
            jax.ShapeDtypeStruct((slots, T, T), BF16),
            jax.ShapeDtypeStruct((ROW_TILES, T, T), F32),
        ],
        compiler_params=pltpu.CompilerParams(vmem_limit_bytes=28 << 20),
        name="word_products",
    )(rows, cols, counts, words_all, contexts_all, band)


def chain_steps(length):
    steps = []
    for s in range(length):
        for way, half in ((0, 1), (1, 0), (0, 0), (1, 1)):
            if s > 0 or way == half:
                steps.append((s, way, half))
    return steps


Z_STEPS = chain_steps(NZ // 2)
X_STEPS = chain_steps(NX // 2)


def word_panel_kernel(partial, share, everyone, sib, sendb, recvb, ysend, yrecv, mine,
                      xss, xrs, zss, zrs, yss, yrs, gss, grs, hss, hrs, ms):
    z, yh, c = lax.axis_index("z"), lax.axis_index("yh"), lax.axis_index("core")
    ways = ({"z": lax.rem(z + 1, NZ)}, {"z": lax.rem(z + NZ - 1, NZ)})
    other_y, other_core = {"yh": 1 - yh}, {"core": 1 - c}

    swaps = {}
    order = [(dz, h) for dz in (4, 3, 5, 2, 6, 1, 7, 0) for h in range(2)]
    greet([*ways, other_y, other_core])
    for dz, h in order:
        slot, zz = dz * 2 + h, lax.rem(z + dz, NZ)
        swaps[dz, h] = remote(partial.at[zz, h, 1 - c], sib.at[slot], xss.at[slot], xrs.at[slot], other_core)
        swaps[dz, h].start()

    def block(dz, h):
        swaps[dz, h].wait_recv()
        return partial[lax.rem(z + dz, NZ), h, c] + sib[dz * 2 + h]

    sends = {}
    for n, (s, way, half) in enumerate(Z_STEPS):
        value = block((NZ // 2 - s) if way == 0 else (NZ // 2 + s), half)
        if (s - 1, way, half) in sends:
            before = sends[s - 1, way, half]
            before[1].wait_recv()
            value = value + decode(recvb.at[before[0]])
        encode(value, sendb.at[n])
        copy = remote(sendb.at[n], recvb.at[n], zss.at[n], zrs.at[n], ways[way])
        copy.start()
        sends[s, way, half] = (n, copy)

    last = NZ // 2 - 1
    for h in range(2):
        swaps[0, h].wait_recv()
        for way in range(2):
            sends[last, way, h][1].wait_recv()

    def arrived(h):
        value = partial[z, h, c] + sib[h]
        for way in range(2):
            first, second = sends[last, way, 0][0], sends[last, way, 1][0]
            value = value + decode(recvb.at[first + h * (second - first)])
        return value

    encode(arrived(1 - yh), ysend)
    ycopy = remote(ysend, yrecv, yss.at[0], yrs.at[0], other_y)
    ycopy.start()
    kept = arrived(yh)
    ycopy.wait_recv()
    total = kept + decode(yrecv)
    share[...] = total
    for t in range(4):
        mine[t] = total[t * T : (t + 1) * T].T.astype(BF16)

    halves = (yh, 1 - yh)
    home = everyone.at[z, yh, c]
    keep = pltpu.make_async_copy(mine, home, ms.at[0])
    keep.start()
    ygive = remote(mine, home, yss.at[1], yrs.at[1], other_y)
    ygive.start()
    gives, hands = {}, []

    def hand(src, place, k):
        copy = remote(src, place, hss.at[k], hrs.at[k], other_core)
        copy.start()
        hands.append(copy)

    def give(s, way, r, src):
        zz = lax.rem(z + (NZ - s if way == 0 else s), NZ)
        place = everyone.at[zz, halves[r], c]
        k = (s * 2 + way) * 2 + r
        copy = remote(place if src is None else src, place, gss.at[k], grs.at[k], ways[way])
        copy.start()
        gives[s, way, r] = copy

    give(0, 0, 0, mine)
    give(0, 1, 0, mine)
    hand(mine, home, 0)
    ygive.wait_recv()
    give(0, 0, 1, None)
    give(0, 1, 1, None)
    hand(everyone.at[z, 1 - yh, c], everyone.at[z, 1 - yh, c], 1)
    k = 2
    for s in range(1, NZ // 2 + 1):
        for r in range(2):
            for way in range(2):
                if (s - 1, way, r) not in gives:
                    continue
                gives[s - 1, way, r].wait_recv()
                if s < last or (s == last and way == r):
                    give(s, way, r, None)
                zz = lax.rem(z + (NZ - s if way == 0 else s), NZ)
                place = everyone.at[zz, halves[r], c]
                hand(place, place, k)
                k += 1

    for copy in hands:
        copy.wait()
    for copy in gives.values():
        copy.wait_send()
    for _, copy in sends.values():
        copy.wait_send()
    for copy in swaps.values():
        copy.wait_send()
    ycopy.wait_send()
    ygive.wait_send()
    keep.wait()


def word_panel_sum(partial):
    n = len(Z_STEPS)
    return pl.pallas_call(
        word_panel_kernel,
        in_specs=[VMEM],
        out_specs=[VMEM, ANY],
        out_shape=[
            jax.ShapeDtypeStruct((SHARE, T), F32),
            jax.ShapeDtypeStruct((NZ, NYH, NC, 4, T, T), BF16),
        ],
        scratch_shapes=[
            pltpu.VMEM((2 * NZ, SHARE, T), F32),
            pltpu.VMEM((n, CODE, T), I16),
            pltpu.VMEM((n, CODE, T), I16),
            pltpu.VMEM((CODE, T), I16),
            pltpu.VMEM((CODE, T), I16),
            pltpu.VMEM((4, T, T), BF16),
            DMA((2 * NZ,)), DMA((2 * NZ,)), DMA((n,)), DMA((n,)),
            DMA((2,)), DMA((2,)), DMA((2 * NZ,)), DMA((2 * NZ,)),
            DMA((2 * NZ,)), DMA((2 * NZ,)), DMA((1,)),
        ],
        compiler_params=pltpu.CompilerParams(collective_id=1, has_side_effects=True, vmem_limit_bytes=16 << 20),
        name="word_panel_sum",
    )(partial)


def context_kernel(rows, cols, tiles, rounded, share, partial, share_out):
    share_out[...] = share[...]
    partial[...] = jnp.zeros_like(partial)

    def some(b, carry):
        for g in range(GROUP):
            slot = b * GROUP + g
            partial[cols[slot]] += jnp.dot(rounded[rows[slot]], tiles[slot], preferred_element_type=F32)
        return carry

    lax.fori_loop(0, tiles.shape[0] // GROUP, some, 0)


def context_products(rows, cols, tiles, rounded, share):
    slots = tiles.shape[0]
    return pl.pallas_call(
        context_kernel,
        in_specs=[SMEM, SMEM, VMEM, VMEM, VMEM],
        out_specs=[VMEM, VMEM],
        out_shape=[
            jax.ShapeDtypeStruct((COL_TILES, T, T), F32),
            jax.ShapeDtypeStruct((SHARE, T), F32),
        ],
        compiler_params=pltpu.CompilerParams(vmem_limit_bytes=16 << 20),
        name="context_products",
    )(rows, cols, tiles, rounded, share)


def context_panel_kernel(partial, share, sendb, recvb, ysend, yrecv, xss, xrs, yss, yrs):
    x, yl = lax.axis_index("x"), lax.axis_index("yl")
    ways = ({"x": lax.rem(x + 1, NX)}, {"x": lax.rem(x + NX - 1, NX)})
    other_y = {"yl": 1 - yl}
    greet([*ways, other_y])
    sends = {}
    for n, (s, way, half) in enumerate(X_STEPS):
        value = partial[half, lax.rem(x + (NX // 2 - s if way == 0 else NX // 2 + s), NX)]
        if (s - 1, way, half) in sends:
            before = sends[s - 1, way, half]
            before[1].wait_recv()
            value = value + decode(recvb.at[before[0]])
        encode(value, sendb.at[n])
        copy = remote(sendb.at[n], recvb.at[n], xss.at[n], xrs.at[n], ways[way])
        copy.start()
        sends[s, way, half] = (n, copy)
    last = NX // 2 - 1
    for h in range(2):
        for way in range(2):
            sends[last, way, h][1].wait_recv()

    def arrived(h):
        value = partial[h, x]
        for way in range(2):
            first, second = sends[last, way, 0][0], sends[last, way, 1][0]
            value = value + decode(recvb.at[first + h * (second - first)])
        return value

    encode(arrived(1 - yl), ysend)
    ycopy = remote(ysend, yrecv, yss.at[0], yrs.at[0], other_y)
    ycopy.start()
    kept = arrived(yl)
    ycopy.wait_recv()
    total = (kept + decode(yrecv)) * (1.0 / T)
    for t in range(4):
        share[pl.ds(t * T, T), :] = total[t * T : (t + 1) * T].T
    for _, copy in sends.values():
        copy.wait_send()
    ycopy.wait_send()


def context_panel_sum(partial):
    n = len(X_STEPS)
    return pl.pallas_call(
        context_panel_kernel,
        in_specs=[VMEM],
        out_specs=VMEM,
        out_shape=jax.ShapeDtypeStruct((SHARE, T), F32),
        scratch_shapes=[
            pltpu.VMEM((n, CODE, T), I16),
            pltpu.VMEM((n, CODE, T), I16),
            pltpu.VMEM((CODE, T), I16),
            pltpu.VMEM((CODE, T), I16),
            DMA((n,)), DMA((n,)), DMA((1,)), DMA((1,)),
        ],
        compiler_params=pltpu.CompilerParams(collective_id=2, has_side_effects=True, vmem_limit_bytes=8 << 20),
        name="context_panel_sum",
    )(partial)


def shards(tile_counts, tile_rows, tile_cols, panel):
    counts, rows, cols = tile_counts[0, 0], tile_rows[0, 0], tile_cols[0, 0]
    counts = pltpu.with_memory_space_constraint(counts, pltpu.HBM)
    words_all, contexts_all, band, held = totals(rows, cols, counts, panel)
    band = band.reshape(COL_TILES, T, T)
    tiles, partial = word_products(rows, cols, held, words_all, contexts_all, band)
    share, everyone = word_panel_sum(partial.reshape(NZ, NYH, NC, SHARE, T))
    rounded = everyone.reshape(ROW_TILES, T, T)
    context_partial, share = context_products(rows, cols, tiles, rounded, share)
    context_share = context_panel_sum(context_partial.reshape(NYL, NX, SHARE, T))
    return share, context_share


def solution(mesh):
    split = Mesh(
        mesh.devices.reshape(NYL, NX, NZ, NYH, NC), ("yl", "x", "z", "yh", "core")
    )
    row, col = ("yl", "x"), ("z", "yh", "core")
    in_specs = (
        P(row, col, None, None, None),
        P(row, col, None),
        P(row, col, None),
        P(col + row, None),
    )
    out_specs = (P(row + col, None), P(col + row, None))
    return jax.shard_map(shards, mesh=split, in_specs=in_specs, out_specs=out_specs, check_vma=False)
```

```python
import functools
import math

import jax
import jax.numpy as jnp
from jax import lax
from jax.experimental import pallas as pl
from jax.experimental.pallas import tpu as pltpu
from jax.sharding import Mesh
from jax.sharding import PartitionSpec as P

NEG_SAMPLES = 15
T = 128
NX, NYL, NYH, NZ, NC = 4, 2, 2, 8, 2
N_ROW, N_COL = NX * NYL, NZ * NYH * NC
ROW_TILES, COL_TILES = 128, 32
SHARE = 512
HALF = SHARE // 2
CODE = HALF + 16
MESH = pl.DeviceIdType.MESH
F32, BF16, I32, I16 = jnp.float32, jnp.bfloat16, jnp.int32, jnp.int16
ANY = pl.BlockSpec(memory_space=pl.ANY)
VMEM = pl.BlockSpec(memory_space=pltpu.VMEM)
SMEM = pl.BlockSpec(memory_space=pltpu.SMEM)
DMA = pltpu.SemaphoreType.DMA
LN2 = math.log(2.0)


def remote(src, dst, ssem, rsem, device):
    return pltpu.make_async_remote_copy(
        src_ref=src, dst_ref=dst, send_sem=ssem, recv_sem=rsem,
        device_id=device, device_id_type=MESH,
    )


def greet(devices):
    barrier = pltpu.get_barrier_semaphore()
    for device in devices:
        pl.semaphore_signal(barrier, inc=1, device_id=device, device_id_type=MESH)
    pl.semaphore_wait(barrier, len(devices))


def encode(value, ref):
    top = jnp.max(jnp.abs(value), axis=0, keepdims=True)
    expo = jnp.ceil(jnp.log(jnp.maximum(top, 1e-30)) * (1.0 / LN2) + 0.001) - 14.0
    scaled = jnp.round(value * jnp.exp(expo * -LN2))
    ref[pl.ds(0, HALF), :] = scaled.astype(I32).astype(I16)
    ref[pl.ds(HALF, 16), :] = jnp.broadcast_to(expo, (16, T)).astype(I32).astype(I16)


def decode(ref):
    expo = ref[pl.ds(HALF, 16), :].astype(I32).astype(F32)[0:1]
    return ref[pl.ds(0, HALF), :].astype(I32).astype(F32) * jnp.exp(expo * LN2)


GROUP = 16


def powers_of(totals):
    root = jnp.sqrt(totals)
    return root * jnp.sqrt(root)


def load_counts(counts, held, sem):
    copies = []
    for b in range(counts.shape[0] // GROUP):
        part = pl.ds(b * GROUP, GROUP)
        copies.append(pltpu.make_async_copy(counts.at[part], held.at[part], sem.at[b]))
        copies[-1].start()
    return copies


def await_counts(counts, held, sem, b):
    part = pl.ds(b * GROUP, GROUP)
    pltpu.make_async_copy(counts.at[part], held.at[part], sem.at[b]).wait()


def totals_kernel(rows, cols, counts, panel, words_all, contexts_all, band, held,
                  wacc, words, contexts, wrecv, crecv, mine,
                  cs, wss, wrs, css, crs, ass, ars, pss, prs, lsem):
    x, yl = lax.axis_index("x"), lax.axis_index("yl")
    z, yh, c = lax.axis_index("z"), lax.axis_index("yh"), lax.axis_index("core")
    row = yl * NX + x
    col = (z * NYH + yh) * NC + c
    row_peers = [
        (dx * NYL + dy, {"x": lax.rem(x + dx, NX), "yl": lax.rem(yl + dy, NYL)})
        for dx in range(NX) for dy in range(NYL) if dx or dy
    ]
    col_peers = []
    for dz in (4, 3, 5, 2, 6, 1, 7, 0):
        for dy in (1, 0):
            for dc in range(NC):
                if dz or dy or dc:
                    pz, py, pc = lax.rem(z + dz, NZ), lax.rem(yh + dy, NYH), lax.rem(c + dc, NC)
                    col_peers.append(
                        ((dz * NYH + dy) * NC + dc, (pz * NYH + py) * NC + pc,
                         {"z": pz, "yh": py, "core": pc})
                    )
    load_counts(counts, held, cs)
    greet([d for _, d in row_peers] + [d for _, _, d in col_peers])
    psends = {k: remote(panel, band.at[row], pss.at[k], prs.at[k], d) for k, d in row_peers}
    own = pltpu.make_async_copy(panel, band.at[row], lsem.at[0])
    for dx, dy in ((1, 0), (3, 0), (0, 1)):
        psends[dx * NYL + dy].start()
    own.start()

    wacc[...] = jnp.zeros_like(wacc)
    lanes = lax.broadcasted_iota(I32, (T, T), 1)
    bands = lax.broadcasted_iota(I32, (COL_TILES, T), 0)

    def some(b, per_context):
        await_counts(counts, held, cs, b)
        per_word = wacc[...]
        for g in range(GROUP):
            slot = b * GROUP + g
            value = held[slot]
            per_context = per_context + jnp.where(
                bands == cols[slot], jnp.sum(value, axis=0, keepdims=True), 0
            )
            sums = jnp.sum(value.astype(F32), axis=1, keepdims=True)
            per_word = per_word + jnp.where(lanes == rows[slot], sums, 0.0)
        wacc[...] = per_word
        return per_context

    per_context = lax.fori_loop(0, counts.shape[0] // GROUP, some, jnp.zeros((COL_TILES, T), I32))
    contexts[...] = per_context.astype(F32)
    csends = [remote(contexts, crecv.at[k], css.at[k], crs.at[k], d) for k, d in row_peers]
    for copy in csends:
        copy.start()
    for d in range(N_COL):
        words[d, 0:4, :] = wacc[pl.ds(4 * d, 4), :]
        words[d, 4:8, :] = jnp.zeros((4, T), F32)
    wsends = [remote(words.at[p], wrecv.at[k], wss.at[k], wrs.at[k], d) for k, p, d in col_peers]
    for copy in wsends:
        copy.start()
    for dx, dy in ((1, 1), (3, 1)):
        psends[dx * NYL + dy].start()

    for copy in csends:
        copy.wait_recv()
    contexts_sum = contexts[...]
    for k, _ in row_peers:
        contexts_sum = contexts_sum + crecv[k]
    contexts_all[...] = contexts_sum
    band_power = jnp.sum(powers_of(contexts_sum), keepdims=True)

    for copy in wsends:
        copy.wait_recv()
    words_sum = words[col]
    for k, _, _ in col_peers:
        words_sum = words_sum + wrecv[k]
    at = lax.broadcasted_iota(I32, (8, T), 0)
    mine[...] = jnp.where(at == 4, jnp.broadcast_to(band_power, (8, T)), words_sum)
    asends = [remote(mine, words_all.at[col], ass.at[k], ars.at[k], d) for k, _, d in col_peers]
    for copy in asends:
        copy.start()
    for dx, dy in ((2, 0), (2, 1)):
        psends[dx * NYL + dy].start()
    words_all[col] = mine[...]
    for copy in asends:
        copy.wait()
    for copy in csends + wsends:
        copy.wait_send()
    for copy in psends.values():
        copy.wait()
    own.wait()


def totals(rows, cols, counts, panel):
    slots = counts.shape[0]
    return pl.pallas_call(
        totals_kernel,
        in_specs=[SMEM, SMEM, ANY, ANY],
        out_specs=[VMEM, VMEM, ANY, VMEM],
        out_shape=[
            jax.ShapeDtypeStruct((N_COL, 8, T), F32),
            jax.ShapeDtypeStruct((COL_TILES, T), F32),
            jax.ShapeDtypeStruct((N_ROW, SHARE, T), BF16),
            jax.ShapeDtypeStruct((slots, T, T), I32),
        ],
        scratch_shapes=[
            pltpu.VMEM((T, ROW_TILES), F32),
            pltpu.VMEM((N_COL, 8, T), F32),
            pltpu.VMEM((COL_TILES, T), F32),
            pltpu.VMEM((N_COL, 8, T), F32),
            pltpu.VMEM((N_ROW, COL_TILES, T), F32),
            pltpu.VMEM((8, T), F32),
            DMA((slots // GROUP,)),
            DMA((N_COL,)), DMA((N_COL,)), DMA((N_ROW,)), DMA((N_ROW,)),
            DMA((N_COL,)), DMA((N_COL,)), DMA((N_ROW,)), DMA((N_ROW,)), DMA((1,)),
        ],
        compiler_params=pltpu.CompilerParams(collective_id=0, has_side_effects=True, vmem_limit_bytes=16 << 20),
        name="totals",
    )(rows, cols, counts, panel)


def word_kernel(rows, cols, counts, words_all, contexts_all, band, tiles, partial,
                word_term, context_log):
    power = jnp.zeros((1, T), F32)
    for d in range(N_COL):
        word_term[pl.ds(4 * d, 4), :] = words_all[d, 0:4, :]
        power = power + words_all[d, 4:5, :]
    log_scale = jnp.log(power) - math.log(NEG_SAMPLES)
    word_term[...] = log_scale - jnp.log(jnp.maximum(word_term[...], 1.0))
    context_log[...] = jnp.log(jnp.maximum(powers_of(contexts_all[...]), 1.0))

    def clear(t, carry):
        partial[t] = jnp.zeros((T, T), F32)
        return carry

    lax.fori_loop(0, ROW_TILES, clear, 0, unroll=4)

    def some(b, carry):
        for g in range(GROUP):
            slot = b * GROUP + g
            row, col = rows[slot], cols[slot]
            value = counts[slot]
            per_word = jnp.take_along_axis(word_term[...], jnp.full((T, T), row, I32), axis=1)
            pointwise = jnp.log(value.astype(F32)) + per_word - context_log[pl.ds(col, 1), :]
            tile = jnp.where(value > 0, jnp.maximum(pointwise, 0.0), 0.0).astype(BF16)
            tiles[slot] = tile
            partial[row] += jnp.dot(tile, band[col], preferred_element_type=F32)
        return carry

    lax.fori_loop(0, counts.shape[0] // GROUP, some, 0)


def word_products(rows, cols, counts, words_all, contexts_all, band):
    slots = counts.shape[0]
    return pl.pallas_call(
        word_kernel,
        in_specs=[SMEM, SMEM, VMEM, VMEM, VMEM, VMEM],
        out_specs=[VMEM, VMEM],
        scratch_shapes=[pltpu.VMEM((T, ROW_TILES), F32), pltpu.VMEM((COL_TILES, T), F32)],
        out_shape=[
            jax.ShapeDtypeStruct((slots, T, T), BF16),
            jax.ShapeDtypeStruct((ROW_TILES, T, T), F32),
        ],
        compiler_params=pltpu.CompilerParams(vmem_limit_bytes=28 << 20),
        name="word_products",
    )(rows, cols, counts, words_all, contexts_all, band)


AWAY = (0, 1, 0)


def lane_steps(length):
    steps = []
    for s in range(length):
        for lanes in ((0, 1), (2,)):
            for far in (False, True):
                for lane in lanes:
                    for way in range(2):
                        if (way == AWAY[lane]) == far and (far or s):
                            steps.append((s, way, lane))
    return steps


Z_STEPS = lane_steps(NZ // 2)
X_STEPS = lane_steps(NX // 2)


def ring_sum(steps, length, y, raw, ready, ways, other_y, sendb, recvb, ysendb, yrecvb,
             ss, rs, yss, yrs):
    trades, sends, traded = {}, {}, set()

    def trade(d):
        ready(d)
        encode(raw(d, 1 - y, 1), ysendb.at[d])
        trades[d] = remote(ysendb.at[d], yrecvb.at[d], yss.at[d], yrs.at[d], other_y)
        trades[d].start()

    def term(d, lane):
        if lane < 2:
            return raw(d, lane, 0)
        if d not in traded:
            trades[d].wait_recv()
            traded.add(d)
        return raw(d, y, 1) + decode(yrecvb.at[d])

    trade(length)
    for n, (s, way, lane) in enumerate(steps):
        if lane == 2 and (n == 0 or steps[n - 1][2] != 2):
            for d in sorted({length - s - 1, (length + s + 1) % (2 * length)}):
                trade(d)
        d = length - s if way == 0 else length + s
        value = term(d, lane)
        if (s - 1, way, lane) in sends:
            index, before = sends[s - 1, way, lane]
            before.wait_recv()
            value = value + decode(recvb.at[index])
        encode(value, sendb.at[n])
        copy = remote(sendb.at[n], recvb.at[n], ss.at[n], rs.at[n], ways[way])
        copy.start()
        sends[s, way, lane] = (n, copy)

    last = length - 1
    for lane in (0, 1):
        for way in range(2):
            sends[last, way, lane][1].wait_recv()

    def arrived(h):
        value = raw(0, h, 0)
        for way in range(2):
            first, second = sends[last, way, 0][0], sends[last, way, 1][0]
            value = value + decode(recvb.at[first + h * (second - first)])
        return value

    end = 2 * length
    encode(arrived(1 - y), ysendb.at[end])
    swap = remote(ysendb.at[end], yrecvb.at[end], yss.at[end], yrs.at[end], other_y)
    swap.start()
    second = term(0, 2)
    for way in range(2):
        index, copy = sends[last, way, 2]
        copy.wait_recv()
        second = second + decode(recvb.at[index])
    first = arrived(y)
    swap.wait_recv()
    first = first + decode(yrecvb.at[end])

    def drain():
        for _, copy in sends.values():
            copy.wait_send()
        for copy in trades.values():
            copy.wait_send()
        swap.wait_send()

    return first, second, drain


def ring_scratch(steps, length):
    n, y = len(steps), 2 * length + 1
    return [
        pltpu.VMEM((n, CODE, T), I16), pltpu.VMEM((n, CODE, T), I16),
        pltpu.VMEM((y, CODE, T), I16), pltpu.VMEM((y, CODE, T), I16),
        DMA((n,)), DMA((n,)), DMA((y,)), DMA((y,)),
    ]


def word_panel_kernel(partial, share, everyone, sib, mine, xss, xrs, gss, grs, hss, hrs, pss, prs, ms,
                      *ring):
    z, yh, c = lax.axis_index("z"), lax.axis_index("yh"), lax.axis_index("core")
    ways = ({"z": lax.rem(z + 1, NZ)}, {"z": lax.rem(z + NZ - 1, NZ)})
    other_y, other_core = {"yh": 1 - yh}, {"core": 1 - c}
    length = NZ // 2

    greet([*ways, other_y, other_core])
    swaps = {}
    for dz in (4, 3, 5, 2, 6, 1, 7, 0):
        for h in range(2):
            slot, zz = dz * 2 + h, lax.rem(z + dz, NZ)
            swaps[dz, h] = remote(partial.at[zz, h, 1 - c], sib.at[slot], xss.at[slot], xrs.at[slot], other_core)
            swaps[dz, h].start()

    def ready(d):
        for h in range(2):
            swaps[d, h].wait_recv()

    def raw(d, h, part):
        rows = pl.ds(part * HALF, HALF)
        return partial[lax.rem(z + d, NZ), h, c, rows, :] + sib[d * 2 + h, rows, :]

    first, second, drain = ring_sum(Z_STEPS, length, yh, raw, ready, ways, other_y, *ring)
    for part, total in enumerate((first, second)):
        share[pl.ds(part * HALF, HALF), :] = total
        for t in range(2):
            mine[part * 2 + t] = total[t * T : (t + 1) * T].T.astype(BF16)

    pair = (pl.ds(0, 2), pl.ds(2, 2))

    def place(d, h, part):
        return everyone.at[lax.rem(z + d, NZ), h, c, pair[part]]

    keep = pltpu.make_async_copy(mine, everyone.at[z, yh, c], ms.at[0])
    keep.start()
    gives, hands, passes = {}, [], {}

    def hand(src, dst, k):
        copy = remote(src, dst, hss.at[k], hrs.at[k], other_core)
        copy.start()
        hands.append(copy)

    def along_y(src, dst, k):
        passes[k] = remote(src, dst, pss.at[k], prs.at[k], other_y)
        passes[k].start()

    def lane_place(d, lane):
        return place(d, 1 - yh if lane == 1 else yh, 1 if lane == 2 else 0)

    def give(s, way, lane, src=None):
        dst = lane_place((NZ - s) % NZ if way == 0 else s, lane)
        k = (s * 2 + way) * 3 + lane
        gives[s, way, lane] = remote(dst if src is None else src, dst, gss.at[k], grs.at[k], ways[way])
        gives[s, way, lane].start()

    own = (mine.at[pair[0]], mine.at[pair[1]])
    along_y(own[0], place(0, yh, 0), NZ)
    for way in range(2):
        give(0, way, 2, own[1])
    for way in range(2):
        give(0, way, 0, own[0])
    along_y(own[1], place(0, yh, 1), 0)
    hand(own[0], place(0, yh, 0), 0)
    hand(own[1], place(0, yh, 1), 2 * NZ)
    passes[NZ].wait_recv()
    for way in range(2):
        give(0, way, 1)
    hand(lane_place(0, 1), lane_place(0, 1), 1)
    due = [0]
    for s in range(1, length + 1):
        came = []
        for lane in (2, 0, 1):
            for way in range(2):
                if (s - 1, way, lane) not in gives:
                    continue
                gives[s - 1, way, lane].wait_recv()
                if s < length - 1 or (s == length - 1 and way == AWAY[lane]):
                    give(s, way, lane)
                d = (NZ - s) % NZ if way == 0 else s
                at = lane_place(d, lane)
                if lane == 2:
                    along_y(at, at, d)
                    came.append(d)
                hand(at, at, 2 * NZ + d if lane == 2 else d * 2 + lane)
        for d in due:
            passes[d].wait_recv()
            hand(place(d, 1 - yh, 1), place(d, 1 - yh, 1), 3 * NZ + d)
        due = came
    for d in due:
        passes[d].wait_recv()
        hand(place(d, 1 - yh, 1), place(d, 1 - yh, 1), 3 * NZ + d)

    for copy in hands:
        copy.wait()
    for copy in list(gives.values()) + list(passes.values()) + list(swaps.values()):
        copy.wait_send()
    drain()
    keep.wait()


def word_panel_sum(partial):
    return pl.pallas_call(
        word_panel_kernel,
        in_specs=[VMEM],
        out_specs=[VMEM, ANY],
        out_shape=[
            jax.ShapeDtypeStruct((SHARE, T), F32),
            jax.ShapeDtypeStruct((NZ, NYH, NC, 4, T, T), BF16),
        ],
        scratch_shapes=[
            pltpu.VMEM((2 * NZ, SHARE, T), F32),
            pltpu.VMEM((4, T, T), BF16),
            DMA((2 * NZ,)), DMA((2 * NZ,)), DMA((3 * NZ,)), DMA((3 * NZ,)),
            DMA((4 * NZ,)), DMA((4 * NZ,)), DMA((NZ + 1,)), DMA((NZ + 1,)), DMA((1,)),
            *ring_scratch(Z_STEPS, NZ // 2),
        ],
        compiler_params=pltpu.CompilerParams(collective_id=1, has_side_effects=True, vmem_limit_bytes=16 << 20),
        name="word_panel_sum",
    )(partial)


def context_kernel(rows, cols, tiles, rounded, share, partial, share_out):
    share_out[...] = share[...]
    partial[...] = jnp.zeros_like(partial)

    def some(b, carry):
        for g in range(GROUP):
            slot = b * GROUP + g
            partial[cols[slot]] += jnp.dot(rounded[rows[slot]], tiles[slot], preferred_element_type=F32)
        return carry

    lax.fori_loop(0, tiles.shape[0] // GROUP, some, 0)


def context_products(rows, cols, tiles, rounded, share):
    slots = tiles.shape[0]
    return pl.pallas_call(
        context_kernel,
        in_specs=[SMEM, SMEM, VMEM, VMEM, VMEM],
        out_specs=[VMEM, VMEM],
        out_shape=[
            jax.ShapeDtypeStruct((COL_TILES, T, T), F32),
            jax.ShapeDtypeStruct((SHARE, T), F32),
        ],
        compiler_params=pltpu.CompilerParams(vmem_limit_bytes=16 << 20),
        name="context_products",
    )(rows, cols, tiles, rounded, share)


def context_panel_kernel(partial, share, *ring):
    x, yl = lax.axis_index("x"), lax.axis_index("yl")
    ways = ({"x": lax.rem(x + 1, NX)}, {"x": lax.rem(x + NX - 1, NX)})
    other_y = {"yl": 1 - yl}
    greet([*ways, other_y])

    def raw(d, h, part):
        return partial[h, lax.rem(x + d, NX), pl.ds(part * HALF, HALF), :]

    first, second, drain = ring_sum(
        X_STEPS, NX // 2, yl, raw, lambda d: None, ways, other_y, *ring
    )
    for part, total in enumerate((first, second)):
        total = total * (1.0 / T)
        for t in range(2):
            share[pl.ds(part * HALF + t * T, T), :] = total[t * T : (t + 1) * T].T
    drain()


def context_panel_sum(partial):
    return pl.pallas_call(
        context_panel_kernel,
        in_specs=[VMEM],
        out_specs=VMEM,
        out_shape=jax.ShapeDtypeStruct((SHARE, T), F32),
        scratch_shapes=ring_scratch(X_STEPS, NX // 2),
        compiler_params=pltpu.CompilerParams(collective_id=2, has_side_effects=True, vmem_limit_bytes=8 << 20),
        name="context_panel_sum",
    )(partial)


def shards(tile_counts, tile_rows, tile_cols, panel):
    counts, rows, cols = tile_counts[0, 0], tile_rows[0, 0], tile_cols[0, 0]
    counts = pltpu.with_memory_space_constraint(counts, pltpu.HBM)
    words_all, contexts_all, band, held = totals(rows, cols, counts, panel)
    band = band.reshape(COL_TILES, T, T)
    tiles, partial = word_products(rows, cols, held, words_all, contexts_all, band)
    share, everyone = word_panel_sum(partial.reshape(NZ, NYH, NC, SHARE, T))
    rounded = everyone.reshape(ROW_TILES, T, T)
    context_partial, share = context_products(rows, cols, tiles, rounded, share)
    context_share = context_panel_sum(context_partial.reshape(NYL, NX, SHARE, T))
    return share, context_share


def solution(mesh):
    split = Mesh(
        mesh.devices.reshape(NYL, NX, NZ, NYH, NC), ("yl", "x", "z", "yh", "core")
    )
    row, col = ("yl", "x"), ("z", "yh", "core")
    in_specs = (
        P(row, col, None, None, None),
        P(row, col, None),
        P(row, col, None),
        P(col + row, None),
    )
    out_specs = (P(row + col, None), P(col + row, None))
    return jax.shard_map(shards, mesh=split, in_specs=in_specs, out_specs=out_specs, check_vma=False)
```

```python
import functools
import math

import jax
import jax.numpy as jnp
from jax import lax
from jax.experimental import pallas as pl
from jax.experimental.pallas import tpu as pltpu
from jax.sharding import Mesh
from jax.sharding import PartitionSpec as P

NEG_SAMPLES = 15
T = 128
NX, NYL, NYH, NZ, NC = 4, 2, 2, 8, 2
N_ROW, N_COL = NX * NYL, NZ * NYH * NC
ROW_TILES, COL_TILES = 128, 32
SHARE = 512
HALF = SHARE // 2
CODE = HALF + 16
MESH = pl.DeviceIdType.MESH
F32, BF16, I32, I16 = jnp.float32, jnp.bfloat16, jnp.int32, jnp.int16
ANY = pl.BlockSpec(memory_space=pl.ANY)
VMEM = pl.BlockSpec(memory_space=pltpu.VMEM)
SMEM = pl.BlockSpec(memory_space=pltpu.SMEM)
DMA = pltpu.SemaphoreType.DMA
LN2 = math.log(2.0)


def remote(src, dst, ssem, rsem, device):
    return pltpu.make_async_remote_copy(
        src_ref=src, dst_ref=dst, send_sem=ssem, recv_sem=rsem,
        device_id=device, device_id_type=MESH,
    )


def hail(devices):
    for device in devices:
        pl.semaphore_signal(
            pltpu.get_barrier_semaphore(), inc=1, device_id=device, device_id_type=MESH
        )


def await_hails(devices):
    pl.semaphore_wait(pltpu.get_barrier_semaphore(), len(devices))


def greet(devices):
    hail(devices)
    await_hails(devices)


def encode(value, ref):
    top = jnp.max(jnp.abs(value), axis=0, keepdims=True)
    expo = jnp.ceil(jnp.log(jnp.maximum(top, 1e-30)) * (1.0 / LN2) + 0.001) - 14.0
    scaled = jnp.round(value * jnp.exp(expo * -LN2))
    ref[pl.ds(0, HALF), :] = scaled.astype(I32).astype(I16)
    ref[pl.ds(HALF, 16), :] = jnp.broadcast_to(expo, (16, T)).astype(I32).astype(I16)


def decode(ref):
    expo = ref[pl.ds(HALF, 16), :].astype(I32).astype(F32)[0:1]
    return ref[pl.ds(0, HALF), :].astype(I32).astype(F32) * jnp.exp(expo * LN2)


GROUP = 16


def powers_of(totals):
    root = jnp.sqrt(totals)
    return root * jnp.sqrt(root)


def load_counts(counts, held, sem):
    copies = []
    for b in range(counts.shape[0] // GROUP):
        part = pl.ds(b * GROUP, GROUP)
        copies.append(pltpu.make_async_copy(counts.at[part], held.at[part], sem.at[b]))
        copies[-1].start()
    return copies


def await_counts(counts, held, sem, b):
    part = pl.ds(b * GROUP, GROUP)
    pltpu.make_async_copy(counts.at[part], held.at[part], sem.at[b]).wait()


def totals_kernel(rows_in, cols_in, counts, panel, words_all, band, base,
                  held, rows, cols, wacc, words, contexts, context_log, wrecv, crecv, mine,
                  cs, wss, wrs, css, crs, ass, ars, pss, prs, lsem):
    x, yl = lax.axis_index("x"), lax.axis_index("yl")
    z, yh, c = lax.axis_index("z"), lax.axis_index("yh"), lax.axis_index("core")
    blocks = counts.shape[0] // GROUP
    row = yl * NX + x
    col = (z * NYH + yh) * NC + c
    right, left = lax.rem(x + 1, NX), lax.rem(x + NX - 1, NX)
    row_peers = [
        (dx * NYL + dy, {"x": lax.rem(x + dx, NX), "yl": lax.rem(yl + dy, NYL)})
        for dx in range(NX) for dy in range(NYL) if dx or dy
    ]
    col_peers = []
    for dz in (4, 3, 5, 2, 6, 1, 7, 0):
        for dy in (1, 0):
            for dc in range(NC):
                if dz or dy or dc:
                    pz, py, pc = lax.rem(z + dz, NZ), lax.rem(yh + dy, NYH), lax.rem(c + dc, NC)
                    col_peers.append(
                        ((dz * NYH + dy) * NC + dc, (pz * NYH + py) * NC + pc,
                         {"z": pz, "yh": py, "core": pc})
                    )
    everybody = [d for _, d in row_peers] + [d for _, _, d in col_peers]
    hail(everybody)
    slots = [
        pltpu.make_async_copy(rows_in, rows, lsem.at[1]),
        pltpu.make_async_copy(cols_in, cols, lsem.at[2]),
    ]
    for copy in slots:
        copy.start()
    load_counts(counts, held, cs)
    own = pltpu.make_async_copy(panel, band.at[row], lsem.at[0])
    own.start()

    wacc[...] = jnp.zeros_like(wacc)
    lanes = lax.broadcasted_iota(I32, (T, T), 1)
    bands = lax.broadcasted_iota(I32, (COL_TILES, T), 0)
    for copy in slots:
        copy.wait()

    def some(b, per_context):
        await_counts(counts, held, cs, b)
        per_word = wacc[...]
        for g in range(GROUP):
            slot = b * GROUP + g
            value = held[slot]
            per_context = per_context + jnp.where(
                bands == cols[slot], jnp.sum(value, axis=0, keepdims=True), 0
            )
            sums = jnp.sum(value.astype(F32), axis=1, keepdims=True)
            per_word = per_word + jnp.where(lanes == rows[slot], sums, 0.0)
        wacc[...] = per_word
        return per_context

    per_context = lax.fori_loop(0, blocks, some, jnp.zeros((COL_TILES, T), I32))
    contexts[...] = per_context.astype(F32)
    for d in range(N_COL):
        words[d, 0:4, :] = wacc[pl.ds(4 * d, 4), :]
        words[d, 4:8, :] = jnp.zeros((4, T), F32)
    await_hails(everybody)

    csends = [remote(contexts, crecv.at[k], css.at[k], crs.at[k], d) for k, d in row_peers]
    for copy in csends:
        copy.start()
    wsends = [remote(words.at[p], wrecv.at[k], wss.at[k], wrs.at[k], d) for k, p, d in col_peers]
    for copy in wsends:
        copy.start()

    psends = []

    def pass_on(src, dst, device):
        k = len(psends)
        psends.append(remote(src, dst, pss.at[k], prs.at[k], device))
        psends[k].start()

    def to_right_and_left(first, second):
        pass_on(first, first, {"x": right})
        pass_on(second, second, {"x": left})

    def relay(y):
        to_right_and_left(
            band.at[y * NX + left, pl.ds(0, HALF)], band.at[y * NX + right, pl.ds(HALF, HALF)]
        )

    pass_on(panel, band.at[row], {"yl": 1 - yl})
    pass_on(panel, band.at[row], {"x": right})
    pass_on(panel, band.at[row], {"x": left})

    for copy in csends:
        copy.wait_recv()
    contexts_sum = contexts[...]
    for k, _ in row_peers:
        contexts_sum = contexts_sum + crecv[k]
    powers = powers_of(contexts_sum)
    band_power = jnp.sum(powers, keepdims=True)
    context_log[...] = jnp.log(jnp.maximum(powers, 1.0))

    for copy in psends[0:3]:
        copy.wait_recv()
    there = band.at[(1 - yl) * NX + x]
    to_right_and_left(there, there)
    relay(yl)

    for copy in wsends:
        copy.wait_recv()
    words_sum = words[col]
    for k, _, _ in col_peers:
        words_sum = words_sum + wrecv[k]
    at = lax.broadcasted_iota(I32, (8, T), 0)
    mine[...] = jnp.where(at == 4, jnp.broadcast_to(band_power, (8, T)), words_sum)
    asends = [remote(mine, words_all.at[col], ass.at[k], ars.at[k], d) for k, _, d in col_peers]
    for copy in asends:
        copy.start()
    words_all[col] = mine[...]

    def logs(b, carry):
        for g in range(GROUP):
            slot = b * GROUP + g
            value = held[slot].astype(F32)
            base[slot] = jnp.where(
                value > 0.0, jnp.log(value) - context_log[pl.ds(cols[slot], 1), :], -1e30
            )
        return carry

    lax.fori_loop(0, blocks // 2, logs, 0)
    for copy in psends[3:5]:
        copy.wait_recv()
    relay(1 - yl)
    lax.fori_loop(blocks // 2, blocks, logs, 0)

    for copy in asends:
        copy.wait()
    for copy in csends + wsends + psends[0:5]:
        copy.wait_send()
    for copy in psends[5:9]:
        copy.wait()
    own.wait()


def totals(rows, cols, counts, panel):
    slots = counts.shape[0]
    return pl.pallas_call(
        totals_kernel,
        in_specs=[ANY, ANY, ANY, ANY],
        out_specs=[VMEM, ANY, VMEM],
        out_shape=[
            jax.ShapeDtypeStruct((N_COL, 8, T), F32),
            jax.ShapeDtypeStruct((N_ROW, SHARE, T), BF16),
            jax.ShapeDtypeStruct((slots, T, T), F32),
        ],
        scratch_shapes=[
            pltpu.VMEM((slots, T, T), I32),
            pltpu.SMEM((slots,), I32),
            pltpu.SMEM((slots,), I32),
            pltpu.VMEM((T, ROW_TILES), F32),
            pltpu.VMEM((N_COL, 8, T), F32),
            pltpu.VMEM((COL_TILES, T), F32),
            pltpu.VMEM((COL_TILES, T), F32),
            pltpu.VMEM((N_COL, 8, T), F32),
            pltpu.VMEM((N_ROW, COL_TILES, T), F32),
            pltpu.VMEM((8, T), F32),
            DMA((slots // GROUP,)),
            DMA((N_COL,)), DMA((N_COL,)), DMA((N_ROW,)), DMA((N_ROW,)),
            DMA((N_COL,)), DMA((N_COL,)), DMA((9,)), DMA((9,)), DMA((3,)),
        ],
        compiler_params=pltpu.CompilerParams(collective_id=0, has_side_effects=True, vmem_limit_bytes=16 << 20),
        name="totals",
    )(rows, cols, counts, panel)


def word_kernel(rows, cols, base, words_all, band, tiles, partial, word_term):
    power = jnp.zeros((1, T), F32)
    for d in range(N_COL):
        word_term[pl.ds(4 * d, 4), :] = words_all[d, 0:4, :]
        power = power + words_all[d, 4:5, :]
    log_scale = jnp.log(power) - math.log(NEG_SAMPLES)
    word_term[...] = log_scale - jnp.log(jnp.maximum(word_term[...], 1.0))

    def clear(t, carry):
        partial[t] = jnp.zeros((T, T), F32)
        return carry

    lax.fori_loop(0, ROW_TILES, clear, 0, unroll=4)

    def some(b, carry):
        for g in range(GROUP):
            slot = b * GROUP + g
            row, col = rows[slot], cols[slot]
            per_word = jnp.take_along_axis(word_term[...], jnp.full((T, T), row, I32), axis=1)
            tile = jnp.maximum(base[slot] + per_word, 0.0).astype(BF16)
            tiles[slot] = tile
            partial[row] += jnp.dot(tile, band[col], preferred_element_type=F32)
        return carry

    lax.fori_loop(0, base.shape[0] // GROUP, some, 0)


def word_products(rows, cols, base, words_all, band):
    slots = base.shape[0]
    return pl.pallas_call(
        word_kernel,
        in_specs=[SMEM, SMEM, VMEM, VMEM, VMEM],
        out_specs=[VMEM, VMEM],
        scratch_shapes=[pltpu.VMEM((T, ROW_TILES), F32)],
        out_shape=[
            jax.ShapeDtypeStruct((slots, T, T), BF16),
            jax.ShapeDtypeStruct((ROW_TILES, T, T), F32),
        ],
        compiler_params=pltpu.CompilerParams(vmem_limit_bytes=28 << 20),
        name="word_products",
    )(rows, cols, base, words_all, band)


AWAY = (0, 1, 0)


def lane_steps(length):
    steps = []
    for s in range(length):
        for lanes in ((0, 1), (2,)):
            for far in (False, True):
                for lane in lanes:
                    for way in range(2):
                        if (way == AWAY[lane]) == far and (far or s):
                            steps.append((s, way, lane))
    return steps


Z_STEPS = lane_steps(NZ // 2)
X_STEPS = lane_steps(NX // 2)


def ring_sum(steps, length, y, raw, ready, ways, other_y, use, sendb, recvb,
             ysendb, yrecvb, ss, rs, yss, yrs):
    trades, sends, traded = {}, {}, set()

    def trade(d):
        ready(d)
        encode(raw(d, 1 - y, 1), ysendb.at[d])
        trades[d] = remote(ysendb.at[d], yrecvb.at[d], yss.at[d], yrs.at[d], other_y)
        trades[d].start()

    def term(d, lane):
        if lane < 2:
            return raw(d, lane, 0)
        if d not in traded:
            trades[d].wait_recv()
            traded.add(d)
        return raw(d, y, 1) + decode(yrecvb.at[d])

    trade(length)
    for n, (s, way, lane) in enumerate(steps):
        if lane == 2 and (n == 0 or steps[n - 1][2] != 2):
            for d in sorted({length - s - 1, (length + s + 1) % (2 * length)}):
                trade(d)
        d = length - s if way == 0 else length + s
        value = term(d, lane)
        if (s - 1, way, lane) in sends:
            index, before = sends[s - 1, way, lane]
            before.wait_recv()
            value = value + decode(recvb.at[index])
        encode(value, sendb.at[n])
        copy = remote(sendb.at[n], recvb.at[n], ss.at[n], rs.at[n], ways[way])
        copy.start()
        sends[s, way, lane] = (n, copy)

    last = length - 1
    for lane in (0, 1):
        for way in range(2):
            sends[last, way, lane][1].wait_recv()

    def arrived(h):
        value = raw(0, h, 0)
        for way in range(2):
            first, second = sends[last, way, 0][0], sends[last, way, 1][0]
            value = value + decode(recvb.at[first + h * (second - first)])
        return value

    end = 2 * length
    encode(arrived(1 - y), ysendb.at[end])
    swap = remote(ysendb.at[end], yrecvb.at[end], yss.at[end], yrs.at[end], other_y)
    swap.start()
    second = term(0, 2)
    for way in range(2):
        index, copy = sends[last, way, 2]
        copy.wait_recv()
        second = second + decode(recvb.at[index])
    use(1, second)
    first = arrived(y)
    swap.wait_recv()
    use(0, first + decode(yrecvb.at[end]))

    def drain():
        for _, copy in sends.values():
            copy.wait_send()
        for copy in trades.values():
            copy.wait_send()
        swap.wait_send()

    return drain


def ring_scratch(steps, length):
    n, y = len(steps), 2 * length + 1
    return [
        pltpu.VMEM((n, CODE, T), I16), pltpu.VMEM((n, CODE, T), I16),
        pltpu.VMEM((y, CODE, T), I16), pltpu.VMEM((y, CODE, T), I16),
        DMA((n,)), DMA((n,)), DMA((y,)), DMA((y,)),
    ]


def word_panel_kernel(partial, share, everyone, sib, mine, xss, xrs, gss, grs, hss, hrs, pss, prs, ms,
                      *ring):
    z, yh, c = lax.axis_index("z"), lax.axis_index("yh"), lax.axis_index("core")
    ways = ({"z": lax.rem(z + 1, NZ)}, {"z": lax.rem(z + NZ - 1, NZ)})
    other_y, other_core = {"yh": 1 - yh}, {"core": 1 - c}
    length = NZ // 2

    greet([*ways, other_y, other_core])
    swaps = {}
    for dz in (4, 3, 5, 2, 6, 1, 7, 0):
        for h in range(2):
            slot, zz = dz * 2 + h, lax.rem(z + dz, NZ)
            swaps[dz, h] = remote(partial.at[zz, h, 1 - c], sib.at[slot], xss.at[slot], xrs.at[slot], other_core)
            swaps[dz, h].start()

    def ready(d):
        for h in range(2):
            swaps[d, h].wait_recv()

    def raw(d, h, part):
        rows = pl.ds(part * HALF, HALF)
        return partial[lax.rem(z + d, NZ), h, c, rows, :] + sib[d * 2 + h, rows, :]

    pair = (pl.ds(0, 2), pl.ds(2, 2))

    def place(d, h, part):
        return everyone.at[lax.rem(z + d, NZ), h, c, pair[part]]

    gives, hands, passes, keeps = {}, [], {}, []

    def hand(src, dst, k):
        copy = remote(src, dst, hss.at[k], hrs.at[k], other_core)
        copy.start()
        hands.append(copy)

    def along_y(src, dst, k):
        passes[k] = remote(src, dst, pss.at[k], prs.at[k], other_y)
        passes[k].start()

    def lane_place(d, lane):
        return place(d, 1 - yh if lane == 1 else yh, 1 if lane == 2 else 0)

    def give(s, way, lane, src=None):
        dst = lane_place((NZ - s) % NZ if way == 0 else s, lane)
        k = (s * 2 + way) * 3 + lane
        gives[s, way, lane] = remote(dst if src is None else src, dst, gss.at[k], grs.at[k], ways[way])
        gives[s, way, lane].start()

    own = (mine.at[pair[0]], mine.at[pair[1]])

    def use(part, total):
        for t in range(2):
            mine[part * 2 + t] = total[t * T : (t + 1) * T].T.astype(BF16)
        along_y(own[part], place(0, yh, part), 0 if part else NZ)
        for way in range(2):
            give(0, way, 2 if part else 0, own[part])
        hand(own[part], place(0, yh, part), 2 * NZ if part else 0)
        keeps.append(pltpu.make_async_copy(own[part], place(0, yh, part), ms.at[part]))
        keeps[-1].start()
        share[pl.ds(part * HALF, HALF), :] = total

    drain = ring_sum(Z_STEPS, length, yh, raw, ready, ways, other_y, use, *ring)
    passes[NZ].wait_recv()
    for way in range(2):
        give(0, way, 1)
    hand(lane_place(0, 1), lane_place(0, 1), 1)
    due = [0]
    for s in range(1, length + 1):
        came = []
        for lane in (2, 0, 1):
            for way in range(2):
                if (s - 1, way, lane) not in gives:
                    continue
                gives[s - 1, way, lane].wait_recv()
                if s < length - 1 or (s == length - 1 and way == AWAY[lane]):
                    give(s, way, lane)
                d = (NZ - s) % NZ if way == 0 else s
                at = lane_place(d, lane)
                if lane == 2:
                    along_y(at, at, d)
                    came.append(d)
                hand(at, at, 2 * NZ + d if lane == 2 else d * 2 + lane)
        for d in due:
            passes[d].wait_recv()
            hand(place(d, 1 - yh, 1), place(d, 1 - yh, 1), 3 * NZ + d)
        due = came
    for d in due:
        passes[d].wait_recv()
        hand(place(d, 1 - yh, 1), place(d, 1 - yh, 1), 3 * NZ + d)

    for copy in hands:
        copy.wait()
    for copy in list(gives.values()) + list(passes.values()) + list(swaps.values()):
        copy.wait_send()
    drain()
    for copy in keeps:
        copy.wait()


def word_panel_sum(partial):
    return pl.pallas_call(
        word_panel_kernel,
        in_specs=[VMEM],
        out_specs=[VMEM, ANY],
        out_shape=[
            jax.ShapeDtypeStruct((SHARE, T), F32),
            jax.ShapeDtypeStruct((NZ, NYH, NC, 4, T, T), BF16),
        ],
        scratch_shapes=[
            pltpu.VMEM((2 * NZ, SHARE, T), F32),
            pltpu.VMEM((4, T, T), BF16),
            DMA((2 * NZ,)), DMA((2 * NZ,)), DMA((3 * NZ,)), DMA((3 * NZ,)),
            DMA((4 * NZ,)), DMA((4 * NZ,)), DMA((NZ + 1,)), DMA((NZ + 1,)), DMA((2,)),
            *ring_scratch(Z_STEPS, NZ // 2),
        ],
        compiler_params=pltpu.CompilerParams(collective_id=1, has_side_effects=True, vmem_limit_bytes=16 << 20),
        name="word_panel_sum",
    )(partial)


def context_kernel(rows, cols, tiles, rounded, share, partial, share_out):
    share_out[...] = share[...]
    partial[...] = jnp.zeros_like(partial)

    def some(b, carry):
        for g in range(GROUP):
            slot = b * GROUP + g
            partial[cols[slot]] += jnp.dot(rounded[rows[slot]], tiles[slot], preferred_element_type=F32)
        return carry

    lax.fori_loop(0, tiles.shape[0] // GROUP, some, 0)


def context_products(rows, cols, tiles, rounded, share):
    slots = tiles.shape[0]
    return pl.pallas_call(
        context_kernel,
        in_specs=[SMEM, SMEM, VMEM, VMEM, VMEM],
        out_specs=[VMEM, VMEM],
        out_shape=[
            jax.ShapeDtypeStruct((COL_TILES, T, T), F32),
            jax.ShapeDtypeStruct((SHARE, T), F32),
        ],
        compiler_params=pltpu.CompilerParams(vmem_limit_bytes=16 << 20),
        name="context_products",
    )(rows, cols, tiles, rounded, share)


def context_panel_kernel(partial, share, *ring):
    x, yl = lax.axis_index("x"), lax.axis_index("yl")
    ways = ({"x": lax.rem(x + 1, NX)}, {"x": lax.rem(x + NX - 1, NX)})
    other_y = {"yl": 1 - yl}
    greet([*ways, other_y])

    def raw(d, h, part):
        return partial[h, lax.rem(x + d, NX), pl.ds(part * HALF, HALF), :]

    def use(part, total):
        total = total * (1.0 / T)
        for t in range(2):
            share[pl.ds(part * HALF + t * T, T), :] = total[t * T : (t + 1) * T].T

    ring_sum(X_STEPS, NX // 2, yl, raw, lambda d: None, ways, other_y, use, *ring)()


def context_panel_sum(partial):
    return pl.pallas_call(
        context_panel_kernel,
        in_specs=[VMEM],
        out_specs=VMEM,
        out_shape=jax.ShapeDtypeStruct((SHARE, T), F32),
        scratch_shapes=ring_scratch(X_STEPS, NX // 2),
        compiler_params=pltpu.CompilerParams(collective_id=2, has_side_effects=True, vmem_limit_bytes=8 << 20),
        name="context_panel_sum",
    )(partial)


def shards(tile_counts, tile_rows, tile_cols, panel):
    counts, rows, cols = tile_counts[0, 0], tile_rows[0, 0], tile_cols[0, 0]
    far = [pltpu.with_memory_space_constraint(a, pltpu.HBM) for a in (rows, cols, counts, panel)]
    words_all, band, base = totals(*far)
    band = band.reshape(COL_TILES, T, T)
    tiles, partial = word_products(rows, cols, base, words_all, band)
    share, everyone = word_panel_sum(partial.reshape(NZ, NYH, NC, SHARE, T))
    rounded = everyone.reshape(ROW_TILES, T, T)
    context_partial, share = context_products(rows, cols, tiles, rounded, share)
    context_share = context_panel_sum(context_partial.reshape(NYL, NX, SHARE, T))
    return share, context_share


def solution(mesh):
    split = Mesh(
        mesh.devices.reshape(NYL, NX, NZ, NYH, NC), ("yl", "x", "z", "yh", "core")
    )
    row, col = ("yl", "x"), ("z", "yh", "core")
    in_specs = (
        P(row, col, None, None, None),
        P(row, col, None),
        P(row, col, None),
        P(col + row, None),
    )
    out_specs = (P(row + col, None), P(col + row, None))
    return jax.shard_map(shards, mesh=split, in_specs=in_specs, out_specs=out_specs, check_vma=False)
```

```python
import functools
import math

import jax
import jax.numpy as jnp
from jax import lax
from jax.experimental import pallas as pl
from jax.experimental.pallas import tpu as pltpu
from jax.sharding import Mesh
from jax.sharding import PartitionSpec as P

NEG_SAMPLES = 15
T = 128
NX, NYL, NYH, NZ, NC = 4, 2, 2, 8, 2
N_ROW, N_COL = NX * NYL, NZ * NYH * NC
ROW_TILES, COL_TILES = 128, 32
SHARE = 512
HALF = SHARE // 2
CODE = HALF + 16
MESH = pl.DeviceIdType.MESH
F32, BF16, I32, I16 = jnp.float32, jnp.bfloat16, jnp.int32, jnp.int16
ANY = pl.BlockSpec(memory_space=pl.ANY)
VMEM = pl.BlockSpec(memory_space=pltpu.VMEM)
SMEM = pl.BlockSpec(memory_space=pltpu.SMEM)
DMA = pltpu.SemaphoreType.DMA
LN2 = math.log(2.0)


def remote(src, dst, ssem, rsem, device):
    return pltpu.make_async_remote_copy(
        src_ref=src, dst_ref=dst, send_sem=ssem, recv_sem=rsem,
        device_id=device, device_id_type=MESH,
    )


def hail(devices):
    for device in devices:
        pl.semaphore_signal(
            pltpu.get_barrier_semaphore(), inc=1, device_id=device, device_id_type=MESH
        )


def await_hails(devices):
    pl.semaphore_wait(pltpu.get_barrier_semaphore(), len(devices))


def greet(devices):
    hail(devices)
    await_hails(devices)


def encode(value, ref):
    top = jnp.max(jnp.abs(value), axis=0, keepdims=True)
    expo = jnp.ceil(jnp.log(jnp.maximum(top, 1e-30)) * (1.0 / LN2) + 0.001) - 14.0
    scaled = jnp.round(value * jnp.exp(expo * -LN2))
    ref[pl.ds(0, HALF), :] = scaled.astype(I32).astype(I16)
    ref[pl.ds(HALF, 16), :] = jnp.broadcast_to(expo, (16, T)).astype(I32).astype(I16)


def decode(ref):
    expo = ref[pl.ds(HALF, 16), :].astype(I32).astype(F32)[0:1]
    return ref[pl.ds(0, HALF), :].astype(I32).astype(F32) * jnp.exp(expo * LN2)


GROUP = 16
PART = T // NZ


def powers_of(totals):
    root = jnp.sqrt(totals)
    return root * jnp.sqrt(root)


def load_counts(counts, held, sem):
    copies = []
    for b in range(counts.shape[0] // GROUP):
        part = pl.ds(b * GROUP, GROUP)
        copies.append(pltpu.make_async_copy(counts.at[part], held.at[part], sem.at[b]))
        copies[-1].start()
    return copies


def await_counts(counts, held, sem, b):
    part = pl.ds(b * GROUP, GROUP)
    pltpu.make_async_copy(counts.at[part], held.at[part], sem.at[b]).wait()


def totals_kernel(rows_in, cols_in, counts, panel, words_all, band, base,
                  held, rows, cols, wacc, contexts, context_log, wrecv, crecv, mine, qrecv,
                  cs, wss, wrs, css, crs, qss, qrs, ass, ars, pss, prs, lsem):
    x, yl = lax.axis_index("x"), lax.axis_index("yl")
    z, yh, c = lax.axis_index("z"), lax.axis_index("yh"), lax.axis_index("core")
    blocks = counts.shape[0] // GROUP
    row = yl * NX + x
    right, left = lax.rem(x + 1, NX), lax.rem(x + NX - 1, NX)
    row_peers = [
        (dx * NYL + dy, {"x": lax.rem(x + dx, NX), "yl": lax.rem(yl + dy, NYL)})
        for dx in range(NX) for dy in range(NYL) if dx or dy
    ]
    z_peers = [(dz, lax.rem(z + dz, NZ)) for dz in (4, 3, 5, 2, 6, 1, 7)]
    quad = [
        (dy * NC + dc, {"yh": lax.rem(yh + dy, NYH), "core": lax.rem(c + dc, NC)})
        for dy, dc in ((1, 0), (1, 1), (0, 1))
    ]
    everybody = [d for _, d in row_peers] + [{"z": p} for _, p in z_peers] + [d for _, d in quad]
    hail(everybody)
    slots = [
        pltpu.make_async_copy(rows_in, rows, lsem.at[1]),
        pltpu.make_async_copy(cols_in, cols, lsem.at[2]),
    ]
    for copy in slots:
        copy.start()
    load_counts(counts, held, cs)
    own = pltpu.make_async_copy(panel, band.at[row], lsem.at[0])
    own.start()

    wacc[...] = jnp.zeros_like(wacc)
    lanes = lax.broadcasted_iota(I32, (T, T), 1)
    bands = lax.broadcasted_iota(I32, (COL_TILES, T), 0)
    for copy in slots:
        copy.wait()

    def some(b, per_context):
        await_counts(counts, held, cs, b)
        per_word = wacc[...]
        for g in range(GROUP):
            slot = b * GROUP + g
            value = held[slot]
            per_context = per_context + jnp.where(
                bands == cols[slot], jnp.sum(value, axis=0, keepdims=True), 0
            )
            sums = jnp.sum(value.astype(F32), axis=1, keepdims=True)
            per_word = per_word + jnp.where(lanes == rows[slot], sums, 0.0)
        wacc[...] = per_word
        return per_context

    per_context = lax.fori_loop(0, blocks, some, jnp.zeros((COL_TILES, T), I32))
    contexts[...] = per_context.astype(F32)
    await_hails(everybody)

    csends = [remote(contexts, crecv.at[k], css.at[k], crs.at[k], d) for k, d in row_peers]
    for copy in csends:
        copy.start()
    wsends = [
        remote(wacc.at[pl.ds(pl.multiple_of(p * PART, PART), PART)], wrecv.at[k], wss.at[k], wrs.at[k], {"z": p})
        for k, p in z_peers
    ]
    for copy in wsends:
        copy.start()

    psends = []

    def pass_on(src, dst, device):
        k = len(psends)
        psends.append(remote(src, dst, pss.at[k], prs.at[k], device))
        psends[k].start()

    def to_right_and_left(first, second):
        pass_on(first, first, {"x": right})
        pass_on(second, second, {"x": left})

    def relay(y):
        to_right_and_left(
            band.at[y * NX + left, pl.ds(0, HALF)], band.at[y * NX + right, pl.ds(HALF, HALF)]
        )

    pass_on(panel, band.at[row], {"yl": 1 - yl})
    pass_on(panel, band.at[row], {"x": right})
    pass_on(panel, band.at[row], {"x": left})

    for copy in csends:
        copy.wait_recv()
    contexts_sum = contexts[...]
    for k, _ in row_peers:
        contexts_sum = contexts_sum + crecv[k]
    powers = powers_of(contexts_sum)
    band_power = jnp.sum(powers, keepdims=True)
    context_log[...] = jnp.log(jnp.maximum(powers, 1.0))

    for copy in psends[0:3]:
        copy.wait_recv()
    there = band.at[(1 - yl) * NX + x]
    to_right_and_left(there, there)
    relay(yl)

    for copy in wsends:
        copy.wait_recv()
    words_sum = wacc[pl.ds(pl.multiple_of(z * PART, PART), PART), :]
    for k, _ in z_peers:
        words_sum = words_sum + wrecv[k]
    mine[pl.ds(0, PART), :] = words_sum
    mine[pl.ds(PART, 8), :] = jnp.broadcast_to(band_power, (8, T))
    qsends = [remote(mine, qrecv.at[k], qss.at[k], qrs.at[k], d) for k, d in quad]
    for copy in qsends:
        copy.start()
    for copy in qsends:
        copy.wait_recv()
    total = mine[...]
    for k, _ in quad:
        total = total + qrecv[k]
    words_all[z] = total
    asends = [
        remote(words_all.at[z], words_all.at[z], ass.at[k], ars.at[k], {"z": p}) for k, p in z_peers
    ]
    for copy in asends:
        copy.start()

    def logs(b, carry):
        for g in range(GROUP):
            slot = b * GROUP + g
            value = held[slot].astype(F32)
            base[slot] = jnp.where(
                value > 0.0, jnp.log(value) - context_log[pl.ds(cols[slot], 1), :], -1e30
            )
        return carry

    lax.fori_loop(0, blocks // 2, logs, 0)
    for copy in psends[3:5]:
        copy.wait_recv()
    relay(1 - yl)
    lax.fori_loop(blocks // 2, blocks, logs, 0)

    for copy in asends:
        copy.wait()
    for copy in csends + wsends + qsends + psends[0:5]:
        copy.wait_send()
    for copy in psends[5:9]:
        copy.wait()
    own.wait()


def totals(rows, cols, counts, panel):
    slots = counts.shape[0]
    return pl.pallas_call(
        totals_kernel,
        in_specs=[ANY, ANY, ANY, ANY],
        out_specs=[VMEM, ANY, VMEM],
        out_shape=[
            jax.ShapeDtypeStruct((NZ, PART + 8, T), F32),
            jax.ShapeDtypeStruct((N_ROW, SHARE, T), BF16),
            jax.ShapeDtypeStruct((slots, T, T), F32),
        ],
        scratch_shapes=[
            pltpu.VMEM((slots, T, T), I32),
            pltpu.SMEM((slots,), I32),
            pltpu.SMEM((slots,), I32),
            pltpu.VMEM((T, ROW_TILES), F32),
            pltpu.VMEM((COL_TILES, T), F32),
            pltpu.VMEM((COL_TILES, T), F32),
            pltpu.VMEM((NZ, PART, T), F32),
            pltpu.VMEM((N_ROW, COL_TILES, T), F32),
            pltpu.VMEM((PART + 8, T), F32),
            pltpu.VMEM((NYH * NC, PART + 8, T), F32),
            DMA((slots // GROUP,)),
            DMA((NZ,)), DMA((NZ,)), DMA((N_ROW,)), DMA((N_ROW,)), DMA((NYH * NC,)), DMA((NYH * NC,)),
            DMA((NZ,)), DMA((NZ,)), DMA((9,)), DMA((9,)), DMA((3,)),
        ],
        compiler_params=pltpu.CompilerParams(collective_id=0, has_side_effects=True, vmem_limit_bytes=16 << 20),
        name="totals",
    )(rows, cols, counts, panel)


def word_kernel(rows, cols, base, words_all, band, tiles, partial, word_term):
    power = jnp.zeros((1, T), F32)
    for d in range(NZ):
        word_term[pl.ds(d * PART, PART), :] = words_all[d, 0:PART, :]
        power = power + words_all[d, PART : PART + 1, :]
    log_scale = jnp.log(power) - math.log(NEG_SAMPLES)
    word_term[...] = log_scale - jnp.log(jnp.maximum(word_term[...], 1.0))

    def clear(t, carry):
        partial[t] = jnp.zeros((T, T), F32)
        return carry

    lax.fori_loop(0, ROW_TILES, clear, 0, unroll=4)

    def some(b, carry):
        for g in range(GROUP):
            slot = b * GROUP + g
            row, col = rows[slot], cols[slot]
            per_word = jnp.take_along_axis(word_term[...], jnp.full((T, T), row, I32), axis=1)
            tile = jnp.maximum(base[slot] + per_word, 0.0).astype(BF16)
            tiles[slot] = tile
            partial[row] += jnp.dot(tile, band[col], preferred_element_type=F32)
        return carry

    lax.fori_loop(0, base.shape[0] // GROUP, some, 0)


def word_products(rows, cols, base, words_all, band):
    slots = base.shape[0]
    return pl.pallas_call(
        word_kernel,
        in_specs=[SMEM, SMEM, VMEM, VMEM, VMEM],
        out_specs=[VMEM, VMEM],
        scratch_shapes=[pltpu.VMEM((T, ROW_TILES), F32)],
        out_shape=[
            jax.ShapeDtypeStruct((slots, T, T), BF16),
            jax.ShapeDtypeStruct((ROW_TILES, T, T), F32),
        ],
        compiler_params=pltpu.CompilerParams(vmem_limit_bytes=28 << 20),
        name="word_products",
    )(rows, cols, base, words_all, band)


AWAY = (0, 1, 0)

Z_STEPS = (
    4, (0, 0, 0), (0, 1, 1), 3, 5,
    (1, 1, 0), (1, 0, 1), (1, 0, 0), (1, 1, 1), (0, 0, 2), 2, 6,
    (2, 1, 0), (2, 0, 1), (2, 0, 0), (2, 1, 1), (1, 1, 2), (1, 0, 2), 1, 7,
    (3, 1, 0), (3, 0, 1), (3, 0, 0), (3, 1, 1), 0, (2, 1, 2), (2, 0, 2), None,
    (3, 1, 2), (3, 0, 2),
)
X_STEPS = (
    2, (0, 0, 0), (0, 1, 1), 1, 3,
    (1, 1, 0), (1, 0, 1), (0, 0, 2), (1, 0, 0), (1, 1, 1), 0, None,
    (1, 1, 2), (1, 0, 2),
)


def ring_sum(steps, length, y, raw, ready, ways, other_y, use, sendb, recvb,
             ysendb, yrecvb, ss, rs, yss, yrs):
    trades, sends, traded = {}, {}, set()
    last, end = length - 1, 2 * length

    def exchange(value, k):
        encode(value, ysendb.at[k])
        trades[k] = remote(ysendb.at[k], yrecvb.at[k], yss.at[k], yrs.at[k], other_y)
        trades[k].start()

    def term(d, lane):
        if lane < 2:
            return raw(d, lane, 0)
        if d not in traded:
            trades[d].wait_recv()
            traded.add(d)
        return raw(d, y, 1) + decode(yrecvb.at[d])

    def arrived(h):
        value = raw(0, h, 0)
        for way in range(2):
            first, second = sends[last, way, 0][0], sends[last, way, 1][0]
            value = value + decode(recvb.at[first + h * (second - first)])
        return value

    for step in steps:
        if step is None:
            for lane in (0, 1):
                for way in range(2):
                    sends[last, way, lane][1].wait_recv()
            exchange(arrived(1 - y), end)
        elif isinstance(step, int):
            ready(step)
            exchange(raw(step, 1 - y, 1), step)
        else:
            s, way, lane = step
            value = term(length - s if way == 0 else length + s, lane)
            if (s - 1, way, lane) in sends:
                index, before = sends[s - 1, way, lane]
                before.wait_recv()
                value = value + decode(recvb.at[index])
            n = len(sends)
            encode(value, sendb.at[n])
            copy = remote(sendb.at[n], recvb.at[n], ss.at[n], rs.at[n], ways[way])
            copy.start()
            sends[step] = (n, copy)

    first = arrived(y)
    trades[end].wait_recv()
    use(0, first + decode(yrecvb.at[end]))
    second = term(0, 2)
    for way in range(2):
        index, copy = sends[last, way, 2]
        copy.wait_recv()
        second = second + decode(recvb.at[index])
    use(1, second)

    def drain():
        for _, copy in sends.values():
            copy.wait_send()
        for copy in trades.values():
            copy.wait_send()

    return drain


def ring_scratch(steps, length):
    n, y = sum(isinstance(step, tuple) for step in steps), 2 * length + 1
    return [
        pltpu.VMEM((n, CODE, T), I16), pltpu.VMEM((n, CODE, T), I16),
        pltpu.VMEM((y, CODE, T), I16), pltpu.VMEM((y, CODE, T), I16),
        DMA((n,)), DMA((n,)), DMA((y,)), DMA((y,)),
    ]


def word_panel_kernel(partial, share, everyone, sib, mine, xss, xrs, gss, grs, hss, hrs, pss, prs, ms,
                      *ring):
    z, yh, c = lax.axis_index("z"), lax.axis_index("yh"), lax.axis_index("core")
    ways = ({"z": lax.rem(z + 1, NZ)}, {"z": lax.rem(z + NZ - 1, NZ)})
    other_y, other_core = {"yh": 1 - yh}, {"core": 1 - c}
    length = NZ // 2

    greet([*ways, other_y, other_core])
    swaps = {}
    for dz in (4, 3, 5, 2, 6, 1, 7, 0):
        for h in range(2):
            slot, zz = dz * 2 + h, lax.rem(z + dz, NZ)
            swaps[dz, h] = remote(partial.at[zz, h, 1 - c], sib.at[slot], xss.at[slot], xrs.at[slot], other_core)
            swaps[dz, h].start()

    def ready(d):
        for h in range(2):
            swaps[d, h].wait_recv()

    def raw(d, h, part):
        rows = pl.ds(part * HALF, HALF)
        return partial[lax.rem(z + d, NZ), h, c, rows, :] + sib[d * 2 + h, rows, :]

    pair = (pl.ds(0, 2), pl.ds(2, 2))

    def place(d, h, part):
        return everyone.at[lax.rem(z + d, NZ), h, c, pair[part]]

    gives, hands, passes, keeps = {}, [], {}, []

    def hand(src, dst, k):
        copy = remote(src, dst, hss.at[k], hrs.at[k], other_core)
        copy.start()
        hands.append(copy)

    def along_y(src, dst, k):
        passes[k] = remote(src, dst, pss.at[k], prs.at[k], other_y)
        passes[k].start()

    def lane_place(d, lane):
        return place(d, 1 - yh if lane == 1 else yh, 1 if lane == 2 else 0)

    def give(s, way, lane, src=None):
        dst = lane_place((NZ - s) % NZ if way == 0 else s, lane)
        k = (s * 2 + way) * 3 + lane
        gives[s, way, lane] = remote(dst if src is None else src, dst, gss.at[k], grs.at[k], ways[way])
        gives[s, way, lane].start()

    own = (mine.at[pair[0]], mine.at[pair[1]])

    def use(part, total):
        for t in range(2):
            mine[part * 2 + t] = total[t * T : (t + 1) * T].T.astype(BF16)
        along_y(own[part], place(0, yh, part), 0 if part else NZ)
        for way in range(2):
            give(0, way, 2 if part else 0, own[part])
        hand(own[part], place(0, yh, part), 2 * NZ if part else 0)
        keeps.append(pltpu.make_async_copy(own[part], place(0, yh, part), ms.at[part]))
        keeps[-1].start()
        share[pl.ds(part * HALF, HALF), :] = total

    drain = ring_sum(Z_STEPS, length, yh, raw, ready, ways, other_y, use, *ring)
    passes[NZ].wait_recv()
    for way in range(2):
        give(0, way, 1)
    hand(lane_place(0, 1), lane_place(0, 1), 1)
    due = [0]
    for s in range(1, length + 1):
        came = []
        for lane in (0, 2, 1) if s == 1 else (2, 0, 1):
            for way in range(2):
                if (s - 1, way, lane) not in gives:
                    continue
                gives[s - 1, way, lane].wait_recv()
                if s < length - 1 or (s == length - 1 and way == AWAY[lane]):
                    give(s, way, lane)
                d = (NZ - s) % NZ if way == 0 else s
                at = lane_place(d, lane)
                if lane == 2:
                    along_y(at, at, d)
                    came.append(d)
                hand(at, at, 2 * NZ + d if lane == 2 else d * 2 + lane)
        for d in due:
            passes[d].wait_recv()
            hand(place(d, 1 - yh, 1), place(d, 1 - yh, 1), 3 * NZ + d)
        due = came
    for d in due:
        passes[d].wait_recv()
        hand(place(d, 1 - yh, 1), place(d, 1 - yh, 1), 3 * NZ + d)

    for copy in hands:
        copy.wait()
    for copy in list(gives.values()) + list(passes.values()) + list(swaps.values()):
        copy.wait_send()
    drain()
    for copy in keeps:
        copy.wait()


def word_panel_sum(partial):
    return pl.pallas_call(
        word_panel_kernel,
        in_specs=[VMEM],
        out_specs=[VMEM, ANY],
        out_shape=[
            jax.ShapeDtypeStruct((SHARE, T), F32),
            jax.ShapeDtypeStruct((NZ, NYH, NC, 4, T, T), BF16),
        ],
        scratch_shapes=[
            pltpu.VMEM((2 * NZ, SHARE, T), F32),
            pltpu.VMEM((4, T, T), BF16),
            DMA((2 * NZ,)), DMA((2 * NZ,)), DMA((3 * NZ,)), DMA((3 * NZ,)),
            DMA((4 * NZ,)), DMA((4 * NZ,)), DMA((NZ + 1,)), DMA((NZ + 1,)), DMA((2,)),
            *ring_scratch(Z_STEPS, NZ // 2),
        ],
        compiler_params=pltpu.CompilerParams(collective_id=1, has_side_effects=True, vmem_limit_bytes=16 << 20),
        name="word_panel_sum",
    )(partial)


def context_kernel(rows, cols, tiles, rounded, share, partial, share_out, odd):
    share_out[...] = share[...]
    sums = (partial, odd)
    for ref in sums:
        ref[...] = jnp.zeros_like(ref)

    def some(b, carry):
        for g in range(GROUP):
            slot = b * GROUP + g
            sums[g % 2][cols[slot]] += jnp.dot(rounded[rows[slot]], tiles[slot], preferred_element_type=F32)
        return carry

    lax.fori_loop(0, tiles.shape[0] // GROUP, some, 0)
    partial[...] += odd[...]


def context_products(rows, cols, tiles, rounded, share):
    slots = tiles.shape[0]
    return pl.pallas_call(
        context_kernel,
        in_specs=[SMEM, SMEM, VMEM, VMEM, VMEM],
        out_specs=[VMEM, VMEM],
        out_shape=[
            jax.ShapeDtypeStruct((COL_TILES, T, T), F32),
            jax.ShapeDtypeStruct((SHARE, T), F32),
        ],
        scratch_shapes=[pltpu.VMEM((COL_TILES, T, T), F32)],
        compiler_params=pltpu.CompilerParams(vmem_limit_bytes=16 << 20),
        name="context_products",
    )(rows, cols, tiles, rounded, share)


def context_panel_kernel(partial, share, *ring):
    x, yl = lax.axis_index("x"), lax.axis_index("yl")
    ways = ({"x": lax.rem(x + 1, NX)}, {"x": lax.rem(x + NX - 1, NX)})
    other_y = {"yl": 1 - yl}
    greet([*ways, other_y])

    def raw(d, h, part):
        return partial[h, lax.rem(x + d, NX), pl.ds(part * HALF, HALF), :]

    def use(part, total):
        total = total * (1.0 / T)
        for t in range(2):
            share[pl.ds(part * HALF + t * T, T), :] = total[t * T : (t + 1) * T].T

    ring_sum(X_STEPS, NX // 2, yl, raw, lambda d: None, ways, other_y, use, *ring)()


def context_panel_sum(partial):
    return pl.pallas_call(
        context_panel_kernel,
        in_specs=[VMEM],
        out_specs=VMEM,
        out_shape=jax.ShapeDtypeStruct((SHARE, T), F32),
        scratch_shapes=ring_scratch(X_STEPS, NX // 2),
        compiler_params=pltpu.CompilerParams(collective_id=2, has_side_effects=True, vmem_limit_bytes=8 << 20),
        name="context_panel_sum",
    )(partial)


def shards(tile_counts, tile_rows, tile_cols, panel):
    counts, rows, cols = tile_counts[0, 0], tile_rows[0, 0], tile_cols[0, 0]
    far = [pltpu.with_memory_space_constraint(a, pltpu.HBM) for a in (rows, cols, counts, panel)]
    words_all, band, base = totals(*far)
    band = band.reshape(COL_TILES, T, T)
    tiles, partial = word_products(rows, cols, base, words_all, band)
    share, everyone = word_panel_sum(partial.reshape(NZ, NYH, NC, SHARE, T))
    rounded = everyone.reshape(ROW_TILES, T, T)
    context_partial, share = context_products(rows, cols, tiles, rounded, share)
    context_share = context_panel_sum(context_partial.reshape(NYL, NX, SHARE, T))
    return share, context_share


def solution(mesh):
    split = Mesh(
        mesh.devices.reshape(NYL, NX, NZ, NYH, NC), ("yl", "x", "z", "yh", "core")
    )
    row, col = ("yl", "x"), ("z", "yh", "core")
    in_specs = (
        P(row, col, None, None, None),
        P(row, col, None),
        P(row, col, None),
        P(col + row, None),
    )
    out_specs = (P(row + col, None), P(col + row, None))
    return jax.shard_map(shards, mesh=split, in_specs=in_specs, out_specs=out_specs, check_vma=False)
```

```python
import functools
import math

import jax
import jax.numpy as jnp
from jax import lax
from jax.experimental import pallas as pl
from jax.experimental.pallas import tpu as pltpu
from jax.sharding import Mesh
from jax.sharding import PartitionSpec as P

NEG_SAMPLES = 15
T = 128
NX, NYL, NYH, NZ, NC = 4, 2, 2, 8, 2
N_ROW, N_COL = NX * NYL, NZ * NYH * NC
ROW_TILES, COL_TILES = 128, 32
SHARE = 512
HALF = SHARE // 2
CODE = HALF + 16
MESH = pl.DeviceIdType.MESH
F32, BF16, I32, I16 = jnp.float32, jnp.bfloat16, jnp.int32, jnp.int16
ANY = pl.BlockSpec(memory_space=pl.ANY)
VMEM = pl.BlockSpec(memory_space=pltpu.VMEM)
SMEM = pl.BlockSpec(memory_space=pltpu.SMEM)
DMA = pltpu.SemaphoreType.DMA
LN2 = math.log(2.0)


def remote(src, dst, ssem, rsem, device):
    return pltpu.make_async_remote_copy(
        src_ref=src, dst_ref=dst, send_sem=ssem, recv_sem=rsem,
        device_id=device, device_id_type=MESH,
    )


def hail(devices):
    for device in devices:
        pl.semaphore_signal(
            pltpu.get_barrier_semaphore(), inc=1, device_id=device, device_id_type=MESH
        )


def await_hails(devices):
    pl.semaphore_wait(pltpu.get_barrier_semaphore(), len(devices))


def greet(devices):
    hail(devices)
    await_hails(devices)


def encode(value, ref):
    top = jnp.max(jnp.abs(value), axis=0, keepdims=True)
    expo = jnp.ceil(jnp.log(jnp.maximum(top, 1e-30)) * (1.0 / LN2) + 0.001) - 14.0
    scaled = jnp.round(value * jnp.exp(expo * -LN2))
    ref[pl.ds(0, HALF), :] = scaled.astype(I32).astype(I16)
    ref[pl.ds(HALF, 16), :] = jnp.broadcast_to(expo, (16, T)).astype(I32).astype(I16)


def decode(ref):
    expo = ref[pl.ds(HALF, 16), :].astype(I32).astype(F32)[0:1]
    return ref[pl.ds(0, HALF), :].astype(I32).astype(F32) * jnp.exp(expo * LN2)


GROUP = 16
PART = T // NZ


def powers_of(totals):
    root = jnp.sqrt(totals)
    return root * jnp.sqrt(root)


def load_counts(counts, held, sem):
    copies = []
    for b in range(counts.shape[0] // GROUP):
        part = pl.ds(b * GROUP, GROUP)
        copies.append(pltpu.make_async_copy(counts.at[part], held.at[part], sem.at[b]))
        copies[-1].start()
    return copies


def await_counts(counts, held, sem, b):
    part = pl.ds(b * GROUP, GROUP)
    pltpu.make_async_copy(counts.at[part], held.at[part], sem.at[b]).wait()


def totals_kernel(rows_in, cols_in, counts, panel_in, words_all, band, base, cleared,
                  brought, panel, held, rows, cols, wacc, contexts, context_log, wrecv, crecv, mine, qrecv,
                  cs, wss, wrs, css, crs, qss, qrs, ass, ars, pss, prs, lsem):
    x, yl = lax.axis_index("x"), lax.axis_index("yl")
    z, yh, c = lax.axis_index("z"), lax.axis_index("yh"), lax.axis_index("core")
    blocks = counts.shape[0] // GROUP
    row = yl * NX + x
    right, left = lax.rem(x + 1, NX), lax.rem(x + NX - 1, NX)
    row_peers = [
        (dx * NYL + dy, {"x": lax.rem(x + dx, NX), "yl": lax.rem(yl + dy, NYL)})
        for dx in range(NX) for dy in range(NYL) if dx or dy
    ]
    z_peers = [(dz, lax.rem(z + dz, NZ)) for dz in (4, 3, 5, 2, 6, 1, 7)]
    quad = [
        (dy * NC + dc, {"yh": lax.rem(yh + dy, NYH), "core": lax.rem(c + dc, NC)})
        for dy, dc in ((1, 0), (1, 1), (0, 1))
    ]
    everybody = [d for _, d in row_peers] + [{"z": p} for _, p in z_peers] + [d for _, d in quad]
    slots = [
        pltpu.make_async_copy(rows_in, rows, lsem.at[1]),
        pltpu.make_async_copy(cols_in, cols, lsem.at[2]),
    ]
    bring = pltpu.make_async_copy(panel_in, brought, lsem.at[3])
    for copy in slots:
        copy.start()
    load_counts(counts, held, cs)
    bring.start()
    hail(everybody)
    bring.wait()
    for t in range(4):
        tile = pl.ds(t * T, T)
        panel[tile, :] = brought[tile, :].astype(F32).T.astype(BF16)
    own = pltpu.make_async_copy(panel, band.at[row], lsem.at[0])
    own.start()

    wacc[...] = jnp.zeros_like(wacc)
    lanes = lax.broadcasted_iota(I32, (T, T), 1)
    bands = lax.broadcasted_iota(I32, (COL_TILES, T), 0)
    for copy in slots:
        copy.wait()

    def some(b, per_context):
        await_counts(counts, held, cs, b)
        per_word = wacc[...]
        for g in range(GROUP):
            slot = b * GROUP + g
            value = held[slot]
            per_context = per_context + jnp.where(
                bands == cols[slot], jnp.sum(value, axis=0, keepdims=True), 0
            )
            sums = jnp.sum(value.astype(F32), axis=1, keepdims=True)
            per_word = per_word + jnp.where(lanes == rows[slot], sums, 0.0)
        wacc[...] = per_word
        return per_context

    per_context = lax.fori_loop(0, blocks, some, jnp.zeros((COL_TILES, T), I32))
    contexts[...] = per_context.astype(F32)
    await_hails(everybody)

    csends = [remote(contexts, crecv.at[k], css.at[k], crs.at[k], d) for k, d in row_peers]
    for copy in csends:
        copy.start()
    wsends = [
        remote(wacc.at[pl.ds(pl.multiple_of(p * PART, PART), PART)], wrecv.at[k], wss.at[k], wrs.at[k], {"z": p})
        for k, p in z_peers
    ]
    for copy in wsends:
        copy.start()

    psends = []

    def pass_on(src, dst, device):
        k = len(psends)
        psends.append(remote(src, dst, pss.at[k], prs.at[k], device))
        psends[k].start()

    def to_right_and_left(first, second):
        pass_on(first, first, {"x": right})
        pass_on(second, second, {"x": left})

    def relay(y):
        to_right_and_left(
            band.at[y * NX + left, pl.ds(0, HALF)], band.at[y * NX + right, pl.ds(HALF, HALF)]
        )

    pass_on(panel, band.at[row], {"yl": 1 - yl})
    pass_on(panel, band.at[row], {"x": right})
    pass_on(panel, band.at[row], {"x": left})

    def clear(t, carry):
        cleared[t] = jnp.zeros((T, T), F32)
        return carry

    lax.fori_loop(0, ROW_TILES, clear, 0, unroll=4)
    for copy in csends:
        copy.wait_recv()
    contexts_sum = contexts[...]
    for k, _ in row_peers:
        contexts_sum = contexts_sum + crecv[k]
    powers = powers_of(contexts_sum)
    band_power = jnp.sum(powers, keepdims=True)
    context_log[...] = jnp.log(jnp.maximum(powers, 1.0))

    for copy in psends[0:3]:
        copy.wait_recv()
    there = band.at[(1 - yl) * NX + x]
    to_right_and_left(there, there)
    relay(yl)

    for copy in wsends:
        copy.wait_recv()
    words_sum = wacc[pl.ds(pl.multiple_of(z * PART, PART), PART), :]
    for k, _ in z_peers:
        words_sum = words_sum + wrecv[k]
    mine[pl.ds(0, PART), :] = words_sum
    mine[pl.ds(PART, 8), :] = jnp.broadcast_to(band_power, (8, T))
    qsends = [remote(mine, qrecv.at[k], qss.at[k], qrs.at[k], d) for k, d in quad]
    for copy in qsends:
        copy.start()

    def logs(b, carry):
        for g in range(GROUP):
            slot = b * GROUP + g
            value = held[slot].astype(F32)
            term = jnp.where(
                value > 0.0, jnp.log(value) - context_log[pl.ds(cols[slot], 1), :], -1e30
            )
            base[slot] = term.T
        return carry

    lax.fori_loop(0, blocks // 2, logs, 0)
    for copy in qsends:
        copy.wait_recv()
    total = mine[...]
    for k, _ in quad:
        total = total + qrecv[k]
    words_all[z] = total
    asends = [
        remote(words_all.at[z], words_all.at[z], ass.at[k], ars.at[k], {"z": p}) for k, p in z_peers
    ]
    for copy in asends:
        copy.start()

    lax.fori_loop(blocks // 2, blocks, logs, 0)
    for copy in psends[3:5]:
        copy.wait_recv()
    relay(1 - yl)

    for copy in asends:
        copy.wait()
    for copy in csends + wsends + qsends + psends[0:5]:
        copy.wait_send()
    for copy in psends[5:9]:
        copy.wait()
    own.wait()


def totals(rows, cols, counts, panel):
    slots = counts.shape[0]
    return pl.pallas_call(
        totals_kernel,
        in_specs=[ANY, ANY, ANY, ANY],
        out_specs=[VMEM, ANY, VMEM, VMEM],
        out_shape=[
            jax.ShapeDtypeStruct((NZ, PART + 8, T), F32),
            jax.ShapeDtypeStruct((N_ROW, SHARE, T), BF16),
            jax.ShapeDtypeStruct((slots, T, T), F32),
            jax.ShapeDtypeStruct((ROW_TILES, T, T), F32),
        ],
        scratch_shapes=[
            pltpu.VMEM((SHARE, T), BF16),
            pltpu.VMEM((SHARE, T), BF16),
            pltpu.VMEM((slots, T, T), I32),
            pltpu.SMEM((slots,), I32),
            pltpu.SMEM((slots,), I32),
            pltpu.VMEM((T, ROW_TILES), F32),
            pltpu.VMEM((COL_TILES, T), F32),
            pltpu.VMEM((COL_TILES, T), F32),
            pltpu.VMEM((NZ, PART, T), F32),
            pltpu.VMEM((N_ROW, COL_TILES, T), F32),
            pltpu.VMEM((PART + 8, T), F32),
            pltpu.VMEM((NYH * NC, PART + 8, T), F32),
            DMA((slots // GROUP,)),
            DMA((NZ,)), DMA((NZ,)), DMA((N_ROW,)), DMA((N_ROW,)), DMA((NYH * NC,)), DMA((NYH * NC,)),
            DMA((NZ,)), DMA((NZ,)), DMA((9,)), DMA((9,)), DMA((4,)),
        ],
        compiler_params=pltpu.CompilerParams(collective_id=0, has_side_effects=True, vmem_limit_bytes=16 << 20),
        name="totals",
    )(rows, cols, counts, panel)


def word_kernel(rows, cols, base, words_all, band, cleared, tiles, partial, words, word_term):
    power = jnp.zeros((1, T), F32)
    for d in range(NZ):
        words[pl.ds(d * PART, PART), :] = words_all[d, 0:PART, :]
        power = power + words_all[d, PART : PART + 1, :]
    log_scale = jnp.log(power) - math.log(NEG_SAMPLES)
    word_term[...] = (log_scale - jnp.log(jnp.maximum(words[...], 1.0))).T

    def some(b, carry):
        for g in range(GROUP):
            slot = b * GROUP + g
            row, col = rows[slot], cols[slot]
            tile = jnp.maximum(base[slot] + word_term[pl.ds(row, 1), :], 0.0).astype(BF16)
            tiles[slot] = tile
            partial[row] += jnp.dot(band[col], tile, preferred_element_type=F32)
        return carry

    lax.fori_loop(0, base.shape[0] // GROUP, some, 0)


def word_products(rows, cols, base, words_all, band, cleared):
    slots = base.shape[0]
    return pl.pallas_call(
        word_kernel,
        in_specs=[SMEM, SMEM, VMEM, VMEM, VMEM, VMEM],
        out_specs=[VMEM, VMEM],
        scratch_shapes=[pltpu.VMEM((T, ROW_TILES), F32), pltpu.VMEM((ROW_TILES, T), F32)],
        out_shape=[
            jax.ShapeDtypeStruct((slots, T, T), BF16),
            jax.ShapeDtypeStruct((ROW_TILES, T, T), F32),
        ],
        input_output_aliases={5: 1},
        compiler_params=pltpu.CompilerParams(vmem_limit_bytes=28 << 20),
        name="word_products",
    )(rows, cols, base, words_all, band, cleared)


AWAY = (0, 1, 0)

Z_STEPS = (
    (0, 0, 0), (0, 1, 1), 4, 3, 5,
    (1, 1, 0), (1, 0, 1), (1, 0, 0), (1, 1, 1), (0, 0, 2), 2, 6,
    (2, 1, 0), (2, 0, 1), (2, 0, 0), (2, 1, 1), (1, 1, 2), (1, 0, 2), 1, 7,
    (3, 1, 0), (3, 0, 1), (3, 0, 0), (3, 1, 1), 0, (2, 1, 2), (2, 0, 2), None,
    (3, 1, 2), (3, 0, 2),
)
X_STEPS = (
    2, (0, 0, 0), (0, 1, 1), 1, 3,
    (1, 1, 0), (1, 0, 1), (0, 0, 2), (1, 0, 0), (1, 1, 1), 0, None,
    (1, 1, 2), (1, 0, 2),
)


def ring_sum(steps, length, y, raw, ready, ways, other_y, use, sendb, recvb,
             ysendb, yrecvb, ss, rs, yss, yrs):
    trades, sends, traded = {}, {}, set()
    last, end = length - 1, 2 * length

    def exchange(value, k):
        encode(value, ysendb.at[k])
        trades[k] = remote(ysendb.at[k], yrecvb.at[k], yss.at[k], yrs.at[k], other_y)
        trades[k].start()

    def term(d, lane):
        ready(d, lane // 2)
        if lane < 2:
            return raw(d, lane, 0)
        if d not in traded:
            trades[d].wait_recv()
            traded.add(d)
        return raw(d, y, 1) + decode(yrecvb.at[d])

    def arrived(h):
        value = raw(0, h, 0)
        for way in range(2):
            first, second = sends[last, way, 0][0], sends[last, way, 1][0]
            value = value + decode(recvb.at[first + h * (second - first)])
        return value

    for step in steps:
        if step is None:
            for lane in (0, 1):
                for way in range(2):
                    sends[last, way, lane][1].wait_recv()
            ready(0, 0)
            exchange(arrived(1 - y), end)
        elif isinstance(step, int):
            ready(step, 1)
            exchange(raw(step, 1 - y, 1), step)
        else:
            s, way, lane = step
            value = term(length - s if way == 0 else length + s, lane)
            if (s - 1, way, lane) in sends:
                index, before = sends[s - 1, way, lane]
                before.wait_recv()
                value = value + decode(recvb.at[index])
            n = len(sends)
            encode(value, sendb.at[n])
            copy = remote(sendb.at[n], recvb.at[n], ss.at[n], rs.at[n], ways[way])
            copy.start()
            sends[step] = (n, copy)

    first = arrived(y)
    trades[end].wait_recv()
    use(0, first + decode(yrecvb.at[end]))
    second = term(0, 2)
    for way in range(2):
        index, copy = sends[last, way, 2]
        copy.wait_recv()
        second = second + decode(recvb.at[index])
    use(1, second)

    def drain():
        for _, copy in sends.values():
            copy.wait_send()
        for copy in trades.values():
            copy.wait_send()

    return drain


def ring_scratch(steps, length):
    n, y = sum(isinstance(step, tuple) for step in steps), 2 * length + 1
    return [
        pltpu.VMEM((n, CODE, T), I16), pltpu.VMEM((n, CODE, T), I16),
        pltpu.VMEM((y, CODE, T), I16), pltpu.VMEM((y, CODE, T), I16),
        DMA((n,)), DMA((n,)), DMA((y,)), DMA((y,)),
    ]


def word_panel_kernel(partial, share, everyone, sib, mine, xss, xrs, gss, grs, hss, hrs, pss, prs, ms,
                      *ring):
    z, yh, c = lax.axis_index("z"), lax.axis_index("yh"), lax.axis_index("core")
    ways = ({"z": lax.rem(z + 1, NZ)}, {"z": lax.rem(z + NZ - 1, NZ)})
    other_y, other_core = {"yh": 1 - yh}, {"core": 1 - c}
    length = NZ // 2

    greet([*ways, other_y, other_core])
    swaps, here = {}, set()
    for dz in (4, 3, 5, 2, 6, 1, 7, 0):
        for part in range(2):
            for h in range(2):
                k, rows = (dz * 2 + h) * 2 + part, pl.ds(part * HALF, HALF)
                swaps[dz, h, part] = remote(
                    partial.at[lax.rem(z + dz, NZ), h, 1 - c, rows], sib.at[dz * 2 + h, rows],
                    xss.at[k], xrs.at[k], other_core,
                )
                swaps[dz, h, part].start()

    def ready(d, part):
        if (d, part) not in here:
            here.add((d, part))
            for h in range(2):
                swaps[d, h, part].wait_recv()

    def raw(d, h, part):
        rows = pl.ds(part * HALF, HALF)
        return partial[lax.rem(z + d, NZ), h, c, rows, :] + sib[d * 2 + h, rows, :]

    pair = (pl.ds(0, 2), pl.ds(2, 2))

    def place(d, h, part):
        return everyone.at[lax.rem(z + d, NZ), h, c, pair[part]]

    gives, hands, passes, keeps = {}, [], {}, []

    def hand(src, dst, k):
        copy = remote(src, dst, hss.at[k], hrs.at[k], other_core)
        copy.start()
        hands.append(copy)

    def along_y(src, dst, k):
        passes[k] = remote(src, dst, pss.at[k], prs.at[k], other_y)
        passes[k].start()

    def lane_place(d, lane):
        return place(d, 1 - yh if lane == 1 else yh, 1 if lane == 2 else 0)

    def give(s, way, lane, src=None):
        dst = lane_place((NZ - s) % NZ if way == 0 else s, lane)
        k = (s * 2 + way) * 3 + lane
        gives[s, way, lane] = remote(dst if src is None else src, dst, gss.at[k], grs.at[k], ways[way])
        gives[s, way, lane].start()

    own = (mine.at[pair[0]], mine.at[pair[1]])

    def use(part, total):
        straight = [total[t * T : (t + 1) * T].T for t in range(2)]
        for t in range(2):
            mine[part * 2 + t] = straight[t].astype(BF16)
        along_y(own[part], place(0, yh, part), 0 if part else NZ)
        for way in range(2):
            give(0, way, 2 if part else 0, own[part])
        hand(own[part], place(0, yh, part), 2 * NZ if part else 0)
        keeps.append(pltpu.make_async_copy(own[part], place(0, yh, part), ms.at[part]))
        keeps[-1].start()
        for t in range(2):
            share[pl.ds(part * HALF + t * T, T), :] = straight[t]

    drain = ring_sum(Z_STEPS, length, yh, raw, ready, ways, other_y, use, *ring)
    passes[NZ].wait_recv()
    for way in range(2):
        give(0, way, 1)
    hand(lane_place(0, 1), lane_place(0, 1), 1)
    due = [0]
    for s in range(1, length + 1):
        came = []
        for lane in (0, 2, 1) if s == 1 else (2, 0, 1):
            for way in range(2):
                if (s - 1, way, lane) not in gives:
                    continue
                gives[s - 1, way, lane].wait_recv()
                if s < length - 1 or (s == length - 1 and way == AWAY[lane]):
                    give(s, way, lane)
                d = (NZ - s) % NZ if way == 0 else s
                at = lane_place(d, lane)
                if lane == 2:
                    along_y(at, at, d)
                    came.append(d)
                hand(at, at, 2 * NZ + d if lane == 2 else d * 2 + lane)
        for d in due:
            passes[d].wait_recv()
            hand(place(d, 1 - yh, 1), place(d, 1 - yh, 1), 3 * NZ + d)
        due = came
    for d in due:
        passes[d].wait_recv()
        hand(place(d, 1 - yh, 1), place(d, 1 - yh, 1), 3 * NZ + d)

    for copy in hands:
        copy.wait()
    for copy in list(gives.values()) + list(passes.values()) + list(swaps.values()):
        copy.wait_send()
    drain()
    for copy in keeps:
        copy.wait()


def word_panel_sum(partial):
    return pl.pallas_call(
        word_panel_kernel,
        in_specs=[VMEM],
        out_specs=[VMEM, ANY],
        out_shape=[
            jax.ShapeDtypeStruct((SHARE, T), F32),
            jax.ShapeDtypeStruct((NZ, NYH, NC, 4, T, T), BF16),
        ],
        scratch_shapes=[
            pltpu.VMEM((2 * NZ, SHARE, T), F32),
            pltpu.VMEM((4, T, T), BF16),
            DMA((4 * NZ,)), DMA((4 * NZ,)), DMA((3 * NZ,)), DMA((3 * NZ,)),
            DMA((4 * NZ,)), DMA((4 * NZ,)), DMA((NZ + 1,)), DMA((NZ + 1,)), DMA((2,)),
            *ring_scratch(Z_STEPS, NZ // 2),
        ],
        compiler_params=pltpu.CompilerParams(collective_id=1, has_side_effects=True, vmem_limit_bytes=16 << 20),
        name="word_panel_sum",
    )(partial)


def context_kernel(rows, cols, tiles, rounded, share, partial, share_out):
    share_out[...] = share[...]
    partial[...] = jnp.zeros_like(partial)

    def some(b, carry):
        for g in range(GROUP):
            slot = b * GROUP + g
            partial[cols[slot]] += jnp.dot(tiles[slot], rounded[rows[slot]], preferred_element_type=F32)
        return carry

    lax.fori_loop(0, tiles.shape[0] // GROUP, some, 0)


def context_products(rows, cols, tiles, rounded, share):
    slots = tiles.shape[0]
    return pl.pallas_call(
        context_kernel,
        in_specs=[SMEM, SMEM, VMEM, VMEM, VMEM],
        out_specs=[VMEM, VMEM],
        out_shape=[
            jax.ShapeDtypeStruct((COL_TILES, T, T), F32),
            jax.ShapeDtypeStruct((SHARE, T), F32),
        ],
        compiler_params=pltpu.CompilerParams(vmem_limit_bytes=16 << 20),
        name="context_products",
    )(rows, cols, tiles, rounded, share)


def context_panel_kernel(partial, share, *ring):
    x, yl = lax.axis_index("x"), lax.axis_index("yl")
    ways = ({"x": lax.rem(x + 1, NX)}, {"x": lax.rem(x + NX - 1, NX)})
    other_y = {"yl": 1 - yl}
    greet([*ways, other_y])

    def raw(d, h, part):
        return partial[h, lax.rem(x + d, NX), pl.ds(part * HALF, HALF), :]

    def use(part, total):
        share[pl.ds(part * HALF, HALF), :] = total * (1.0 / T)

    ring_sum(X_STEPS, NX // 2, yl, raw, lambda d, part: None, ways, other_y, use, *ring)()


def context_panel_sum(partial):
    return pl.pallas_call(
        context_panel_kernel,
        in_specs=[VMEM],
        out_specs=VMEM,
        out_shape=jax.ShapeDtypeStruct((SHARE, T), F32),
        scratch_shapes=ring_scratch(X_STEPS, NX // 2),
        compiler_params=pltpu.CompilerParams(collective_id=2, has_side_effects=True, vmem_limit_bytes=8 << 20),
        name="context_panel_sum",
    )(partial)


def shards(tile_counts, tile_rows, tile_cols, panel):
    counts, rows, cols = tile_counts[0, 0], tile_rows[0, 0], tile_cols[0, 0]
    far = [pltpu.with_memory_space_constraint(a, pltpu.HBM) for a in (rows, cols, counts, panel)]
    words_all, band, base, cleared = totals(*far)
    band = band.reshape(COL_TILES, T, T)
    tiles, partial = word_products(rows, cols, base, words_all, band, cleared)
    share, everyone = word_panel_sum(partial.reshape(NZ, NYH, NC, SHARE, T))
    rounded = everyone.reshape(ROW_TILES, T, T)
    context_partial, share = context_products(rows, cols, tiles, rounded, share)
    context_share = context_panel_sum(context_partial.reshape(NYL, NX, SHARE, T))
    return share, context_share


def solution(mesh):
    split = Mesh(
        mesh.devices.reshape(NYL, NX, NZ, NYH, NC), ("yl", "x", "z", "yh", "core")
    )
    row, col = ("yl", "x"), ("z", "yh", "core")
    in_specs = (
        P(row, col, None, None, None),
        P(row, col, None),
        P(row, col, None),
        P(col + row, None),
    )
    out_specs = (P(row + col, None), P(col + row, None))
    return jax.shard_map(shards, mesh=split, in_specs=in_specs, out_specs=out_specs, check_vma=False)
```

```python
import functools
import math

import jax
import jax.numpy as jnp
from jax import lax
from jax.experimental import pallas as pl
from jax.experimental.pallas import tpu as pltpu
from jax.sharding import Mesh
from jax.sharding import PartitionSpec as P

NEG_SAMPLES = 15
T = 128
NX, NYL, NYH, NZ, NC = 4, 2, 2, 8, 2
N_ROW, N_COL = NX * NYL, NZ * NYH * NC
ROW_TILES, COL_TILES = 128, 32
SHARE = 512
HALF = SHARE // 2
CODE = HALF + 16
MESH = pl.DeviceIdType.MESH
F32, BF16, I32, I16 = jnp.float32, jnp.bfloat16, jnp.int32, jnp.int16
ANY = pl.BlockSpec(memory_space=pl.ANY)
VMEM = pl.BlockSpec(memory_space=pltpu.VMEM)
SMEM = pl.BlockSpec(memory_space=pltpu.SMEM)
DMA = pltpu.SemaphoreType.DMA
LN2 = math.log(2.0)


def remote(src, dst, ssem, rsem, device):
    return pltpu.make_async_remote_copy(
        src_ref=src, dst_ref=dst, send_sem=ssem, recv_sem=rsem,
        device_id=device, device_id_type=MESH,
    )


def hail(devices):
    for device in devices:
        pl.semaphore_signal(
            pltpu.get_barrier_semaphore(), inc=1, device_id=device, device_id_type=MESH
        )


def await_hails(devices):
    pl.semaphore_wait(pltpu.get_barrier_semaphore(), len(devices))


def greet(devices):
    hail(devices)
    await_hails(devices)


def encode(value, ref):
    top = jnp.max(jnp.abs(value), axis=0, keepdims=True)
    expo = jnp.ceil(jnp.log(jnp.maximum(top, 1e-30)) * (1.0 / LN2) + 0.001) - 14.0
    scaled = jnp.round(value * jnp.exp(expo * -LN2))
    ref[pl.ds(0, HALF), :] = scaled.astype(I32).astype(I16)
    ref[pl.ds(HALF, 16), :] = jnp.broadcast_to(expo, (16, T)).astype(I32).astype(I16)


def decode(ref):
    expo = ref[pl.ds(HALF, 16), :].astype(I32).astype(F32)[0:1]
    return ref[pl.ds(0, HALF), :].astype(I32).astype(F32) * jnp.exp(expo * LN2)


GROUP = 16
PART = T // NZ


def powers_of(totals):
    root = jnp.sqrt(totals)
    return root * jnp.sqrt(root)


def load_counts(counts, held, sem):
    copies = []
    for b in range(counts.shape[0] // GROUP):
        part = pl.ds(b * GROUP, GROUP)
        copies.append(pltpu.make_async_copy(counts.at[part], held.at[part], sem.at[b]))
        copies[-1].start()
    return copies


def await_counts(counts, held, sem, b):
    part = pl.ds(b * GROUP, GROUP)
    pltpu.make_async_copy(counts.at[part], held.at[part], sem.at[b]).wait()


def totals_kernel(rows_in, cols_in, counts, panel_in, words_all, band, base, cleared,
                  brought, panel, held, rows, cols, wacc, contexts, context_log, wrecv, crecv, mine, qrecv,
                  cs, wss, wrs, css, crs, qss, qrs, ass, ars, pss, prs, lsem):
    x, yl = lax.axis_index("x"), lax.axis_index("yl")
    z, yh, c = lax.axis_index("z"), lax.axis_index("yh"), lax.axis_index("core")
    blocks = counts.shape[0] // GROUP
    row = yl * NX + x
    right, left = lax.rem(x + 1, NX), lax.rem(x + NX - 1, NX)
    row_peers = [
        (dx * NYL + dy, {"x": lax.rem(x + dx, NX), "yl": lax.rem(yl + dy, NYL)})
        for dx in range(NX) for dy in range(NYL) if dx or dy
    ]
    z_peers = [(dz, lax.rem(z + dz, NZ)) for dz in (4, 3, 5, 2, 6, 1, 7)]
    quad = [
        (dy * NC + dc, {"yh": lax.rem(yh + dy, NYH), "core": lax.rem(c + dc, NC)})
        for dy, dc in ((1, 0), (1, 1), (0, 1))
    ]
    everybody = [d for _, d in row_peers] + [{"z": p} for _, p in z_peers] + [d for _, d in quad]
    slots = [
        pltpu.make_async_copy(rows_in, rows, lsem.at[1]),
        pltpu.make_async_copy(cols_in, cols, lsem.at[2]),
    ]
    bring = pltpu.make_async_copy(panel_in, brought, lsem.at[3])
    for copy in (bring, *slots):
        copy.start()
    load_counts(counts, held, cs)
    hail(everybody)
    bring.wait()
    for t in range(4):
        tile = pl.ds(t * T, T)
        panel[tile, :] = brought[tile, :].astype(F32).T.astype(BF16)
    own = pltpu.make_async_copy(panel, band.at[row], lsem.at[0])
    own.start()

    wacc[...] = jnp.zeros_like(wacc)
    lanes = lax.broadcasted_iota(I32, (T, T), 1)
    bands = lax.broadcasted_iota(I32, (COL_TILES, T), 0)
    for copy in slots:
        copy.wait()

    def some(b, per_context):
        await_counts(counts, held, cs, b)
        per_word = wacc[...]
        for g in range(GROUP):
            slot = b * GROUP + g
            value = held[slot]
            per_context = per_context + jnp.where(
                bands == cols[slot], jnp.sum(value, axis=0, keepdims=True), 0
            )
            sums = jnp.sum(value.astype(F32), axis=1, keepdims=True)
            per_word = per_word + jnp.where(lanes == rows[slot], sums, 0.0)
        wacc[...] = per_word
        return per_context

    per_context = lax.fori_loop(0, blocks, some, jnp.zeros((COL_TILES, T), I32))
    contexts[...] = per_context.astype(F32)
    await_hails(everybody)

    csends = [remote(contexts, crecv.at[k], css.at[k], crs.at[k], d) for k, d in row_peers]
    for copy in csends:
        copy.start()
    wsends = [
        remote(wacc.at[pl.ds(pl.multiple_of(p * PART, PART), PART)], wrecv.at[k], wss.at[k], wrs.at[k], {"z": p})
        for k, p in z_peers
    ]
    for copy in wsends:
        copy.start()

    psends = []

    def pass_on(src, dst, device):
        k = len(psends)
        psends.append(remote(src, dst, pss.at[k], prs.at[k], device))
        psends[k].start()

    def to_right_and_left(first, second):
        pass_on(first, first, {"x": right})
        pass_on(second, second, {"x": left})

    def relay(y):
        to_right_and_left(
            band.at[y * NX + left, pl.ds(0, HALF)], band.at[y * NX + right, pl.ds(HALF, HALF)]
        )

    pass_on(panel, band.at[row], {"yl": 1 - yl})
    pass_on(panel, band.at[row], {"x": right})
    pass_on(panel, band.at[row], {"x": left})

    def clear(t, carry):
        cleared[t] = jnp.zeros((T, T), F32)
        return carry

    lax.fori_loop(0, ROW_TILES, clear, 0, unroll=4)
    for copy in csends:
        copy.wait_recv()
    contexts_sum = contexts[...]
    for k, _ in row_peers:
        contexts_sum = contexts_sum + crecv[k]
    powers = powers_of(contexts_sum)
    band_power = jnp.sum(powers, keepdims=True)
    context_log[...] = jnp.log(jnp.maximum(powers, 1.0))

    for copy in psends[0:3]:
        copy.wait_recv()
    there = band.at[(1 - yl) * NX + x]
    to_right_and_left(there, there)
    relay(yl)

    for copy in wsends:
        copy.wait_recv()
    words_sum = wacc[pl.ds(pl.multiple_of(z * PART, PART), PART), :]
    for k, _ in z_peers:
        words_sum = words_sum + wrecv[k]
    mine[pl.ds(0, PART), :] = words_sum
    mine[pl.ds(PART, 8), :] = jnp.broadcast_to(band_power, (8, T))
    qsends = [remote(mine, qrecv.at[k], qss.at[k], qrs.at[k], d) for k, d in quad]
    for copy in qsends:
        copy.start()

    def logs(b, carry):
        for g in range(GROUP):
            slot = b * GROUP + g
            value = held[slot].astype(F32)
            term = jnp.where(
                value > 0.0, jnp.log(value) - context_log[pl.ds(cols[slot], 1), :], -1e30
            )
            base[slot] = term.T
        return carry

    lax.fori_loop(0, blocks // 2, logs, 0)
    for copy in qsends:
        copy.wait_recv()
    total = mine[...]
    for k, _ in quad:
        total = total + qrecv[k]
    words_all[z] = total
    asends = [
        remote(words_all.at[z], words_all.at[z], ass.at[k], ars.at[k], {"z": p}) for k, p in z_peers
    ]
    for copy in asends:
        copy.start()

    lax.fori_loop(blocks // 2, blocks, logs, 0)
    for copy in psends[3:5]:
        copy.wait_recv()
    relay(1 - yl)

    for copy in asends:
        copy.wait()
    for copy in csends + wsends + qsends + psends[0:5]:
        copy.wait_send()
    for copy in psends[5:9]:
        copy.wait()
    own.wait()


def totals(rows, cols, counts, panel):
    slots = counts.shape[0]
    return pl.pallas_call(
        totals_kernel,
        in_specs=[ANY, ANY, ANY, ANY],
        out_specs=[VMEM, ANY, VMEM, VMEM],
        out_shape=[
            jax.ShapeDtypeStruct((NZ, PART + 8, T), F32),
            jax.ShapeDtypeStruct((N_ROW, SHARE, T), BF16),
            jax.ShapeDtypeStruct((slots, T, T), F32),
            jax.ShapeDtypeStruct((ROW_TILES, T, T), F32),
        ],
        scratch_shapes=[
            pltpu.VMEM((SHARE, T), BF16),
            pltpu.VMEM((SHARE, T), BF16),
            pltpu.VMEM((slots, T, T), I32),
            pltpu.SMEM((slots,), I32),
            pltpu.SMEM((slots,), I32),
            pltpu.VMEM((T, ROW_TILES), F32),
            pltpu.VMEM((COL_TILES, T), F32),
            pltpu.VMEM((COL_TILES, T), F32),
            pltpu.VMEM((NZ, PART, T), F32),
            pltpu.VMEM((N_ROW, COL_TILES, T), F32),
            pltpu.VMEM((PART + 8, T), F32),
            pltpu.VMEM((NYH * NC, PART + 8, T), F32),
            DMA((slots // GROUP,)),
            DMA((NZ,)), DMA((NZ,)), DMA((N_ROW,)), DMA((N_ROW,)), DMA((NYH * NC,)), DMA((NYH * NC,)),
            DMA((NZ,)), DMA((NZ,)), DMA((9,)), DMA((9,)), DMA((4,)),
        ],
        compiler_params=pltpu.CompilerParams(collective_id=0, has_side_effects=True, vmem_limit_bytes=16 << 20),
        name="totals",
    )(rows, cols, counts, panel)


def word_kernel(rows, cols, base, words_all, band, cleared, tiles, partial, words, word_term):
    power = jnp.zeros((1, T), F32)
    for d in range(NZ):
        words[pl.ds(d * PART, PART), :] = words_all[d, 0:PART, :]
        power = power + words_all[d, PART : PART + 1, :]
    log_scale = jnp.log(power) - math.log(NEG_SAMPLES)
    word_term[...] = (log_scale - jnp.log(jnp.maximum(words[...], 1.0))).T

    def some(b, carry):
        for g in range(GROUP):
            slot = b * GROUP + g
            row, col = rows[slot], cols[slot]
            tile = jnp.maximum(base[slot] + word_term[pl.ds(row, 1), :], 0.0).astype(BF16)
            tiles[slot] = tile
            partial[row] += jnp.dot(band[col], tile, preferred_element_type=F32)
        return carry

    lax.fori_loop(0, base.shape[0] // GROUP, some, 0)


def word_products(rows, cols, base, words_all, band, cleared):
    slots = base.shape[0]
    return pl.pallas_call(
        word_kernel,
        in_specs=[SMEM, SMEM, VMEM, VMEM, VMEM, VMEM],
        out_specs=[VMEM, VMEM],
        scratch_shapes=[pltpu.VMEM((T, ROW_TILES), F32), pltpu.VMEM((ROW_TILES, T), F32)],
        out_shape=[
            jax.ShapeDtypeStruct((slots, T, T), BF16),
            jax.ShapeDtypeStruct((ROW_TILES, T, T), F32),
        ],
        input_output_aliases={5: 1},
        compiler_params=pltpu.CompilerParams(vmem_limit_bytes=28 << 20),
        name="word_products",
    )(rows, cols, base, words_all, band, cleared)


AWAY = (0, 1, 0)

Z_STEPS = (
    (0, 0, 0), (0, 1, 1), 4, 3, 5,
    (1, 1, 0), (1, 0, 1), (1, 0, 0), (1, 1, 1), (0, 0, 2), 2, 6,
    (2, 1, 0), (2, 0, 1), (2, 0, 0), (2, 1, 1), (1, 1, 2), (1, 0, 2), 1, 7,
    (3, 1, 0), (3, 0, 1), (3, 0, 0), (3, 1, 1), 0, (2, 1, 2), (2, 0, 2), None,
    (3, 1, 2), (3, 0, 2),
)
X_STEPS = (
    2, (0, 0, 0), (0, 1, 1), 1, 3,
    (1, 1, 0), (1, 0, 1), (0, 0, 2), (1, 0, 0), (1, 1, 1), 0, None,
    (1, 1, 2), (1, 0, 2),
)


def ring_sum(steps, length, y, raw, ready, ways, other_y, use, sendb, recvb,
             ysendb, yrecvb, ss, rs, yss, yrs):
    trades, sends, traded = {}, {}, set()
    last, end = length - 1, 2 * length

    def exchange(value, k):
        encode(value, ysendb.at[k])
        trades[k] = remote(ysendb.at[k], yrecvb.at[k], yss.at[k], yrs.at[k], other_y)
        trades[k].start()

    def term(d, lane):
        ready(d, lane // 2)
        if lane < 2:
            return raw(d, lane, 0)
        if d not in traded:
            trades[d].wait_recv()
            traded.add(d)
        return raw(d, y, 1) + decode(yrecvb.at[d])

    def arrived(h):
        value = raw(0, h, 0)
        for way in range(2):
            first, second = sends[last, way, 0][0], sends[last, way, 1][0]
            value = value + decode(recvb.at[first + h * (second - first)])
        return value

    for step in steps:
        if step is None:
            for lane in (0, 1):
                for way in range(2):
                    sends[last, way, lane][1].wait_recv()
            ready(0, 0)
            exchange(arrived(1 - y), end)
        elif isinstance(step, int):
            ready(step, 1)
            exchange(raw(step, 1 - y, 1), step)
        else:
            s, way, lane = step
            value = term(length - s if way == 0 else length + s, lane)
            if (s - 1, way, lane) in sends:
                index, before = sends[s - 1, way, lane]
                before.wait_recv()
                value = value + decode(recvb.at[index])
            n = len(sends)
            encode(value, sendb.at[n])
            copy = remote(sendb.at[n], recvb.at[n], ss.at[n], rs.at[n], ways[way])
            copy.start()
            sends[step] = (n, copy)

    first = arrived(y)
    trades[end].wait_recv()
    use(0, first + decode(yrecvb.at[end]))
    second = term(0, 2)
    for way in range(2):
        index, copy = sends[last, way, 2]
        copy.wait_recv()
        second = second + decode(recvb.at[index])
    use(1, second)

    def drain():
        for _, copy in sends.values():
            copy.wait_send()
        for copy in trades.values():
            copy.wait_send()

    return drain


def ring_scratch(steps, length):
    n, y = sum(isinstance(step, tuple) for step in steps), 2 * length + 1
    return [
        pltpu.VMEM((n, CODE, T), I16), pltpu.VMEM((n, CODE, T), I16),
        pltpu.VMEM((y, CODE, T), I16), pltpu.VMEM((y, CODE, T), I16),
        DMA((n,)), DMA((n,)), DMA((y,)), DMA((y,)),
    ]


def word_panel_kernel(partial, share, everyone, sib, mine, xss, xrs, gss, grs, hss, hrs, pss, prs, ms,
                      *ring):
    z, yh, c = lax.axis_index("z"), lax.axis_index("yh"), lax.axis_index("core")
    ways = ({"z": lax.rem(z + 1, NZ)}, {"z": lax.rem(z + NZ - 1, NZ)})
    other_y, other_core = {"yh": 1 - yh}, {"core": 1 - c}
    length = NZ // 2

    greet([*ways, other_y, other_core])
    swaps, here = {}, set()
    for dz in (4, 3, 5, 2, 6, 1, 7, 0):
        for part in range(2):
            for h in range(2):
                k, rows = (dz * 2 + h) * 2 + part, pl.ds(part * HALF, HALF)
                swaps[dz, h, part] = remote(
                    partial.at[lax.rem(z + dz, NZ), h, 1 - c, rows], sib.at[dz * 2 + h, rows],
                    xss.at[k], xrs.at[k], other_core,
                )
                swaps[dz, h, part].start()

    def ready(d, part):
        if (d, part) not in here:
            here.add((d, part))
            for h in range(2):
                swaps[d, h, part].wait_recv()

    def raw(d, h, part):
        rows = pl.ds(part * HALF, HALF)
        return partial[lax.rem(z + d, NZ), h, c, rows, :] + sib[d * 2 + h, rows, :]

    pair = (pl.ds(0, 2), pl.ds(2, 2))

    def place(d, h, part):
        return everyone.at[lax.rem(z + d, NZ), h, c, pair[part]]

    gives, hands, passes, keeps = {}, [], {}, []

    def hand(src, dst, k):
        copy = remote(src, dst, hss.at[k], hrs.at[k], other_core)
        copy.start()
        hands.append(copy)

    def along_y(src, dst, k):
        passes[k] = remote(src, dst, pss.at[k], prs.at[k], other_y)
        passes[k].start()

    def lane_place(d, lane):
        return place(d, 1 - yh if lane == 1 else yh, 1 if lane == 2 else 0)

    def give(s, way, lane, src=None):
        dst = lane_place((NZ - s) % NZ if way == 0 else s, lane)
        k = (s * 2 + way) * 3 + lane
        gives[s, way, lane] = remote(dst if src is None else src, dst, gss.at[k], grs.at[k], ways[way])
        gives[s, way, lane].start()

    own = (mine.at[pair[0]], mine.at[pair[1]])

    def use(part, total):
        straight = [total[t * T : (t + 1) * T].T for t in range(2)]
        for t in range(2):
            mine[part * 2 + t] = straight[t].astype(BF16)
        along_y(own[part], place(0, yh, part), 0 if part else NZ)
        for way in range(2):
            give(0, way, 2 if part else 0, own[part])
        hand(own[part], place(0, yh, part), 2 * NZ if part else 0)
        keeps.append(pltpu.make_async_copy(own[part], place(0, yh, part), ms.at[part]))
        keeps[-1].start()
        for t in range(2):
            share[pl.ds(part * HALF + t * T, T), :] = straight[t]

    drain = ring_sum(Z_STEPS, length, yh, raw, ready, ways, other_y, use, *ring)
    due = [0]
    for s in range(1, length + 1):
        came = []
        for lane in (0, 2, 1) if s == 1 else (2, 0, 1):
            if s == 1 and lane == 1:
                passes[NZ].wait_recv()
                for way in range(2):
                    give(0, way, 1)
                hand(lane_place(0, 1), lane_place(0, 1), 1)
            for way in range(2):
                if (s - 1, way, lane) not in gives:
                    continue
                gives[s - 1, way, lane].wait_recv()
                if s < length - 1 or (s == length - 1 and way == AWAY[lane]):
                    give(s, way, lane)
                d = (NZ - s) % NZ if way == 0 else s
                at = lane_place(d, lane)
                if lane == 2:
                    along_y(at, at, d)
                    came.append(d)
                hand(at, at, 2 * NZ + d if lane == 2 else d * 2 + lane)
        for d in due:
            passes[d].wait_recv()
            hand(place(d, 1 - yh, 1), place(d, 1 - yh, 1), 3 * NZ + d)
        due = came
    for d in due:
        passes[d].wait_recv()
        hand(place(d, 1 - yh, 1), place(d, 1 - yh, 1), 3 * NZ + d)

    for copy in hands:
        copy.wait()
    for copy in list(gives.values()) + list(passes.values()) + list(swaps.values()):
        copy.wait_send()
    drain()
    for copy in keeps:
        copy.wait()


def word_panel_sum(partial):
    return pl.pallas_call(
        word_panel_kernel,
        in_specs=[VMEM],
        out_specs=[VMEM, ANY],
        out_shape=[
            jax.ShapeDtypeStruct((SHARE, T), F32),
            jax.ShapeDtypeStruct((NZ, NYH, NC, 4, T, T), BF16),
        ],
        scratch_shapes=[
            pltpu.VMEM((2 * NZ, SHARE, T), F32),
            pltpu.VMEM((4, T, T), BF16),
            DMA((4 * NZ,)), DMA((4 * NZ,)), DMA((3 * NZ,)), DMA((3 * NZ,)),
            DMA((4 * NZ,)), DMA((4 * NZ,)), DMA((NZ + 1,)), DMA((NZ + 1,)), DMA((2,)),
            *ring_scratch(Z_STEPS, NZ // 2),
        ],
        compiler_params=pltpu.CompilerParams(collective_id=1, has_side_effects=True, vmem_limit_bytes=16 << 20),
        name="word_panel_sum",
    )(partial)


def context_kernel(rows, cols, tiles, rounded, share, partial, share_out):
    share_out[...] = share[...]
    partial[...] = jnp.zeros_like(partial)

    def some(b, carry):
        for g in range(GROUP):
            slot = b * GROUP + g
            partial[cols[slot]] += jnp.dot(tiles[slot], rounded[rows[slot]], preferred_element_type=F32)
        return carry

    lax.fori_loop(0, tiles.shape[0] // GROUP, some, 0)


def context_products(rows, cols, tiles, rounded, share):
    slots = tiles.shape[0]
    return pl.pallas_call(
        context_kernel,
        in_specs=[SMEM, SMEM, VMEM, VMEM, VMEM],
        out_specs=[VMEM, VMEM],
        out_shape=[
            jax.ShapeDtypeStruct((COL_TILES, T, T), F32),
            jax.ShapeDtypeStruct((SHARE, T), F32),
        ],
        compiler_params=pltpu.CompilerParams(vmem_limit_bytes=16 << 20),
        name="context_products",
    )(rows, cols, tiles, rounded, share)


def context_panel_kernel(partial, share, *ring):
    x, yl = lax.axis_index("x"), lax.axis_index("yl")
    ways = ({"x": lax.rem(x + 1, NX)}, {"x": lax.rem(x + NX - 1, NX)})
    other_y = {"yl": 1 - yl}
    greet([*ways, other_y])

    def raw(d, h, part):
        return partial[h, lax.rem(x + d, NX), pl.ds(part * HALF, HALF), :]

    def use(part, total):
        share[pl.ds(part * HALF, HALF), :] = total * (1.0 / T)

    ring_sum(X_STEPS, NX // 2, yl, raw, lambda d, part: None, ways, other_y, use, *ring)()


def context_panel_sum(partial):
    return pl.pallas_call(
        context_panel_kernel,
        in_specs=[VMEM],
        out_specs=VMEM,
        out_shape=jax.ShapeDtypeStruct((SHARE, T), F32),
        scratch_shapes=ring_scratch(X_STEPS, NX // 2),
        compiler_params=pltpu.CompilerParams(collective_id=2, has_side_effects=True, vmem_limit_bytes=8 << 20),
        name="context_panel_sum",
    )(partial)


def shards(tile_counts, tile_rows, tile_cols, panel):
    counts, rows, cols = tile_counts[0, 0], tile_rows[0, 0], tile_cols[0, 0]
    far = [pltpu.with_memory_space_constraint(a, pltpu.HBM) for a in (rows, cols, counts, panel)]
    words_all, band, base, cleared = totals(*far)
    band = band.reshape(COL_TILES, T, T)
    tiles, partial = word_products(rows, cols, base, words_all, band, cleared)
    share, everyone = word_panel_sum(partial.reshape(NZ, NYH, NC, SHARE, T))
    rounded = everyone.reshape(ROW_TILES, T, T)
    context_partial, share = context_products(rows, cols, tiles, rounded, share)
    context_share = context_panel_sum(context_partial.reshape(NYL, NX, SHARE, T))
    return share, context_share


def solution(mesh):
    split = Mesh(
        mesh.devices.reshape(NYL, NX, NZ, NYH, NC), ("yl", "x", "z", "yh", "core")
    )
    row, col = ("yl", "x"), ("z", "yh", "core")
    in_specs = (
        P(row, col, None, None, None),
        P(row, col, None),
        P(row, col, None),
        P(col + row, None),
    )
    out_specs = (P(row + col, None), P(col + row, None))
    return jax.shard_map(shards, mesh=split, in_specs=in_specs, out_specs=out_specs, check_vma=False)
```

```python
import functools
import math

import jax
import jax.numpy as jnp
from jax import lax
from jax.experimental import pallas as pl
from jax.experimental.pallas import tpu as pltpu
from jax.sharding import Mesh
from jax.sharding import PartitionSpec as P

NEG_SAMPLES = 15
T = 128
NX, NYL, NYH, NZ, NC = 4, 2, 2, 8, 2
N_ROW, N_COL = NX * NYL, NZ * NYH * NC
ROW_TILES, COL_TILES = 128, 32
SHARE = 512
HALF = SHARE // 2
CODE = HALF + 16
MESH = pl.DeviceIdType.MESH
F32, BF16, I32, I16 = jnp.float32, jnp.bfloat16, jnp.int32, jnp.int16
ANY = pl.BlockSpec(memory_space=pl.ANY)
VMEM = pl.BlockSpec(memory_space=pltpu.VMEM)
SMEM = pl.BlockSpec(memory_space=pltpu.SMEM)
DMA = pltpu.SemaphoreType.DMA
LN2 = math.log(2.0)


def remote(src, dst, ssem, rsem, device):
    return pltpu.make_async_remote_copy(
        src_ref=src, dst_ref=dst, send_sem=ssem, recv_sem=rsem,
        device_id=device, device_id_type=MESH,
    )


def hail(devices):
    for device in devices:
        pl.semaphore_signal(
            pltpu.get_barrier_semaphore(), inc=1, device_id=device, device_id_type=MESH
        )


def await_hails(devices):
    pl.semaphore_wait(pltpu.get_barrier_semaphore(), len(devices))


def greet(devices):
    hail(devices)
    await_hails(devices)


def encode(value, ref):
    top = jnp.max(jnp.abs(value), axis=0, keepdims=True)
    expo = jnp.ceil(jnp.log(jnp.maximum(top, 1e-30)) * (1.0 / LN2) + 0.001) - 14.0
    scaled = jnp.round(value * jnp.exp(expo * -LN2))
    ref[pl.ds(0, HALF), :] = scaled.astype(I32).astype(I16)
    ref[pl.ds(HALF, 16), :] = jnp.broadcast_to(expo, (16, T)).astype(I32).astype(I16)


def decode(ref):
    expo = ref[pl.ds(HALF, 16), :].astype(I32).astype(F32)[0:1]
    return ref[pl.ds(0, HALF), :].astype(I32).astype(F32) * jnp.exp(expo * LN2)


GROUP = 16
PART = T // NZ


def powers_of(totals):
    root = jnp.sqrt(totals)
    return root * jnp.sqrt(root)


def load_counts(counts, held, sem):
    copies = []
    for b in range(counts.shape[0] // GROUP):
        part = pl.ds(b * GROUP, GROUP)
        copies.append(pltpu.make_async_copy(counts.at[part], held.at[part], sem.at[b]))
        copies[-1].start()
    return copies


def await_counts(counts, held, sem, b):
    part = pl.ds(b * GROUP, GROUP)
    pltpu.make_async_copy(counts.at[part], held.at[part], sem.at[b]).wait()


def totals_kernel(rows_in, cols_in, counts, panel_in, words_all, band, base, cleared,
                  brought, panel, held, rows, cols, wacc, contexts, context_log, wrecv, crecv, mine, qrecv,
                  cs, wss, wrs, css, crs, qss, qrs, ass, ars, pss, prs, lsem):
    x, yl = lax.axis_index("x"), lax.axis_index("yl")
    z, yh, c = lax.axis_index("z"), lax.axis_index("yh"), lax.axis_index("core")
    blocks = counts.shape[0] // GROUP
    row = yl * NX + x
    right, left = lax.rem(x + 1, NX), lax.rem(x + NX - 1, NX)
    row_peers = [
        (dx * NYL + dy, {"x": lax.rem(x + dx, NX), "yl": lax.rem(yl + dy, NYL)})
        for dx in range(NX) for dy in range(NYL) if dx or dy
    ]
    z_peers = [(dz, lax.rem(z + dz, NZ)) for dz in (4, 3, 5, 2, 6, 1, 7)]
    quad = [
        (dy * NC + dc, {"yh": lax.rem(yh + dy, NYH), "core": lax.rem(c + dc, NC)})
        for dy, dc in ((1, 0), (1, 1), (0, 1))
    ]
    everybody = [d for _, d in row_peers] + [{"z": p} for _, p in z_peers] + [d for _, d in quad]
    slots = [
        pltpu.make_async_copy(rows_in, rows, lsem.at[1]),
        pltpu.make_async_copy(cols_in, cols, lsem.at[2]),
    ]
    bring = pltpu.make_async_copy(panel_in, brought, lsem.at[3])
    hail(everybody)
    for copy in (bring, *slots):
        copy.start()
    load_counts(counts, held, cs)
    bring.wait()
    for t in range(4):
        tile = pl.ds(t * T, T)
        panel[tile, :] = brought[tile, :].astype(F32).T.astype(BF16)
    own = pltpu.make_async_copy(panel, band.at[row], lsem.at[0])
    own.start()

    wacc[...] = jnp.zeros_like(wacc)
    lanes = lax.broadcasted_iota(I32, (T, T), 1)
    bands = lax.broadcasted_iota(I32, (COL_TILES, T), 0)
    ones = jnp.ones((2 * T, T), BF16)
    for copy in slots:
        copy.wait()

    def some(b, per_context):
        await_counts(counts, held, cs, b)
        per_word = wacc[...]
        for g in range(GROUP):
            slot = b * GROUP + g
            value = held[slot]
            per_context = per_context + jnp.where(
                bands == cols[slot], jnp.sum(value, axis=0, keepdims=True), 0
            )
            if g % 4 == 3:
                eights = jnp.bitwise_and(value, -8)
                parts = [a.astype(F32).astype(BF16) for a in (eights, value - eights)]
                sums = jnp.dot(jnp.concatenate(parts, axis=1), ones, preferred_element_type=F32)
            else:
                sums = jnp.sum(value.astype(F32), axis=1, keepdims=True)
            per_word = per_word + jnp.where(lanes == rows[slot], sums, 0.0)
        wacc[...] = per_word
        return per_context

    per_context = lax.fori_loop(0, blocks, some, jnp.zeros((COL_TILES, T), I32))
    contexts[...] = per_context.astype(F32)
    await_hails(everybody)

    csends = [remote(contexts, crecv.at[k], css.at[k], crs.at[k], d) for k, d in row_peers]
    for copy in csends:
        copy.start()
    wsends = [
        remote(wacc.at[pl.ds(pl.multiple_of(p * PART, PART), PART)], wrecv.at[k], wss.at[k], wrs.at[k], {"z": p})
        for k, p in z_peers
    ]
    for copy in wsends:
        copy.start()

    psends = []

    def pass_on(src, dst, device):
        k = len(psends)
        psends.append(remote(src, dst, pss.at[k], prs.at[k], device))
        psends[k].start()

    def to_right_and_left(first, second):
        pass_on(first, first, {"x": right})
        pass_on(second, second, {"x": left})

    def relay(y):
        to_right_and_left(
            band.at[y * NX + left, pl.ds(0, HALF)], band.at[y * NX + right, pl.ds(HALF, HALF)]
        )

    pass_on(panel, band.at[row], {"yl": 1 - yl})
    pass_on(panel, band.at[row], {"x": right})
    pass_on(panel, band.at[row], {"x": left})

    def clear(t, carry):
        cleared[t] = jnp.zeros((T, T), F32)
        return carry

    lax.fori_loop(0, ROW_TILES, clear, 0, unroll=4)
    for copy in csends:
        copy.wait_recv()
    contexts_sum = contexts[...]
    for k, _ in row_peers:
        contexts_sum = contexts_sum + crecv[k]
    powers = powers_of(contexts_sum)
    band_power = jnp.sum(powers, keepdims=True)
    context_log[...] = jnp.log(jnp.maximum(powers, 1.0))

    for copy in psends[0:3]:
        copy.wait_recv()
    there = band.at[(1 - yl) * NX + x]
    to_right_and_left(there, there)
    relay(yl)

    for copy in wsends:
        copy.wait_recv()
    words_sum = wacc[pl.ds(pl.multiple_of(z * PART, PART), PART), :]
    for k, _ in z_peers:
        words_sum = words_sum + wrecv[k]
    mine[pl.ds(0, PART), :] = words_sum
    mine[pl.ds(PART, 8), :] = jnp.broadcast_to(band_power, (8, T))
    qsends = [remote(mine, qrecv.at[k], qss.at[k], qrs.at[k], d) for k, d in quad]
    for copy in qsends:
        copy.start()

    def logs(b, carry):
        for g in range(GROUP):
            slot = b * GROUP + g
            value = held[slot].astype(F32)
            term = jnp.where(
                value > 0.0, jnp.log(value) - context_log[pl.ds(cols[slot], 1), :], -1e30
            )
            base[slot] = term.T
        return carry

    lax.fori_loop(0, blocks // 2, logs, 0)
    for copy in qsends:
        copy.wait_recv()
    total = mine[...]
    for k, _ in quad:
        total = total + qrecv[k]
    words_all[z] = total
    asends = [
        remote(words_all.at[z], words_all.at[z], ass.at[k], ars.at[k], {"z": p}) for k, p in z_peers
    ]
    for copy in asends:
        copy.start()

    lax.fori_loop(blocks // 2, blocks, logs, 0)
    for copy in psends[3:5]:
        copy.wait_recv()
    relay(1 - yl)

    for copy in asends:
        copy.wait()
    for copy in csends + wsends + qsends + psends[0:5]:
        copy.wait_send()
    for copy in psends[5:9]:
        copy.wait()
    own.wait()


def totals(rows, cols, counts, panel):
    slots = counts.shape[0]
    return pl.pallas_call(
        totals_kernel,
        in_specs=[ANY, ANY, ANY, ANY],
        out_specs=[VMEM, ANY, VMEM, VMEM],
        out_shape=[
            jax.ShapeDtypeStruct((NZ, PART + 8, T), F32),
            jax.ShapeDtypeStruct((N_ROW, SHARE, T), BF16),
            jax.ShapeDtypeStruct((slots, T, T), F32),
            jax.ShapeDtypeStruct((ROW_TILES, T, T), F32),
        ],
        scratch_shapes=[
            pltpu.VMEM((SHARE, T), BF16),
            pltpu.VMEM((SHARE, T), BF16),
            pltpu.VMEM((slots, T, T), I32),
            pltpu.SMEM((slots,), I32),
            pltpu.SMEM((slots,), I32),
            pltpu.VMEM((T, ROW_TILES), F32),
            pltpu.VMEM((COL_TILES, T), F32),
            pltpu.VMEM((COL_TILES, T), F32),
            pltpu.VMEM((NZ, PART, T), F32),
            pltpu.VMEM((N_ROW, COL_TILES, T), F32),
            pltpu.VMEM((PART + 8, T), F32),
            pltpu.VMEM((NYH * NC, PART + 8, T), F32),
            DMA((slots // GROUP,)),
            DMA((NZ,)), DMA((NZ,)), DMA((N_ROW,)), DMA((N_ROW,)), DMA((NYH * NC,)), DMA((NYH * NC,)),
            DMA((NZ,)), DMA((NZ,)), DMA((9,)), DMA((9,)), DMA((4,)),
        ],
        compiler_params=pltpu.CompilerParams(collective_id=0, has_side_effects=True, vmem_limit_bytes=16 << 20),
        name="totals",
    )(rows, cols, counts, panel)


def word_kernel(rows, cols, base, words_all, band, cleared, tiles, partial, words, word_term):
    power = jnp.zeros((1, T), F32)
    for d in range(NZ):
        words[pl.ds(d * PART, PART), :] = words_all[d, 0:PART, :]
        power = power + words_all[d, PART : PART + 1, :]
    log_scale = jnp.log(power) - math.log(NEG_SAMPLES)
    word_term[...] = (log_scale - jnp.log(jnp.maximum(words[...], 1.0))).T

    def some(b, carry):
        for g in range(GROUP):
            slot = b * GROUP + g
            row, col = rows[slot], cols[slot]
            tile = jnp.maximum(base[slot] + word_term[pl.ds(row, 1), :], 0.0).astype(BF16)
            tiles[slot] = tile
            partial[row] += jnp.dot(band[col], tile, preferred_element_type=F32)
        return carry

    lax.fori_loop(0, base.shape[0] // GROUP, some, 0)


def word_products(rows, cols, base, words_all, band, cleared):
    slots = base.shape[0]
    return pl.pallas_call(
        word_kernel,
        in_specs=[SMEM, SMEM, VMEM, VMEM, VMEM, VMEM],
        out_specs=[VMEM, VMEM],
        scratch_shapes=[pltpu.VMEM((T, ROW_TILES), F32), pltpu.VMEM((ROW_TILES, T), F32)],
        out_shape=[
            jax.ShapeDtypeStruct((slots, T, T), BF16),
            jax.ShapeDtypeStruct((ROW_TILES, T, T), F32),
        ],
        input_output_aliases={5: 1},
        compiler_params=pltpu.CompilerParams(vmem_limit_bytes=28 << 20),
        name="word_products",
    )(rows, cols, base, words_all, band, cleared)


AWAY = (0, 1, 0)

Z_STEPS = (
    (0, 0, 0), (0, 1, 1), 4, 3, 5,
    (1, 1, 0), (1, 0, 1), (1, 0, 0), (1, 1, 1), (0, 0, 2), 2, 6,
    (2, 1, 0), (2, 0, 1), (2, 0, 0), (2, 1, 1), (1, 1, 2), (1, 0, 2), 1, 7,
    (3, 1, 0), (3, 0, 1), (3, 0, 0), (3, 1, 1), 0, (2, 1, 2), (2, 0, 2), None,
    (3, 1, 2), (3, 0, 2),
)
X_STEPS = (
    2, (0, 0, 0), (0, 1, 1), 1, 3,
    (1, 1, 0), (1, 0, 1), (0, 0, 2), (1, 0, 0), (1, 1, 1), 0, None,
    (1, 1, 2), (1, 0, 2),
)


def ring_sum(steps, length, y, raw, ready, ways, other_y, use, sendb, recvb,
             ysendb, yrecvb, ss, rs, yss, yrs):
    trades, sends, traded = {}, {}, set()
    last, end = length - 1, 2 * length

    def exchange(value, k):
        encode(value, ysendb.at[k])
        trades[k] = remote(ysendb.at[k], yrecvb.at[k], yss.at[k], yrs.at[k], other_y)
        trades[k].start()

    def term(d, lane):
        ready(d, lane // 2)
        if lane < 2:
            return raw(d, lane, 0)
        if d not in traded:
            trades[d].wait_recv()
            traded.add(d)
        return raw(d, y, 1) + decode(yrecvb.at[d])

    def arrived(h):
        value = raw(0, h, 0)
        for way in range(2):
            first, second = sends[last, way, 0][0], sends[last, way, 1][0]
            value = value + decode(recvb.at[first + h * (second - first)])
        return value

    for step in steps:
        if step is None:
            for lane in (0, 1):
                for way in range(2):
                    sends[last, way, lane][1].wait_recv()
            ready(0, 0)
            exchange(arrived(1 - y), end)
        elif isinstance(step, int):
            ready(step, 1)
            exchange(raw(step, 1 - y, 1), step)
        else:
            s, way, lane = step
            value = term(length - s if way == 0 else length + s, lane)
            if (s - 1, way, lane) in sends:
                index, before = sends[s - 1, way, lane]
                before.wait_recv()
                value = value + decode(recvb.at[index])
            n = len(sends)
            encode(value, sendb.at[n])
            copy = remote(sendb.at[n], recvb.at[n], ss.at[n], rs.at[n], ways[way])
            copy.start()
            sends[step] = (n, copy)

    first = arrived(y)
    trades[end].wait_recv()
    use(0, first + decode(yrecvb.at[end]))
    second = term(0, 2)
    for way in range(2):
        index, copy = sends[last, way, 2]
        copy.wait_recv()
        second = second + decode(recvb.at[index])
    use(1, second)

    def drain():
        for _, copy in sends.values():
            copy.wait_send()
        for copy in trades.values():
            copy.wait_send()

    return drain


def ring_scratch(steps, length):
    n, y = sum(isinstance(step, tuple) for step in steps), 2 * length + 1
    return [
        pltpu.VMEM((n, CODE, T), I16), pltpu.VMEM((n, CODE, T), I16),
        pltpu.VMEM((y, CODE, T), I16), pltpu.VMEM((y, CODE, T), I16),
        DMA((n,)), DMA((n,)), DMA((y,)), DMA((y,)),
    ]


def word_panel_kernel(partial, share, everyone, sib, mine, xss, xrs, gss, grs, hss, hrs, pss, prs, ms,
                      *ring):
    z, yh, c = lax.axis_index("z"), lax.axis_index("yh"), lax.axis_index("core")
    ways = ({"z": lax.rem(z + 1, NZ)}, {"z": lax.rem(z + NZ - 1, NZ)})
    other_y, other_core = {"yh": 1 - yh}, {"core": 1 - c}
    length = NZ // 2

    greet([*ways, other_y, other_core])
    swaps, here = {}, set()
    for dz in (4, 3, 5, 2, 6, 1, 7, 0):
        for part in range(2):
            for h in range(2):
                k, rows = (dz * 2 + h) * 2 + part, pl.ds(part * HALF, HALF)
                swaps[dz, h, part] = remote(
                    partial.at[lax.rem(z + dz, NZ), h, 1 - c, rows], sib.at[dz * 2 + h, rows],
                    xss.at[k], xrs.at[k], other_core,
                )
                swaps[dz, h, part].start()

    def ready(d, part):
        if (d, part) not in here:
            here.add((d, part))
            for h in range(2):
                swaps[d, h, part].wait_recv()

    def raw(d, h, part):
        rows = pl.ds(part * HALF, HALF)
        return partial[lax.rem(z + d, NZ), h, c, rows, :] + sib[d * 2 + h, rows, :]

    pair = (pl.ds(0, 2), pl.ds(2, 2))

    def place(d, h, part):
        return everyone.at[lax.rem(z + d, NZ), h, c, pair[part]]

    gives, hands, passes, keeps = {}, [], {}, []

    def hand(src, dst, k):
        copy = remote(src, dst, hss.at[k], hrs.at[k], other_core)
        copy.start()
        hands.append(copy)

    def along_y(src, dst, k):
        passes[k] = remote(src, dst, pss.at[k], prs.at[k], other_y)
        passes[k].start()

    def lane_place(d, lane):
        return place(d, 1 - yh if lane == 1 else yh, 1 if lane == 2 else 0)

    def give(s, way, lane, src=None):
        dst = lane_place((NZ - s) % NZ if way == 0 else s, lane)
        k = (s * 2 + way) * 3 + lane
        gives[s, way, lane] = remote(dst if src is None else src, dst, gss.at[k], grs.at[k], ways[way])
        gives[s, way, lane].start()

    own = (mine.at[pair[0]], mine.at[pair[1]])

    def use(part, total):
        straight = [total[t * T : (t + 1) * T].T for t in range(2)]
        for t in range(2):
            mine[part * 2 + t] = straight[t].astype(BF16)
        along_y(own[part], place(0, yh, part), 0 if part else NZ)
        for way in range(2):
            give(0, way, 2 if part else 0, own[part])
        hand(own[part], place(0, yh, part), 2 * NZ if part else 0)
        keeps.append(pltpu.make_async_copy(own[part], place(0, yh, part), ms.at[part]))
        keeps[-1].start()
        for t in range(2):
            share[pl.ds(part * HALF + t * T, T), :] = straight[t]

    drain = ring_sum(Z_STEPS, length, yh, raw, ready, ways, other_y, use, *ring)
    passes[NZ].wait_recv()
    for way in range(2):
        give(0, way, 1)
    hand(lane_place(0, 1), lane_place(0, 1), 1)
    due = [0]
    for s in range(1, length + 1):
        came = []
        for lane in (0, 2, 1) if s == 1 else (2, 0, 1):
            for way in range(2):
                if (s - 1, way, lane) not in gives:
                    continue
                gives[s - 1, way, lane].wait_recv()
                if s < length - 1 or (s == length - 1 and way == AWAY[lane]):
                    give(s, way, lane)
                d = (NZ - s) % NZ if way == 0 else s
                at = lane_place(d, lane)
                if lane == 2:
                    along_y(at, at, d)
                    came.append(d)
                hand(at, at, 2 * NZ + d if lane == 2 else d * 2 + lane)
        for d in due:
            passes[d].wait_recv()
            hand(place(d, 1 - yh, 1), place(d, 1 - yh, 1), 3 * NZ + d)
        due = came
    for d in due:
        passes[d].wait_recv()
        hand(place(d, 1 - yh, 1), place(d, 1 - yh, 1), 3 * NZ + d)

    for copy in hands:
        copy.wait()
    for copy in list(gives.values()) + list(passes.values()) + list(swaps.values()):
        copy.wait_send()
    drain()
    for copy in keeps:
        copy.wait()


def word_panel_sum(partial):
    return pl.pallas_call(
        word_panel_kernel,
        in_specs=[VMEM],
        out_specs=[VMEM, ANY],
        out_shape=[
            jax.ShapeDtypeStruct((SHARE, T), F32),
            jax.ShapeDtypeStruct((NZ, NYH, NC, 4, T, T), BF16),
        ],
        scratch_shapes=[
            pltpu.VMEM((2 * NZ, SHARE, T), F32),
            pltpu.VMEM((4, T, T), BF16),
            DMA((4 * NZ,)), DMA((4 * NZ,)), DMA((3 * NZ,)), DMA((3 * NZ,)),
            DMA((4 * NZ,)), DMA((4 * NZ,)), DMA((NZ + 1,)), DMA((NZ + 1,)), DMA((2,)),
            *ring_scratch(Z_STEPS, NZ // 2),
        ],
        compiler_params=pltpu.CompilerParams(collective_id=1, has_side_effects=True, vmem_limit_bytes=16 << 20),
        name="word_panel_sum",
    )(partial)


def context_kernel(rows, cols, tiles, rounded, share, partial, share_out):
    share_out[...] = share[...]
    partial[...] = jnp.zeros_like(partial)

    def some(b, carry):
        for g in range(GROUP):
            slot = b * GROUP + g
            partial[cols[slot]] += jnp.dot(tiles[slot], rounded[rows[slot]], preferred_element_type=F32)
        return carry

    lax.fori_loop(0, tiles.shape[0] // GROUP, some, 0)


def context_products(rows, cols, tiles, rounded, share):
    slots = tiles.shape[0]
    return pl.pallas_call(
        context_kernel,
        in_specs=[SMEM, SMEM, VMEM, VMEM, VMEM],
        out_specs=[VMEM, VMEM],
        out_shape=[
            jax.ShapeDtypeStruct((COL_TILES, T, T), F32),
            jax.ShapeDtypeStruct((SHARE, T), F32),
        ],
        compiler_params=pltpu.CompilerParams(vmem_limit_bytes=16 << 20),
        name="context_products",
    )(rows, cols, tiles, rounded, share)


def context_panel_kernel(partial, share, *ring):
    x, yl = lax.axis_index("x"), lax.axis_index("yl")
    ways = ({"x": lax.rem(x + 1, NX)}, {"x": lax.rem(x + NX - 1, NX)})
    other_y = {"yl": 1 - yl}
    greet([*ways, other_y])

    def raw(d, h, part):
        return partial[h, lax.rem(x + d, NX), pl.ds(part * HALF, HALF), :]

    def use(part, total):
        share[pl.ds(part * HALF, HALF), :] = total * (1.0 / T)

    ring_sum(X_STEPS, NX // 2, yl, raw, lambda d, part: None, ways, other_y, use, *ring)()


def context_panel_sum(partial):
    return pl.pallas_call(
        context_panel_kernel,
        in_specs=[VMEM],
        out_specs=VMEM,
        out_shape=jax.ShapeDtypeStruct((SHARE, T), F32),
        scratch_shapes=ring_scratch(X_STEPS, NX // 2),
        compiler_params=pltpu.CompilerParams(collective_id=2, has_side_effects=True, vmem_limit_bytes=8 << 20),
        name="context_panel_sum",
    )(partial)


def shards(tile_counts, tile_rows, tile_cols, panel):
    counts, rows, cols = tile_counts[0, 0], tile_rows[0, 0], tile_cols[0, 0]
    far = [pltpu.with_memory_space_constraint(a, pltpu.HBM) for a in (rows, cols, counts, panel)]
    words_all, band, base, cleared = totals(*far)
    band = band.reshape(COL_TILES, T, T)
    tiles, partial = word_products(rows, cols, base, words_all, band, cleared)
    share, everyone = word_panel_sum(partial.reshape(NZ, NYH, NC, SHARE, T))
    rounded = everyone.reshape(ROW_TILES, T, T)
    context_partial, share = context_products(rows, cols, tiles, rounded, share)
    context_share = context_panel_sum(context_partial.reshape(NYL, NX, SHARE, T))
    return share, context_share


def solution(mesh):
    split = Mesh(
        mesh.devices.reshape(NYL, NX, NZ, NYH, NC), ("yl", "x", "z", "yh", "core")
    )
    row, col = ("yl", "x"), ("z", "yh", "core")
    in_specs = (
        P(row, col, None, None, None),
        P(row, col, None),
        P(row, col, None),
        P(col + row, None),
    )
    out_specs = (P(row + col, None), P(col + row, None))
    return jax.shard_map(shards, mesh=split, in_specs=in_specs, out_specs=out_specs, check_vma=False)
```

```python
import functools
import math

import jax
import jax.numpy as jnp
from jax import lax
from jax.experimental import pallas as pl
from jax.experimental.pallas import tpu as pltpu
from jax.sharding import Mesh
from jax.sharding import PartitionSpec as P

NEG_SAMPLES = 15
T = 128
NX, NYL, NYH, NZ, NC = 4, 2, 2, 8, 2
N_ROW, N_COL = NX * NYL, NZ * NYH * NC
ROW_TILES, COL_TILES = 128, 32
SHARE = 512
HALF = SHARE // 2
CODE = HALF + 16
MESH = pl.DeviceIdType.MESH
F32, BF16, I32, I16 = jnp.float32, jnp.bfloat16, jnp.int32, jnp.int16
ANY = pl.BlockSpec(memory_space=pl.ANY)
VMEM = pl.BlockSpec(memory_space=pltpu.VMEM)
SMEM = pl.BlockSpec(memory_space=pltpu.SMEM)
DMA = pltpu.SemaphoreType.DMA
LN2 = math.log(2.0)


def remote(src, dst, ssem, rsem, device):
    return pltpu.make_async_remote_copy(
        src_ref=src, dst_ref=dst, send_sem=ssem, recv_sem=rsem,
        device_id=device, device_id_type=MESH,
    )


def hail(devices):
    for device in devices:
        pl.semaphore_signal(
            pltpu.get_barrier_semaphore(), inc=1, device_id=device, device_id_type=MESH
        )


def await_hails(devices):
    pl.semaphore_wait(pltpu.get_barrier_semaphore(), len(devices))


def greet(devices):
    hail(devices)
    await_hails(devices)


def encode(value, ref):
    top = jnp.max(jnp.abs(value), axis=0, keepdims=True)
    expo = jnp.ceil(jnp.log(jnp.maximum(top, 1e-30)) * (1.0 / LN2) + 0.001) - 14.0
    scaled = jnp.round(value * jnp.exp(expo * -LN2))
    ref[pl.ds(0, HALF), :] = scaled.astype(I32).astype(I16)
    ref[pl.ds(HALF, 16), :] = jnp.broadcast_to(expo, (16, T)).astype(I32).astype(I16)


def decode(ref):
    expo = ref[pl.ds(HALF, 16), :].astype(I32).astype(F32)[0:1]
    return ref[pl.ds(0, HALF), :].astype(I32).astype(F32) * jnp.exp(expo * LN2)


GROUP = 16
PART = T // NZ


def powers_of(totals):
    root = jnp.sqrt(totals)
    return root * jnp.sqrt(root)


def load_counts(counts, held, sem):
    copies = []
    for b in range(counts.shape[0] // GROUP):
        part = pl.ds(b * GROUP, GROUP)
        copies.append(pltpu.make_async_copy(counts.at[part], held.at[part], sem.at[b]))
        copies[-1].start()
    return copies


def await_counts(counts, held, sem, b):
    part = pl.ds(b * GROUP, GROUP)
    pltpu.make_async_copy(counts.at[part], held.at[part], sem.at[b]).wait()


def totals_kernel(rows_in, cols_in, counts, panel_in, words_all, band, base, cleared,
                  brought, panel, held, rows, cols, wacc, contexts, context_log, wrecv, crecv, mine, qrecv,
                  cs, wss, wrs, css, crs, qss, qrs, ass, ars, pss, prs, lsem):
    x, yl = lax.axis_index("x"), lax.axis_index("yl")
    z, yh, c = lax.axis_index("z"), lax.axis_index("yh"), lax.axis_index("core")
    blocks = counts.shape[0] // GROUP
    row = yl * NX + x
    right, left = lax.rem(x + 1, NX), lax.rem(x + NX - 1, NX)
    row_peers = [
        (dx * NYL + dy, {"x": lax.rem(x + dx, NX), "yl": lax.rem(yl + dy, NYL)})
        for dx in range(NX) for dy in range(NYL) if dx or dy
    ]
    z_peers = [(dz, lax.rem(z + dz, NZ)) for dz in (4, 3, 5, 2, 6, 1, 7)]
    quad = [
        (dy * NC + dc, {"yh": lax.rem(yh + dy, NYH), "core": lax.rem(c + dc, NC)})
        for dy, dc in ((1, 0), (1, 1), (0, 1))
    ]
    everybody = [d for _, d in row_peers] + [{"z": p} for _, p in z_peers] + [d for _, d in quad]
    slots = [
        pltpu.make_async_copy(rows_in, rows, lsem.at[1]),
        pltpu.make_async_copy(cols_in, cols, lsem.at[2]),
    ]
    bring = pltpu.make_async_copy(panel_in, brought, lsem.at[3])
    hail(everybody)
    for copy in (bring, *slots):
        copy.start()
    load_counts(counts, held, cs)

    wacc[...] = jnp.zeros_like(wacc)
    lanes = lax.broadcasted_iota(I32, (T, T), 1)
    bands = lax.broadcasted_iota(I32, (COL_TILES, T), 0)
    ones = jnp.ones((2 * T, T), BF16)
    for copy in slots:
        copy.wait()

    def some(b, per_context):
        await_counts(counts, held, cs, b)
        per_word = wacc[...]
        for g in range(GROUP):
            slot = b * GROUP + g
            value = held[slot]
            per_context = per_context + jnp.where(
                bands == cols[slot], jnp.sum(value, axis=0, keepdims=True), 0
            )
            if g % 4 == 3:
                eights = jnp.bitwise_and(value, -8)
                parts = [a.astype(F32).astype(BF16) for a in (eights, value - eights)]
                sums = jnp.dot(jnp.concatenate(parts, axis=1), ones, preferred_element_type=F32)
            else:
                sums = jnp.sum(value.astype(F32), axis=1, keepdims=True)
            per_word = per_word + jnp.where(lanes == rows[slot], sums, 0.0)
        wacc[...] = per_word
        return per_context

    per_context = lax.fori_loop(0, blocks, some, jnp.zeros((COL_TILES, T), I32))
    contexts[...] = per_context.astype(F32)
    await_hails(everybody)

    csends = [remote(contexts, crecv.at[k], css.at[k], crs.at[k], d) for k, d in row_peers]
    for copy in csends:
        copy.start()
    wsends = [
        remote(wacc.at[pl.ds(pl.multiple_of(p * PART, PART), PART)], wrecv.at[k], wss.at[k], wrs.at[k], {"z": p})
        for k, p in z_peers
    ]
    for copy in wsends:
        copy.start()

    bring.wait()
    for t in range(4):
        tile = pl.ds(t * T, T)
        panel[tile, :] = brought[tile, :].astype(F32).T.astype(BF16)
    own = pltpu.make_async_copy(panel, band.at[row], lsem.at[0])
    own.start()

    psends = []

    def pass_on(src, dst, device):
        k = len(psends)
        psends.append(remote(src, dst, pss.at[k], prs.at[k], device))
        psends[k].start()

    def to_right_and_left(first, second):
        pass_on(first, first, {"x": right})
        pass_on(second, second, {"x": left})

    def relay(y):
        to_right_and_left(
            band.at[y * NX + left, pl.ds(0, HALF)], band.at[y * NX + right, pl.ds(HALF, HALF)]
        )

    pass_on(panel, band.at[row], {"yl": 1 - yl})
    pass_on(panel, band.at[row], {"x": right})
    pass_on(panel, band.at[row], {"x": left})

    def clear(t, carry):
        cleared[t] = jnp.zeros((T, T), F32)
        return carry

    lax.fori_loop(0, ROW_TILES, clear, 0, unroll=4)
    for copy in csends:
        copy.wait_recv()
    contexts_sum = contexts[...]
    for k, _ in row_peers:
        contexts_sum = contexts_sum + crecv[k]
    powers = powers_of(contexts_sum)
    band_power = jnp.sum(powers, keepdims=True)
    context_log[...] = jnp.log(jnp.maximum(powers, 1.0))

    for copy in wsends:
        copy.wait_recv()
    words_sum = wacc[pl.ds(pl.multiple_of(z * PART, PART), PART), :]
    for k, _ in z_peers:
        words_sum = words_sum + wrecv[k]
    mine[pl.ds(0, PART), :] = words_sum
    mine[pl.ds(PART, 8), :] = jnp.broadcast_to(band_power, (8, T))
    qsends = [remote(mine, qrecv.at[k], qss.at[k], qrs.at[k], d) for k, d in quad]
    for copy in qsends:
        copy.start()

    def logs(b, carry):
        for g in range(GROUP):
            slot = b * GROUP + g
            value = held[slot].astype(F32)
            term = jnp.where(
                value > 0.0, jnp.log(value) - context_log[pl.ds(cols[slot], 1), :], -1e30
            )
            base[slot] = term.T
        return carry

    for copy in psends[0:3]:
        copy.wait_recv()
    there = band.at[(1 - yl) * NX + x]
    to_right_and_left(there, there)
    relay(yl)

    lax.fori_loop(0, blocks // 2, logs, 0)
    for copy in qsends:
        copy.wait_recv()
    total = mine[...]
    for k, _ in quad:
        total = total + qrecv[k]
    words_all[z] = total
    asends = [
        remote(words_all.at[z], words_all.at[z], ass.at[k], ars.at[k], {"z": p}) for k, p in z_peers
    ]
    for copy in asends:
        copy.start()

    for copy in psends[3:5]:
        copy.wait_recv()
    relay(1 - yl)
    lax.fori_loop(blocks // 2, blocks, logs, 0)

    for copy in asends:
        copy.wait()
    for copy in csends + wsends + qsends + psends[0:5]:
        copy.wait_send()
    for copy in psends[5:9]:
        copy.wait()
    own.wait()


def totals(rows, cols, counts, panel):
    slots = counts.shape[0]
    return pl.pallas_call(
        totals_kernel,
        in_specs=[ANY, ANY, ANY, ANY],
        out_specs=[VMEM, ANY, VMEM, VMEM],
        out_shape=[
            jax.ShapeDtypeStruct((NZ, PART + 8, T), F32),
            jax.ShapeDtypeStruct((N_ROW, SHARE, T), BF16),
            jax.ShapeDtypeStruct((slots, T, T), F32),
            jax.ShapeDtypeStruct((ROW_TILES, T, T), F32),
        ],
        scratch_shapes=[
            pltpu.VMEM((SHARE, T), BF16),
            pltpu.VMEM((SHARE, T), BF16),
            pltpu.VMEM((slots, T, T), I32),
            pltpu.SMEM((slots,), I32),
            pltpu.SMEM((slots,), I32),
            pltpu.VMEM((T, ROW_TILES), F32),
            pltpu.VMEM((COL_TILES, T), F32),
            pltpu.VMEM((COL_TILES, T), F32),
            pltpu.VMEM((NZ, PART, T), F32),
            pltpu.VMEM((N_ROW, COL_TILES, T), F32),
            pltpu.VMEM((PART + 8, T), F32),
            pltpu.VMEM((NYH * NC, PART + 8, T), F32),
            DMA((slots // GROUP,)),
            DMA((NZ,)), DMA((NZ,)), DMA((N_ROW,)), DMA((N_ROW,)), DMA((NYH * NC,)), DMA((NYH * NC,)),
            DMA((NZ,)), DMA((NZ,)), DMA((9,)), DMA((9,)), DMA((4,)),
        ],
        compiler_params=pltpu.CompilerParams(collective_id=0, has_side_effects=True, vmem_limit_bytes=16 << 20),
        name="totals",
    )(rows, cols, counts, panel)


def word_kernel(rows, cols, base, words_all, band, cleared, tiles, partial, words, word_term):
    power = jnp.zeros((1, T), F32)
    for d in range(NZ):
        words[pl.ds(d * PART, PART), :] = words_all[d, 0:PART, :]
        power = power + words_all[d, PART : PART + 1, :]
    log_scale = jnp.log(power) - math.log(NEG_SAMPLES)
    word_term[...] = (log_scale - jnp.log(jnp.maximum(words[...], 1.0))).T

    def some(b, carry):
        for g in range(GROUP):
            slot = b * GROUP + g
            row, col = rows[slot], cols[slot]
            tile = jnp.maximum(base[slot] + word_term[pl.ds(row, 1), :], 0.0).astype(BF16)
            tiles[slot] = tile
            partial[row] += jnp.dot(band[col], tile, preferred_element_type=F32)
        return carry

    lax.fori_loop(0, base.shape[0] // GROUP, some, 0)


def word_products(rows, cols, base, words_all, band, cleared):
    slots = base.shape[0]
    return pl.pallas_call(
        word_kernel,
        in_specs=[SMEM, SMEM, VMEM, VMEM, VMEM, VMEM],
        out_specs=[VMEM, VMEM],
        scratch_shapes=[pltpu.VMEM((T, ROW_TILES), F32), pltpu.VMEM((ROW_TILES, T), F32)],
        out_shape=[
            jax.ShapeDtypeStruct((slots, T, T), BF16),
            jax.ShapeDtypeStruct((ROW_TILES, T, T), F32),
        ],
        input_output_aliases={5: 1},
        compiler_params=pltpu.CompilerParams(vmem_limit_bytes=28 << 20),
        name="word_products",
    )(rows, cols, base, words_all, band, cleared)


AWAY = (0, 1, 0)

Z_STEPS = (
    (0, 0, 0), (0, 1, 1), 4, 3, 5,
    (1, 1, 0), (1, 0, 1), (1, 0, 0), (1, 1, 1), (0, 0, 2), 2, 6,
    (2, 1, 0), (2, 0, 1), (2, 0, 0), (2, 1, 1), (1, 1, 2), (1, 0, 2), 1, 7,
    (3, 1, 0), (3, 0, 1), (3, 0, 0), (3, 1, 1), 0, (2, 1, 2), (2, 0, 2), None,
    (3, 1, 2), (3, 0, 2),
)
X_STEPS = (
    2, (0, 0, 0), (0, 1, 1), 1, 3,
    (1, 1, 0), (1, 0, 1), (0, 0, 2), (1, 0, 0), (1, 1, 1), 0, None,
    (1, 1, 2), (1, 0, 2),
)


def ring_sum(steps, length, y, raw, ready, ways, other_y, use, sendb, recvb,
             ysendb, yrecvb, ss, rs, yss, yrs):
    trades, sends, traded = {}, {}, set()
    last, end = length - 1, 2 * length

    def exchange(value, k):
        encode(value, ysendb.at[k])
        trades[k] = remote(ysendb.at[k], yrecvb.at[k], yss.at[k], yrs.at[k], other_y)
        trades[k].start()

    def term(d, lane):
        ready(d, lane // 2)
        if lane < 2:
            return raw(d, lane, 0)
        if d not in traded:
            trades[d].wait_recv()
            traded.add(d)
        return raw(d, y, 1) + decode(yrecvb.at[d])

    def arrived(h):
        value = raw(0, h, 0)
        for way in range(2):
            first, second = sends[last, way, 0][0], sends[last, way, 1][0]
            value = value + decode(recvb.at[first + h * (second - first)])
        return value

    for step in steps:
        if step is None:
            for lane in (0, 1):
                for way in range(2):
                    sends[last, way, lane][1].wait_recv()
            ready(0, 0)
            exchange(arrived(1 - y), end)
        elif isinstance(step, int):
            ready(step, 1)
            exchange(raw(step, 1 - y, 1), step)
        else:
            s, way, lane = step
            value = term(length - s if way == 0 else length + s, lane)
            if (s - 1, way, lane) in sends:
                index, before = sends[s - 1, way, lane]
                before.wait_recv()
                value = value + decode(recvb.at[index])
            n = len(sends)
            encode(value, sendb.at[n])
            copy = remote(sendb.at[n], recvb.at[n], ss.at[n], rs.at[n], ways[way])
            copy.start()
            sends[step] = (n, copy)

    first = arrived(y)
    trades[end].wait_recv()
    use(0, first + decode(yrecvb.at[end]))
    second = term(0, 2)
    for way in range(2):
        index, copy = sends[last, way, 2]
        copy.wait_recv()
        second = second + decode(recvb.at[index])
    use(1, second)

    def drain():
        for _, copy in sends.values():
            copy.wait_send()
        for copy in trades.values():
            copy.wait_send()

    return drain


def ring_scratch(steps, length):
    n, y = sum(isinstance(step, tuple) for step in steps), 2 * length + 1
    return [
        pltpu.VMEM((n, CODE, T), I16), pltpu.VMEM((n, CODE, T), I16),
        pltpu.VMEM((y, CODE, T), I16), pltpu.VMEM((y, CODE, T), I16),
        DMA((n,)), DMA((n,)), DMA((y,)), DMA((y,)),
    ]


def word_panel_kernel(partial, share, everyone, sib, mine, xss, xrs, gss, grs, hss, hrs, pss, prs, ms,
                      *ring):
    z, yh, c = lax.axis_index("z"), lax.axis_index("yh"), lax.axis_index("core")
    ways = ({"z": lax.rem(z + 1, NZ)}, {"z": lax.rem(z + NZ - 1, NZ)})
    other_y, other_core = {"yh": 1 - yh}, {"core": 1 - c}
    length = NZ // 2

    greet([*ways, other_y, other_core])
    swaps, here = {}, set()
    for dz in (4, 3, 5, 2, 6, 1, 7, 0):
        for part in range(2):
            for h in range(2):
                k, rows = (dz * 2 + h) * 2 + part, pl.ds(part * HALF, HALF)
                swaps[dz, h, part] = remote(
                    partial.at[lax.rem(z + dz, NZ), h, 1 - c, rows], sib.at[dz * 2 + h, rows],
                    xss.at[k], xrs.at[k], other_core,
                )
                swaps[dz, h, part].start()

    def ready(d, part):
        if (d, part) not in here:
            here.add((d, part))
            for h in range(2):
                swaps[d, h, part].wait_recv()

    def raw(d, h, part):
        rows = pl.ds(part * HALF, HALF)
        return partial[lax.rem(z + d, NZ), h, c, rows, :] + sib[d * 2 + h, rows, :]

    pair = (pl.ds(0, 2), pl.ds(2, 2))

    def place(d, h, part):
        return everyone.at[lax.rem(z + d, NZ), h, c, pair[part]]

    gives, hands, passes, keeps = {}, [], {}, []

    def hand(src, dst, k):
        copy = remote(src, dst, hss.at[k], hrs.at[k], other_core)
        copy.start()
        hands.append(copy)

    def along_y(src, dst, k):
        passes[k] = remote(src, dst, pss.at[k], prs.at[k], other_y)
        passes[k].start()

    def lane_place(d, lane):
        return place(d, 1 - yh if lane == 1 else yh, 1 if lane == 2 else 0)

    def give(s, way, lane, src=None):
        dst = lane_place((NZ - s) % NZ if way == 0 else s, lane)
        k = (s * 2 + way) * 3 + lane
        gives[s, way, lane] = remote(dst if src is None else src, dst, gss.at[k], grs.at[k], ways[way])
        gives[s, way, lane].start()

    own = (mine.at[pair[0]], mine.at[pair[1]])

    def use(part, total):
        straight = [total[t * T : (t + 1) * T].T for t in range(2)]
        for t in range(2):
            mine[part * 2 + t] = straight[t].astype(BF16)
        along_y(own[part], place(0, yh, part), 0 if part else NZ)
        for way in range(2):
            give(0, way, 2 if part else 0, own[part])
        hand(own[part], place(0, yh, part), 2 * NZ if part else 0)
        keeps.append(pltpu.make_async_copy(own[part], place(0, yh, part), ms.at[part]))
        keeps[-1].start()
        for t in range(2):
            share[pl.ds(part * HALF + t * T, T), :] = straight[t]

    drain = ring_sum(Z_STEPS, length, yh, raw, ready, ways, other_y, use, *ring)
    passes[NZ].wait_recv()
    for way in range(2):
        give(0, way, 1)
    hand(lane_place(0, 1), lane_place(0, 1), 1)
    due = [0]
    for s in range(1, length + 1):
        came = []
        for lane in (0, 2, 1) if s == 1 else (2, 0, 1):
            for way in range(2):
                if (s - 1, way, lane) not in gives:
                    continue
                gives[s - 1, way, lane].wait_recv()
                if s < length - 1 or (s == length - 1 and way == AWAY[lane]):
                    give(s, way, lane)
                d = (NZ - s) % NZ if way == 0 else s
                at = lane_place(d, lane)
                if lane == 2:
                    along_y(at, at, d)
                    came.append(d)
                hand(at, at, 2 * NZ + d if lane == 2 else d * 2 + lane)
        for d in due:
            passes[d].wait_recv()
            hand(place(d, 1 - yh, 1), place(d, 1 - yh, 1), 3 * NZ + d)
        due = came
    for d in due:
        passes[d].wait_recv()
        hand(place(d, 1 - yh, 1), place(d, 1 - yh, 1), 3 * NZ + d)

    for copy in hands:
        copy.wait()
    for copy in list(gives.values()) + list(passes.values()) + list(swaps.values()):
        copy.wait_send()
    drain()
    for copy in keeps:
        copy.wait()


def word_panel_sum(partial):
    return pl.pallas_call(
        word_panel_kernel,
        in_specs=[VMEM],
        out_specs=[VMEM, ANY],
        out_shape=[
            jax.ShapeDtypeStruct((SHARE, T), F32),
            jax.ShapeDtypeStruct((NZ, NYH, NC, 4, T, T), BF16),
        ],
        scratch_shapes=[
            pltpu.VMEM((2 * NZ, SHARE, T), F32),
            pltpu.VMEM((4, T, T), BF16),
            DMA((4 * NZ,)), DMA((4 * NZ,)), DMA((3 * NZ,)), DMA((3 * NZ,)),
            DMA((4 * NZ,)), DMA((4 * NZ,)), DMA((NZ + 1,)), DMA((NZ + 1,)), DMA((2,)),
            *ring_scratch(Z_STEPS, NZ // 2),
        ],
        compiler_params=pltpu.CompilerParams(collective_id=1, has_side_effects=True, vmem_limit_bytes=16 << 20),
        name="word_panel_sum",
    )(partial)


def context_kernel(rows, cols, tiles, rounded, share, partial, share_out):
    share_out[...] = share[...]
    partial[...] = jnp.zeros_like(partial)

    def some(b, carry):
        for g in range(GROUP):
            slot = b * GROUP + g
            partial[cols[slot]] += jnp.dot(tiles[slot], rounded[rows[slot]], preferred_element_type=F32)
        return carry

    lax.fori_loop(0, tiles.shape[0] // GROUP, some, 0)


def context_products(rows, cols, tiles, rounded, share):
    slots = tiles.shape[0]
    return pl.pallas_call(
        context_kernel,
        in_specs=[SMEM, SMEM, VMEM, VMEM, VMEM],
        out_specs=[VMEM, VMEM],
        out_shape=[
            jax.ShapeDtypeStruct((COL_TILES, T, T), F32),
            jax.ShapeDtypeStruct((SHARE, T), F32),
        ],
        compiler_params=pltpu.CompilerParams(vmem_limit_bytes=16 << 20),
        name="context_products",
    )(rows, cols, tiles, rounded, share)


def context_panel_kernel(partial, share, *ring):
    x, yl = lax.axis_index("x"), lax.axis_index("yl")
    ways = ({"x": lax.rem(x + 1, NX)}, {"x": lax.rem(x + NX - 1, NX)})
    other_y = {"yl": 1 - yl}
    greet([*ways, other_y])

    def raw(d, h, part):
        return partial[h, lax.rem(x + d, NX), pl.ds(part * HALF, HALF), :]

    def use(part, total):
        share[pl.ds(part * HALF, HALF), :] = total * (1.0 / T)

    ring_sum(X_STEPS, NX // 2, yl, raw, lambda d, part: None, ways, other_y, use, *ring)()


def context_panel_sum(partial):
    return pl.pallas_call(
        context_panel_kernel,
        in_specs=[VMEM],
        out_specs=VMEM,
        out_shape=jax.ShapeDtypeStruct((SHARE, T), F32),
        scratch_shapes=ring_scratch(X_STEPS, NX // 2),
        compiler_params=pltpu.CompilerParams(collective_id=2, has_side_effects=True, vmem_limit_bytes=8 << 20),
        name="context_panel_sum",
    )(partial)


def shards(tile_counts, tile_rows, tile_cols, panel):
    counts, rows, cols = tile_counts[0, 0], tile_rows[0, 0], tile_cols[0, 0]
    far = [pltpu.with_memory_space_constraint(a, pltpu.HBM) for a in (rows, cols, counts, panel)]
    words_all, band, base, cleared = totals(*far)
    band = band.reshape(COL_TILES, T, T)
    tiles, partial = word_products(rows, cols, base, words_all, band, cleared)
    share, everyone = word_panel_sum(partial.reshape(NZ, NYH, NC, SHARE, T))
    rounded = everyone.reshape(ROW_TILES, T, T)
    context_partial, share = context_products(rows, cols, tiles, rounded, share)
    context_share = context_panel_sum(context_partial.reshape(NYL, NX, SHARE, T))
    return share, context_share


def solution(mesh):
    split = Mesh(
        mesh.devices.reshape(NYL, NX, NZ, NYH, NC), ("yl", "x", "z", "yh", "core")
    )
    row, col = ("yl", "x"), ("z", "yh", "core")
    in_specs = (
        P(row, col, None, None, None),
        P(row, col, None),
        P(row, col, None),
        P(col + row, None),
    )
    out_specs = (P(row + col, None), P(col + row, None))
    return jax.shard_map(shards, mesh=split, in_specs=in_specs, out_specs=out_specs, check_vma=False)
```

```python
import functools
import math

import jax
import jax.numpy as jnp
from jax import lax
from jax.experimental import pallas as pl
from jax.experimental.pallas import tpu as pltpu
from jax.sharding import Mesh
from jax.sharding import PartitionSpec as P

NEG_SAMPLES = 15
T = 128
NX, NYL, NYH, NZ, NC = 4, 2, 2, 8, 2
N_ROW, N_COL = NX * NYL, NZ * NYH * NC
ROW_TILES, COL_TILES = 128, 32
SHARE = 512
HALF = SHARE // 2
CODE = HALF + 16
MESH = pl.DeviceIdType.MESH
F32, BF16, I32, I16 = jnp.float32, jnp.bfloat16, jnp.int32, jnp.int16
ANY = pl.BlockSpec(memory_space=pl.ANY)
VMEM = pl.BlockSpec(memory_space=pltpu.VMEM)
SMEM = pl.BlockSpec(memory_space=pltpu.SMEM)
DMA = pltpu.SemaphoreType.DMA
LN2 = math.log(2.0)


def remote(src, dst, ssem, rsem, device):
    return pltpu.make_async_remote_copy(
        src_ref=src, dst_ref=dst, send_sem=ssem, recv_sem=rsem,
        device_id=device, device_id_type=MESH,
    )


def hail(devices):
    for device in devices:
        pl.semaphore_signal(
            pltpu.get_barrier_semaphore(), inc=1, device_id=device, device_id_type=MESH
        )


def await_hails(devices):
    pl.semaphore_wait(pltpu.get_barrier_semaphore(), len(devices))


def greet(devices):
    hail(devices)
    await_hails(devices)


def encode(value, ref):
    top = jnp.max(jnp.abs(value), axis=0, keepdims=True)
    expo = jnp.ceil(jnp.log(jnp.maximum(top, 1e-30)) * (1.0 / LN2) + 0.001) - 14.0
    scaled = jnp.round(value * jnp.exp(expo * -LN2))
    ref[pl.ds(0, HALF), :] = scaled.astype(I32).astype(I16)
    ref[pl.ds(HALF, 16), :] = jnp.broadcast_to(expo, (16, T)).astype(I32).astype(I16)


def decode(ref):
    expo = ref[pl.ds(HALF, 16), :].astype(I32).astype(F32)[0:1]
    return ref[pl.ds(0, HALF), :].astype(I32).astype(F32) * jnp.exp(expo * LN2)


GROUP = 16
PART = T // NZ


def powers_of(totals):
    root = jnp.sqrt(totals)
    return root * jnp.sqrt(root)


def load_counts(counts, held, sem):
    copies = []
    for b in range(counts.shape[0] // GROUP):
        part = pl.ds(b * GROUP, GROUP)
        copies.append(pltpu.make_async_copy(counts.at[part], held.at[part], sem.at[b]))
        copies[-1].start()
    return copies


def await_counts(counts, held, sem, b):
    part = pl.ds(b * GROUP, GROUP)
    pltpu.make_async_copy(counts.at[part], held.at[part], sem.at[b]).wait()


def totals_kernel(rows_in, cols_in, counts, panel_in, words_all, band, base, cleared,
                  brought, panel, held, rows, cols, wacc, contexts, context_log, wrecv, crecv, mine, qrecv,
                  cs, wss, wrs, css, crs, qss, qrs, ass, ars, pss, prs, lsem):
    x, yl = lax.axis_index("x"), lax.axis_index("yl")
    z, yh, c = lax.axis_index("z"), lax.axis_index("yh"), lax.axis_index("core")
    blocks = counts.shape[0] // GROUP
    row = yl * NX + x
    right, left = lax.rem(x + 1, NX), lax.rem(x + NX - 1, NX)
    row_peers = [
        (dx * NYL + dy, {"x": lax.rem(x + dx, NX), "yl": lax.rem(yl + dy, NYL)})
        for dx in range(NX) for dy in range(NYL) if dx or dy
    ]
    z_peers = [(dz, lax.rem(z + dz, NZ)) for dz in (4, 3, 5, 2, 6, 1, 7)]
    quad = [
        (dy * NC + dc, {"yh": lax.rem(yh + dy, NYH), "core": lax.rem(c + dc, NC)})
        for dy, dc in ((1, 0), (1, 1), (0, 1))
    ]
    everybody = [d for _, d in row_peers] + [{"z": p} for _, p in z_peers] + [d for _, d in quad]
    slots = [
        pltpu.make_async_copy(rows_in, rows, lsem.at[1]),
        pltpu.make_async_copy(cols_in, cols, lsem.at[2]),
    ]
    bring = pltpu.make_async_copy(panel_in, brought, lsem.at[3])
    hail(everybody)
    for copy in (bring, *slots):
        copy.start()
    load_counts(counts, held, cs)

    wacc[...] = jnp.zeros_like(wacc)
    lanes = lax.broadcasted_iota(I32, (T, T), 1)
    bands = lax.broadcasted_iota(I32, (COL_TILES, T), 0)
    ones = jnp.ones((2 * T, T), BF16)
    for copy in slots:
        copy.wait()

    def some(b, per_context):
        await_counts(counts, held, cs, b)
        per_word = wacc[...]
        for g in range(GROUP):
            slot = b * GROUP + g
            value = held[slot]
            per_context = per_context + jnp.where(
                bands == cols[slot], jnp.sum(value, axis=0, keepdims=True), 0
            )
            if g % 4 == 3:
                eights = jnp.bitwise_and(value, -8)
                parts = [a.astype(F32).astype(BF16) for a in (eights, value - eights)]
                sums = jnp.dot(jnp.concatenate(parts, axis=1), ones, preferred_element_type=F32)
            else:
                sums = jnp.sum(value.astype(F32), axis=1, keepdims=True)
            per_word = per_word + jnp.where(lanes == rows[slot], sums, 0.0)
        wacc[...] = per_word
        return per_context

    per_context = lax.fori_loop(0, blocks, some, jnp.zeros((COL_TILES, T), I32))
    contexts[...] = per_context.astype(F32)
    await_hails(everybody)

    csends = [remote(contexts, crecv.at[k], css.at[k], crs.at[k], d) for k, d in row_peers]
    for copy in csends:
        copy.start()
    wsends = [
        remote(wacc.at[pl.ds(pl.multiple_of(p * PART, PART), PART)], wrecv.at[k], wss.at[k], wrs.at[k], {"z": p})
        for k, p in z_peers
    ]
    for copy in wsends:
        copy.start()

    bring.wait()
    for t in range(4):
        tile = pl.ds(t * T, T)
        panel[tile, :] = brought[tile, :].astype(F32).T.astype(BF16)
    own = pltpu.make_async_copy(panel, band.at[row], lsem.at[0])
    own.start()

    psends = []

    def pass_on(src, dst, device):
        k = len(psends)
        psends.append(remote(src, dst, pss.at[k], prs.at[k], device))
        psends[k].start()

    def to_right_and_left(first, second):
        pass_on(first, first, {"x": right})
        pass_on(second, second, {"x": left})

    def relay(y):
        to_right_and_left(
            band.at[y * NX + left, pl.ds(0, HALF)], band.at[y * NX + right, pl.ds(HALF, HALF)]
        )

    pass_on(panel, band.at[row], {"yl": 1 - yl})
    pass_on(panel, band.at[row], {"x": right})
    pass_on(panel, band.at[row], {"x": left})

    def clear(t, carry):
        cleared[t] = jnp.zeros((T, T), F32)
        return carry

    lax.fori_loop(0, ROW_TILES, clear, 0, unroll=4)
    for copy in csends:
        copy.wait_recv()
    contexts_sum = contexts[...]
    for k, _ in row_peers:
        contexts_sum = contexts_sum + crecv[k]
    powers = powers_of(contexts_sum)
    band_power = jnp.sum(powers, keepdims=True)
    context_log[...] = jnp.log(jnp.maximum(powers, 1.0))

    for copy in wsends:
        copy.wait_recv()
    words_sum = wacc[pl.ds(pl.multiple_of(z * PART, PART), PART), :]
    for k, _ in z_peers:
        words_sum = words_sum + wrecv[k]
    mine[pl.ds(0, PART), :] = words_sum
    mine[pl.ds(PART, 8), :] = jnp.broadcast_to(band_power, (8, T))
    qsends = [remote(mine, qrecv.at[k], qss.at[k], qrs.at[k], d) for k, d in quad]
    for copy in qsends:
        copy.start()

    def logs(b, carry):
        for g in range(GROUP):
            slot = b * GROUP + g
            value = held[slot].astype(F32)
            term = jnp.where(
                value > 0.0, jnp.log(value) - context_log[pl.ds(cols[slot], 1), :], -1e30
            )
            base[slot] = term.T
        return carry

    for copy in psends[0:3]:
        copy.wait_recv()
    there = band.at[(1 - yl) * NX + x]
    to_right_and_left(there, there)
    relay(yl)

    lax.fori_loop(0, blocks // 2, logs, 0)
    for copy in qsends:
        copy.wait_recv()
    total = mine[...]
    for k, _ in quad:
        total = total + qrecv[k]
    words_all[z] = total
    asends = [
        remote(words_all.at[z], words_all.at[z], ass.at[k], ars.at[k], {"z": p}) for k, p in z_peers
    ]
    for copy in asends:
        copy.start()

    for copy in psends[3:5]:
        copy.wait_recv()
    relay(1 - yl)
    lax.fori_loop(blocks // 2, blocks, logs, 0)

    for copy in asends:
        copy.wait()
    for copy in csends + wsends + qsends + psends[0:5]:
        copy.wait_send()
    for copy in psends[5:9]:
        copy.wait()
    own.wait()


def totals(rows, cols, counts, panel):
    slots = counts.shape[0]
    return pl.pallas_call(
        totals_kernel,
        in_specs=[ANY, ANY, ANY, ANY],
        out_specs=[VMEM, ANY, VMEM, VMEM],
        out_shape=[
            jax.ShapeDtypeStruct((NZ, PART + 8, T), F32),
            jax.ShapeDtypeStruct((N_ROW, SHARE, T), BF16),
            jax.ShapeDtypeStruct((slots, T, T), F32),
            jax.ShapeDtypeStruct((ROW_TILES, T, T), F32),
        ],
        scratch_shapes=[
            pltpu.VMEM((SHARE, T), BF16),
            pltpu.VMEM((SHARE, T), BF16),
            pltpu.VMEM((slots, T, T), I32),
            pltpu.SMEM((slots,), I32),
            pltpu.SMEM((slots,), I32),
            pltpu.VMEM((T, ROW_TILES), F32),
            pltpu.VMEM((COL_TILES, T), F32),
            pltpu.VMEM((COL_TILES, T), F32),
            pltpu.VMEM((NZ, PART, T), F32),
            pltpu.VMEM((N_ROW, COL_TILES, T), F32),
            pltpu.VMEM((PART + 8, T), F32),
            pltpu.VMEM((NYH * NC, PART + 8, T), F32),
            DMA((slots // GROUP,)),
            DMA((NZ,)), DMA((NZ,)), DMA((N_ROW,)), DMA((N_ROW,)), DMA((NYH * NC,)), DMA((NYH * NC,)),
            DMA((NZ,)), DMA((NZ,)), DMA((9,)), DMA((9,)), DMA((4,)),
        ],
        compiler_params=pltpu.CompilerParams(collective_id=0, has_side_effects=True, vmem_limit_bytes=16 << 20),
        name="totals",
    )(rows, cols, counts, panel)


def word_kernel(rows, cols, base, words_all, band, cleared, tiles, partial, words, word_term):
    power = jnp.zeros((1, T), F32)
    for d in range(NZ):
        words[pl.ds(d * PART, PART), :] = words_all[d, 0:PART, :]
        power = power + words_all[d, PART : PART + 1, :]
    log_scale = jnp.log(power) - math.log(NEG_SAMPLES)
    word_term[...] = (log_scale - jnp.log(jnp.maximum(words[...], 1.0))).T

    def some(b, carry):
        for g in range(GROUP):
            slot = b * GROUP + g
            row, col = rows[slot], cols[slot]
            tile = jnp.maximum(base[slot] + word_term[pl.ds(row, 1), :], 0.0).astype(BF16)
            tiles[slot] = tile
            partial[row] += jnp.dot(band[col], tile, preferred_element_type=F32)
        return carry

    lax.fori_loop(0, base.shape[0] // GROUP, some, 0)


def word_products(rows, cols, base, words_all, band, cleared):
    slots = base.shape[0]
    return pl.pallas_call(
        word_kernel,
        in_specs=[SMEM, SMEM, VMEM, VMEM, VMEM, VMEM],
        out_specs=[VMEM, VMEM],
        scratch_shapes=[pltpu.VMEM((T, ROW_TILES), F32), pltpu.VMEM((ROW_TILES, T), F32)],
        out_shape=[
            jax.ShapeDtypeStruct((slots, T, T), BF16),
            jax.ShapeDtypeStruct((ROW_TILES, T, T), F32),
        ],
        input_output_aliases={5: 1},
        compiler_params=pltpu.CompilerParams(vmem_limit_bytes=28 << 20),
        name="word_products",
    )(rows, cols, base, words_all, band, cleared)


AWAY = (0, 1, 0)

ACROSS = (0, 2, 2)

Z_STEPS = (
    (0, 0, 0), (0, 1, 1), 4, 3, 5,
    (1, 1, 0), (1, 0, 1), (1, 0, 0), (1, 1, 1), (0, 0, 2), 2, 6,
    (2, 1, 0), (2, 0, 1), (2, 0, 0), (2, 1, 1), (1, 1, 2), (1, 0, 2), 1, 7,
    (3, 1, 0), (3, 0, 1), (3, 0, 0), (3, 1, 1), 0, (2, 1, 2), (2, 0, 2), None,
    (3, 1, 2), (3, 0, 2),
)
X_STEPS = (
    2, (0, 0, 0), (0, 1, 1), 1, 3,
    (1, 1, 0), (1, 0, 1), (1, 0, 0), (1, 1, 1), ACROSS, 0,
    (1, 0, 2), (1, 1, 2), None,
)


def ring_sum(steps, length, y, raw, ready, ways, other_y, use, sendb, recvb,
             ysendb, yrecvb, ss, rs, yss, yrs):
    trades, sends, traded = {}, {}, set()
    last, end = length - 1, 2 * length

    def exchange(value, k):
        encode(value, ysendb.at[k])
        trades[k] = remote(ysendb.at[k], yrecvb.at[k], yss.at[k], yrs.at[k], other_y)
        trades[k].start()

    def term(d, lane):
        ready(d, lane // 2)
        if lane < 2:
            return raw(d, lane, 0)
        if d not in traded:
            trades[d].wait_recv()
            traded.add(d)
        return raw(d, y, 1) + decode(yrecvb.at[d])

    def arrived(h):
        value = raw(0, h, 0)
        for way in range(2):
            first, second = sends[last, way, 0][0], sends[last, way, 1][0]
            value = value + decode(recvb.at[first + h * (second - first)])
        return value

    for step in steps:
        if step is None:
            for lane in (0, 1):
                for way in range(2):
                    sends[last, way, lane][1].wait_recv()
            ready(0, 0)
            exchange(arrived(1 - y), end)
        elif isinstance(step, int):
            ready(step, 1)
            exchange(raw(step, 1 - y, 1), step)
        else:
            s, way, lane = step
            value = term(length + s if way == 1 else length - s, lane)
            if (s - 1, way, lane) in sends:
                index, before = sends[s - 1, way, lane]
                before.wait_recv()
                value = value + decode(recvb.at[index])
            n = len(sends)
            encode(value, sendb.at[n])
            copy = remote(sendb.at[n], recvb.at[n], ss.at[n], rs.at[n], ways[way])
            copy.start()
            sends[step] = (n, copy)

    first = arrived(y)
    trades[end].wait_recv()
    use(0, first + decode(yrecvb.at[end]))
    second = term(0, 2)
    for step in ((last, 0, 2), (last, 1, 2), ACROSS):
        if step in sends:
            index, copy = sends[step]
            copy.wait_recv()
            second = second + decode(recvb.at[index])
    use(1, second)

    def drain():
        for _, copy in sends.values():
            copy.wait_send()
        for copy in trades.values():
            copy.wait_send()

    return drain


def ring_scratch(steps, length):
    n, y = sum(isinstance(step, tuple) for step in steps), 2 * length + 1
    return [
        pltpu.VMEM((n, CODE, T), I16), pltpu.VMEM((n, CODE, T), I16),
        pltpu.VMEM((y, CODE, T), I16), pltpu.VMEM((y, CODE, T), I16),
        DMA((n,)), DMA((n,)), DMA((y,)), DMA((y,)),
    ]


def word_panel_kernel(partial, share, everyone, cleared, sib, mine, xss, xrs, gss, grs, hss, hrs, pss, prs, ms,
                      *ring):
    z, yh, c = lax.axis_index("z"), lax.axis_index("yh"), lax.axis_index("core")
    ways = ({"z": lax.rem(z + 1, NZ)}, {"z": lax.rem(z + NZ - 1, NZ)})
    other_y, other_core = {"yh": 1 - yh}, {"core": 1 - c}
    length = NZ // 2

    greet([*ways, other_y, other_core])
    swaps, here = {}, set()
    for dz in (4, 3, 5, 2, 6, 1, 7, 0):
        for part in range(2):
            for h in range(2):
                k, rows = (dz * 2 + h) * 2 + part, pl.ds(part * HALF, HALF)
                swaps[dz, h, part] = remote(
                    partial.at[lax.rem(z + dz, NZ), h, 1 - c, rows], sib.at[dz * 2 + h, rows],
                    xss.at[k], xrs.at[k], other_core,
                )
                swaps[dz, h, part].start()

    def clear(t, carry):
        cleared[t] = jnp.zeros((T, T), F32)
        return carry

    lax.fori_loop(0, COL_TILES, clear, 0)

    def ready(d, part):
        if (d, part) not in here:
            here.add((d, part))
            for h in range(2):
                swaps[d, h, part].wait_recv()

    def raw(d, h, part):
        rows = pl.ds(part * HALF, HALF)
        return partial[lax.rem(z + d, NZ), h, c, rows, :] + sib[d * 2 + h, rows, :]

    pair = (pl.ds(0, 2), pl.ds(2, 2))

    def place(d, h, part):
        return everyone.at[lax.rem(z + d, NZ), h, c, pair[part]]

    gives, hands, passes, keeps = {}, [], {}, []

    def hand(src, dst, k):
        copy = remote(src, dst, hss.at[k], hrs.at[k], other_core)
        copy.start()
        hands.append(copy)

    def along_y(src, dst, k):
        passes[k] = remote(src, dst, pss.at[k], prs.at[k], other_y)
        passes[k].start()

    def lane_place(d, lane):
        return place(d, 1 - yh if lane == 1 else yh, 1 if lane == 2 else 0)

    def give(s, way, lane, src=None):
        dst = lane_place((NZ - s) % NZ if way == 0 else s, lane)
        k = (s * 2 + way) * 3 + lane
        gives[s, way, lane] = remote(dst if src is None else src, dst, gss.at[k], grs.at[k], ways[way])
        gives[s, way, lane].start()

    own = (mine.at[pair[0]], mine.at[pair[1]])

    def use(part, total):
        straight = [total[t * T : (t + 1) * T].T for t in range(2)]
        for t in range(2):
            mine[part * 2 + t] = straight[t].astype(BF16)
        along_y(own[part], place(0, yh, part), 0 if part else NZ)
        for way in range(2):
            give(0, way, 2 if part else 0, own[part])
        hand(own[part], place(0, yh, part), 2 * NZ if part else 0)
        keeps.append(pltpu.make_async_copy(own[part], place(0, yh, part), ms.at[part]))
        keeps[-1].start()
        for t in range(2):
            share[pl.ds(part * HALF + t * T, T), :] = straight[t]

    drain = ring_sum(Z_STEPS, length, yh, raw, ready, ways, other_y, use, *ring)
    passes[NZ].wait_recv()
    for way in range(2):
        give(0, way, 1)
    hand(lane_place(0, 1), lane_place(0, 1), 1)
    due = [0]
    for s in range(1, length + 1):
        came = []
        for lane in (0, 2, 1) if s == 1 else (2, 0, 1):
            for way in range(2):
                if (s - 1, way, lane) not in gives:
                    continue
                gives[s - 1, way, lane].wait_recv()
                if s < length - 1 or (s == length - 1 and way == AWAY[lane]):
                    give(s, way, lane)
                d = (NZ - s) % NZ if way == 0 else s
                at = lane_place(d, lane)
                if lane == 2:
                    along_y(at, at, d)
                    came.append(d)
                hand(at, at, 2 * NZ + d if lane == 2 else d * 2 + lane)
        for d in due:
            passes[d].wait_recv()
            hand(place(d, 1 - yh, 1), place(d, 1 - yh, 1), 3 * NZ + d)
        due = came
    for d in due:
        passes[d].wait_recv()
        hand(place(d, 1 - yh, 1), place(d, 1 - yh, 1), 3 * NZ + d)

    for copy in hands:
        copy.wait()
    for copy in list(gives.values()) + list(passes.values()) + list(swaps.values()):
        copy.wait_send()
    drain()
    for copy in keeps:
        copy.wait()


def word_panel_sum(partial):
    return pl.pallas_call(
        word_panel_kernel,
        in_specs=[VMEM],
        out_specs=[VMEM, ANY, VMEM],
        out_shape=[
            jax.ShapeDtypeStruct((SHARE, T), F32),
            jax.ShapeDtypeStruct((NZ, NYH, NC, 4, T, T), BF16),
            jax.ShapeDtypeStruct((COL_TILES, T, T), F32),
        ],
        scratch_shapes=[
            pltpu.VMEM((2 * NZ, SHARE, T), F32),
            pltpu.VMEM((4, T, T), BF16),
            DMA((4 * NZ,)), DMA((4 * NZ,)), DMA((3 * NZ,)), DMA((3 * NZ,)),
            DMA((4 * NZ,)), DMA((4 * NZ,)), DMA((NZ + 1,)), DMA((NZ + 1,)), DMA((2,)),
            *ring_scratch(Z_STEPS, NZ // 2),
        ],
        compiler_params=pltpu.CompilerParams(collective_id=1, has_side_effects=True, vmem_limit_bytes=16 << 20),
        name="word_panel_sum",
    )(partial)


def context_kernel(rows, cols, tiles, rounded, share, cleared, partial, share_out):
    share_out[...] = share[...]

    def some(b, carry):
        for g in range(GROUP):
            slot = b * GROUP + g
            partial[cols[slot]] += jnp.dot(tiles[slot], rounded[rows[slot]], preferred_element_type=F32)
        return carry

    lax.fori_loop(0, tiles.shape[0] // GROUP, some, 0)


def context_products(rows, cols, tiles, rounded, share, cleared):
    slots = tiles.shape[0]
    return pl.pallas_call(
        context_kernel,
        in_specs=[SMEM, SMEM, VMEM, VMEM, VMEM, VMEM],
        out_specs=[VMEM, VMEM],
        input_output_aliases={5: 0},
        out_shape=[
            jax.ShapeDtypeStruct((COL_TILES, T, T), F32),
            jax.ShapeDtypeStruct((SHARE, T), F32),
        ],
        compiler_params=pltpu.CompilerParams(vmem_limit_bytes=16 << 20),
        name="context_products",
    )(rows, cols, tiles, rounded, share, cleared)


def context_panel_kernel(partial, share, *ring):
    x, yl = lax.axis_index("x"), lax.axis_index("yl")
    ways = tuple({"x": lax.rem(x + d, NX)} for d in (1, NX - 1, NX // 2))
    other_y = {"yl": 1 - yl}
    greet([*ways, other_y])

    def raw(d, h, part):
        return partial[h, lax.rem(x + d, NX), pl.ds(part * HALF, HALF), :]

    def use(part, total):
        share[pl.ds(part * HALF, HALF), :] = total * (1.0 / T)

    ring_sum(X_STEPS, NX // 2, yl, raw, lambda d, part: None, ways, other_y, use, *ring)()


def context_panel_sum(partial):
    return pl.pallas_call(
        context_panel_kernel,
        in_specs=[VMEM],
        out_specs=VMEM,
        out_shape=jax.ShapeDtypeStruct((SHARE, T), F32),
        scratch_shapes=ring_scratch(X_STEPS, NX // 2),
        compiler_params=pltpu.CompilerParams(collective_id=2, has_side_effects=True, vmem_limit_bytes=8 << 20),
        name="context_panel_sum",
    )(partial)


def shards(tile_counts, tile_rows, tile_cols, panel):
    counts, rows, cols = tile_counts[0, 0], tile_rows[0, 0], tile_cols[0, 0]
    far = [pltpu.with_memory_space_constraint(a, pltpu.HBM) for a in (rows, cols, counts, panel)]
    words_all, band, base, cleared = totals(*far)
    band = band.reshape(COL_TILES, T, T)
    tiles, partial = word_products(rows, cols, base, words_all, band, cleared)
    share, everyone, clear_contexts = word_panel_sum(partial.reshape(NZ, NYH, NC, SHARE, T))
    rounded = everyone.reshape(ROW_TILES, T, T)
    context_partial, share = context_products(rows, cols, tiles, rounded, share, clear_contexts)
    context_share = context_panel_sum(context_partial.reshape(NYL, NX, SHARE, T))
    return share, context_share


def solution(mesh):
    split = Mesh(
        mesh.devices.reshape(NYL, NX, NZ, NYH, NC), ("yl", "x", "z", "yh", "core")
    )
    row, col = ("yl", "x"), ("z", "yh", "core")
    in_specs = (
        P(row, col, None, None, None),
        P(row, col, None),
        P(row, col, None),
        P(col + row, None),
    )
    out_specs = (P(row + col, None), P(col + row, None))
    return jax.shard_map(shards, mesh=split, in_specs=in_specs, out_specs=out_specs, check_vma=False)
```
